128 devices in a mesh: dict: 8 (over x, z_hi), dp: 16 (over z_lo, y, core).
Axes of the slice: x: 4, y: 4, z: 4 (z_hi: 2, z_lo: 2; z = z_hi * 2 + z_lo), core: 2. Of those that a mesh axis runs over, the one named last changes fastest.
Arguments:
- activations: bfloat16 [4096, 3584], P('dp', 'dict'), may hold values from -6 to 6
- dictionary: bfloat16 [65536, 3584], P(('dict', 'dp')), may hold values from -0.09375 to 0.09375
- enc_bias: bfloat16 [65536], P(('dict', 'dp')), may hold values from -1.5 to 0
- dec_bias: float32 [3584], replicated, may hold values from -3 to 3
- block_codes: int32 [32, 8, 16], P('dp'), may hold values from -1 to 511, as said below
Outputs:
- error: bfloat16 [4096, 3584], P('dp', 'dict')
- grad_dict: float32 [65536, 3584], P(('dict', 'dp'))
- grad_enc_bias: float32 [65536], P(('dict', 'dp'))
The draws below stay inside these ranges and needn't reach their ends.
Inputs may be any that keep to these rules, and one draw needn't show every extreme that they name: `block_codes`: entry [b, s, m] is either -1 (an empty slot) or a latent block of shard s, that is one of the blocks s * 64 upward. Block k is held by the dp index (k % 64) // 4. Every token block names exactly 64 blocks in all and at most 16 in one shard, reached in every draw; within one shard its blocks are held by distinct dp indices. All token blocks of one dp index that name a block held by the same dp index of the same shard name the same block.
All inputs are finite; a program needn't handle non-finite values.
Results may differ from the reference program's by a relative error of at most 0.012.
The reference program's roundings to bfloat16 on the way count: a program that leaves them out, or rounds other values in their place, can miss the bound.
Values may be sent and summed in bfloat16 or wider, within the bound.
A program may use at most 128 MiB of HBM per device.

```python
import jax
import jax.numpy as jnp
from jax import lax

D = 3584
LAT_DICT = 8192
DICT_SPAN = 128
SAMPLE_SPAN = 128
ACT_S = 8
SAMPLES_REPLICA = 256
LAT = 65536
SWING = 8
MOST = 16
TOKENS = 4096
NBLK = 32
NTB = 2
N_DICT = 8
N_DP = 16


def draw_block_codes(key, part):
    key_pick, key_order, key_shift, key_owner = jax.random.split(key, 4)
    shard_blocks = LAT_DICT // DICT_SPAN
    own_blocks = shard_blocks // N_DP
    per_group = SAMPLES_REPLICA // SAMPLE_SPAN
    choose = jax.random.randint(key_pick, (N_DP, N_DICT, N_DP), 0, own_blocks, dtype=jnp.int32)
    ranking_scores = jax.random.randint(key_order, (NBLK, N_DICT), 0, 1 << 20, dtype=jnp.int32) * N_DICT + jnp.arange(N_DICT, dtype=jnp.int32)
    shard_order = jnp.argsort(ranking_scores, axis=1, stable=True).astype(jnp.int32)
    pair_count = N_DICT // 2
    shifts = jax.random.randint(key_shift, (NBLK, pair_count), -SWING, SWING + 1, dtype=jnp.int32)
    leading = jnp.arange(NBLK, dtype=jnp.int32) % per_group == 0
    shifts = shifts.at[:, 0].set(jnp.where(leading, SWING, shifts[:, 0]))
    signed = jnp.stack([shifts, -shifts], axis=2).reshape(NBLK, N_DICT)
    onehot = (shard_order[:, :, None] == jnp.arange(N_DICT, dtype=jnp.int32)).astype(jnp.int32)
    counts = ACT_S + jnp.sum(onehot * signed[:, :, None], axis=1)
    owner_scores = jax.random.randint(key_owner, (NBLK, N_DICT, N_DP), 0, 1 << 20, dtype=jnp.int32) * N_DP + jnp.arange(N_DP, dtype=jnp.int32)
    _, owners = lax.top_k(owner_scores, MOST)
    group_of = jnp.arange(NBLK, dtype=jnp.int32) // per_group
    inner_pick = jnp.take_along_axis(choose[group_of], owners, axis=2)
    block_ids = jnp.arange(N_DICT, dtype=jnp.int32)[None, :, None] * shard_blocks + owners * own_blocks + inner_pick
    slot_pos = jnp.arange(MOST, dtype=jnp.int32)[None, None, :]
    return jnp.where(slot_pos < counts[:, :, None], block_ids, -1).astype(jnp.int32)


def block_scale(stream_key, dims, pieces, smallest, high):
    gain = 1.0
    for position, parts in pieces:
        steps = jax.random.uniform(jax.random.fold_in(jax.random.fold_in(stream_key, 6), position), (parts,), jnp.float32, smallest / len(pieces), high / len(pieces))
        gain = gain * jnp.repeat(jnp.exp(steps), dims[position] // parts).reshape((-1,) + (1,) * (len(dims) - 1 - position))
    return gain


def noise(stream_key, dims, scale, reach, pieces=(), kind=jnp.bfloat16):
    level = block_scale(stream_key, dims, pieces, -0.22, 0.18) if pieces else 1.0
    entries = jax.random.normal(stream_key, dims, jnp.float32) * scale * level
    return jnp.minimum(jnp.maximum(entries, -reach), reach).astype(kind)


def setup_inputs(seed: int = 0) -> dict:
    keys = jax.random.split(jax.random.key(seed), 6)
    activations = noise(keys[0], (TOKENS, D), 1.0, 6.0, ((0, 16), (1, 8)))
    dictionary = noise(keys[1], (LAT, D), D ** -0.5, 0.09375, ((0, 128),))
    enc_bias = jnp.clip(-1.5 + 1.5 * jax.random.uniform(keys[2], (LAT,), jnp.float32) ** block_scale(keys[2], (LAT,), ((0, 128),), -0.2, 0.2), -1.5, 0.0).astype(jnp.bfloat16)
    dec_bias = noise(keys[3], (D,), 0.5, 3.0, (), jnp.float32)
    block_codes = draw_block_codes(jax.random.fold_in(keys[5], 71), 0)
    return dict(activations=activations, dictionary=dictionary, enc_bias=enc_bias, dec_bias=dec_bias, block_codes=block_codes)


def reference(activations, dictionary, enc_bias, dec_bias, block_codes):
    shard_blocks = LAT_DICT // DICT_SPAN
    own_blocks = shard_blocks // N_DP
    all_blocks = LAT // DICT_SPAN
    position_total = N_DICT * N_DP
    slot_rows = position_total * DICT_SPAN
    table_w = dictionary.reshape(all_blocks, DICT_SPAN, D)
    table_b = enc_bias.reshape(all_blocks, DICT_SPAN)
    shard_ids = jnp.arange(N_DICT, dtype=jnp.int32)[None, :, None]
    peer_ids = jnp.arange(N_DP, dtype=jnp.int32)

    def group_step(carry, inputs):
        grad_w, grad_b = carry
        tokens, group_codes = inputs
        filled = group_codes >= 0
        owning = jnp.where(filled, (group_codes - shard_ids * shard_blocks) // own_blocks, -1)
        matches = owning[..., None] == peer_ids
        picked = jnp.max(jnp.where(matches, group_codes[..., None], -1), axis=(0, 2)).reshape(position_total)
        selected_entries = jnp.any(matches, axis=2).reshape(group_codes.shape[0], position_total)
        safe_ids = jnp.maximum(picked, 0).astype(jnp.int32)
        fetched = table_w[safe_ids].reshape(slot_rows, D)
        bias_flat = table_b[safe_ids].reshape(slot_rows).astype(jnp.float32)
        mean_removed = (tokens.astype(jnp.float32) - dec_bias).astype(jnp.bfloat16)
        preact = lax.dot_general(mean_removed, fetched, (((1,), (1,)), ((), ())), preferred_element_type=jnp.float32) + bias_flat
        encoder_input_tiles = preact.reshape(SAMPLES_REPLICA, position_total, DICT_SPAN)
        nonzero_indicator = jnp.repeat(selected_entries, SAMPLE_SPAN, axis=0)[:, :, None]
        hidden_activity = jnp.where(nonzero_indicator, jnp.maximum(encoder_input_tiles, 0.0), 0.0).astype(jnp.bfloat16)
        recon = jnp.dot(hidden_activity.reshape(SAMPLES_REPLICA, slot_rows), fetched, preferred_element_type=jnp.float32) + dec_bias
        error = (recon - tokens.astype(jnp.float32)).astype(jnp.bfloat16)
        returned_entries = lax.dot_general(error, fetched, (((1,), (1,)), ((), ())), preferred_element_type=jnp.float32)
        derivative_factor = jnp.where(nonzero_indicator & (encoder_input_tiles > 0), returned_entries.reshape(SAMPLES_REPLICA, position_total, DICT_SPAN), 0.0).astype(jnp.bfloat16)
        weight_summands = jnp.einsum("eaw,ep->awp", hidden_activity.astype(jnp.float32), error.astype(jnp.float32))
        weight_summands = weight_summands + jnp.einsum("eaw,ep->awp", derivative_factor.astype(jnp.float32), mean_removed.astype(jnp.float32))
        weight_summands = weight_summands.astype(jnp.bfloat16)
        terms_b = jnp.sum(derivative_factor.astype(jnp.float32), axis=0).astype(jnp.bfloat16)
        grad_w = grad_w.at[safe_ids].add(weight_summands.astype(jnp.float32))
        grad_b = grad_b.at[safe_ids].add(terms_b.astype(jnp.float32))
        return (grad_w, grad_b), error

    zeros_w = jnp.zeros((all_blocks, DICT_SPAN, D), jnp.float32)
    zeros_b = jnp.zeros((all_blocks, DICT_SPAN), jnp.float32)
    inputs = (activations.reshape(N_DP, SAMPLES_REPLICA, D), block_codes.reshape(N_DP, NTB, N_DICT, MOST))
    (grad_w, grad_b), errors = lax.scan(group_step, (zeros_w, zeros_b), inputs)
    return errors.reshape(TOKENS, D), grad_w.reshape(LAT, D), grad_b.reshape(LAT)
```

```python
import functools
import jax, jax.numpy as jnp
from jax import lax
from jax.experimental import pallas as pl
from jax.experimental.pallas import tpu as pltpu
from jax.sharding import Mesh, PartitionSpec as P

ROWS, TOK = 448, 256
C0 = (0, 144, 288)
CN = (144, 144, 160)
CH = (80, 64, 80)
ORDER = (("x", "y", "z"), ("y", "z", "x"), ("z", "x", "y"))


def coords():
    x, y = lax.axis_index("x"), lax.axis_index("y")
    z = lax.axis_index("zh") * 2 + lax.axis_index("zl")
    return {"x": x, "y": y, "z": z}


def shift(me, dim, by):
    return lax.rem(me[dim] + (by + 4), 4)


def device(dim, value):
    if dim == "z":
        return {"zh": value // 2, "zl": lax.rem(value, 2)}
    return {dim: value}


def region(ref, at, lo, n):
    z = at["z"]
    zl = slice(None) if z is None else lax.rem(z, 2)
    zh = slice(None) if z is None else z // 2
    y = slice(None) if at["y"] is None else at["y"]
    x = slice(None) if at["x"] is None else at["x"]
    return ref.at[zl, y, x, zh, pl.ds(lo, n), :]


def remote(src, dst, send, recv, dim, value):
    return pltpu.make_async_remote_copy(
        src_ref=src, dst_ref=dst, send_sem=send, recv_sem=recv,
        device_id=device(dim, value), device_id_type=pl.DeviceIdType.MESH)


def barrier(me):
    sem = pltpu.get_barrier_semaphore()
    for dim in ("x", "y", "z"):
        for by in (-1, 1):
            pl.semaphore_signal(sem, inc=1, device_id=device(dim, shift(me, dim, by)),
                                device_id_type=pl.DeviceIdType.MESH)
    pl.semaphore_wait(sem, 6)


def gather(me, own, out, local, send, recv):
    mine = pltpu.make_async_copy(own, region(out, me, 0, ROWS), local)
    mine.start()
    started = []
    for p in range(3):
        near = []
        for k in range(3):
            dim, prev = ORDER[k][p], ORDER[k][:p]
            at = {d: (None if d in prev else me[d]) for d in me}
            lo, n, h = C0[k], CN[k], CH[k]
            copies = []
            for s, by in enumerate((1, -1)):
                src = own.at[pl.ds(lo, n), :] if p == 0 else region(out, at, lo, n)
                c = remote(src, region(out, at, lo, n), send.at[k, p, s], recv.at[k, p, s], dim, shift(me, dim, by))
                c.start()
                copies.append(c)
            near.append(copies)
            started += copies
        far = []
        for k in range(3):
            dim, prev = ORDER[k][p], ORDER[k][:p]
            lo, n, h = C0[k], CN[k], CH[k]
            copies = []
            for s, by in enumerate((1, -1)):
                at = {d: (None if d in prev else me[d]) for d in me}
                at[dim] = shift(me, dim, -by)
                near[k][s].wait_recv()
                a, b = (lo, h) if s == 0 else (lo + h, n - h)
                c = remote(region(out, at, a, b), region(out, at, a, b), send.at[k, p, 2 + s], recv.at[k, p, 2 + s],
                           dim, shift(me, dim, by))
                c.start()
                copies.append(c)
            far.append(copies)
            started += copies
        for k in range(3):
            for c in far[k]:
                c.wait_recv()
        if p == 0:
            mine.wait()
    for c in started:
        c.wait_send()


def held(ref, dims, at, lo, n):
    index = []
    for name in ("zl", "y", "x", "zh"):
        dim = name[0]
        if dim not in dims:
            continue
        value = at[dim]
        if value is None:
            index.append(slice(None))
        elif name == "zl":
            index.append(lax.rem(value, 2))
        elif name == "zh":
            index.append(value // 2)
        else:
            index.append(value)
    return ref.at[(*index, pl.ds(lo, n), slice(None))]


def lead(dims):
    return tuple(s for name, s in (("zl", 2), ("y", 4), ("x", 4), ("zh", 2)) if name[0] in dims)


def each(shape, body):
    total = 1
    for s in shape:
        total *= s
    if total == 1:
        body(())
        return

    def step(i, carry):
        index = []
        for s in reversed(shape):
            index.append(lax.rem(i, s))
            i = i // s
        body(tuple(reversed(index)))
        return carry

    lax.fori_loop(0, total, step, 0)


def reduce_scratch():
    shapes = []
    for k in range(3):
        n, h = CN[k], CH[k]
        for q in range(3):
            dims = lead(ORDER[k][: 2 - q])
            for rows in (h, n - h, h, n - h, h, n - h):
                shapes.append(pltpu.VMEM((*dims, rows, TOK), jnp.bfloat16))
            if q < 2:
                shapes.append(pltpu.VMEM((*dims, n, TOK), jnp.bfloat16))
    return shapes


def reduce_error(me, parts, base, err, slots, send, recv):
    slots = list(slots)
    table = []
    for k in range(3):
        row = []
        for q in range(3):
            row.append([slots.pop(0) for _ in range(7 if q < 2 else 6)])
        table.append(row)
    started = []

    def source(k, q, at, lo, n):
        if q == 0:
            return region(parts, at, C0[k] + lo, n)
        return held(table[k][q - 1][6], ORDER[k][: 3 - q], at, lo, n)

    for q in range(3):
        first = []
        for k in range(3):
            dim, rest = ORDER[k][2 - q], ORDER[k][: 2 - q]
            n, h = CN[k], CH[k]
            at = {d: (None if d in rest else me[d]) for d in me}
            far = {**at, dim: shift(me, dim, 2)}
            up, down = shift(me, dim, 1), shift(me, dim, -1)
            opp_p, opp_m, sum_p, raw_p, raw_m, sum_m = table[k][q][:6]
            copies = [
                remote(source(k, q, far, 0, h), opp_p, send.at[k, q, 0], recv.at[k, q, 0], dim, up),
                remote(source(k, q, far, h, n - h), opp_m, send.at[k, q, 1], recv.at[k, q, 1], dim, down),
                remote(source(k, q, {**at, dim: up}, h, n - h), raw_p, send.at[k, q, 2], recv.at[k, q, 2], dim, up),
                remote(source(k, q, {**at, dim: down}, 0, h), raw_m, send.at[k, q, 3], recv.at[k, q, 3], dim, down),
            ]
            for c in copies:
                c.start()
            first.append(copies)
            started += copies
        second = []
        for k in range(3):
            dim, rest = ORDER[k][2 - q], ORDER[k][: 2 - q]
            n, h = CN[k], CH[k]
            at = {d: (None if d in rest else me[d]) for d in me}
            up, down = shift(me, dim, 1), shift(me, dim, -1)
            opp_p, opp_m, sum_p, raw_p, raw_m, sum_m = table[k][q][:6]
            copies = []
            for s, (slot, to, lo, rows, into) in enumerate(((opp_p, up, 0, h, sum_p), (opp_m, down, h, n - h, sum_m))):
                first[k][s].wait_recv()
                own = source(k, q, {**at, dim: to}, lo, rows)

                def add(index, slot=slot, own=own):
                    a = slot[index].astype(jnp.float32) + own[index].astype(jnp.float32)
                    slot[index] = a.astype(jnp.bfloat16)

                each(lead(rest), add)
                c = remote(slot, into, send.at[k, q, 4 + s], recv.at[k, q, 4 + s], dim, to)
                c.start()
                copies.append(c)
            second.append(copies)
            started += copies
        for k in range(3):
            dim, rest = ORDER[k][2 - q], ORDER[k][: 2 - q]
            n, h = CN[k], CH[k]
            at = {d: (None if d in rest else me[d]) for d in me}
            opp_p, opp_m, sum_p, raw_p, raw_m, sum_m = table[k][q][:6]
            first[k][2].wait_recv()
            first[k][3].wait_recv()
            second[k][0].wait_recv()
            second[k][1].wait_recv()
            for lo, rows, a, b in ((0, h, sum_p, raw_m), (h, n - h, raw_p, sum_m)):
                own = source(k, q, at, lo, rows)

                def add(index, own=own, a=a, b=b, lo=lo, rows=rows):
                    total = own[index].astype(jnp.float32) + a[index].astype(jnp.float32) + b[index].astype(jnp.float32)
                    if q < 2:
                        table[k][q][6][(*index, pl.ds(lo, rows), slice(None))] = total.astype(jnp.bfloat16)
                    else:
                        at_rows = pl.ds(C0[k] + lo, rows)
                        err[at_rows, :] = (total + base[at_rows, :]).astype(jnp.bfloat16)

                each(lead(rest), add)
    return started


def params(collective=None):
    return pltpu.CompilerParams(collective_id=collective, has_side_effects=collective is not None,
                                vmem_limit_bytes=60 * 1024 * 1024)


PIECES = (2, 4, 4, 2, ROWS, TOK)
VMEM = pl.BlockSpec(memory_space=pltpu.VMEM)
ANY = pl.BlockSpec(memory_space=pl.ANY)


def gather_kernel(own, out, local, send, recv):
    me = coords()
    barrier(me)
    gather(me, own, out, local, send, recv)


def gather_call(x):
    return pl.pallas_call(
        gather_kernel,
        out_shape=jax.ShapeDtypeStruct(PIECES, jnp.bfloat16),
        in_specs=[VMEM], out_specs=ANY,
        scratch_shapes=[pltpu.SemaphoreType.DMA, pltpu.SemaphoreType.DMA((3, 3, 4)), pltpu.SemaphoreType.DMA((3, 3, 4))],
        compiler_params=params(0), name="gather",
        cost_estimate=pl.CostEstimate(flops=0, bytes_accessed=150_000_000, transcendentals=0),
    )(x)


def error_kernel(parts, base, err, out, local, send, recv, rsend, rrecv, *slots):
    me = coords()
    barrier(me)
    started = reduce_error(me, parts, base, err, slots, rsend, rrecv)
    gather(me, err, out, local, send, recv)
    for c in started:
        c.wait_send()


def error_call(parts, base):
    dma = pltpu.SemaphoreType.DMA
    return pl.pallas_call(
        error_kernel,
        out_shape=(jax.ShapeDtypeStruct((ROWS, TOK), jnp.bfloat16), jax.ShapeDtypeStruct(PIECES, jnp.bfloat16)),
        in_specs=[VMEM, VMEM], out_specs=(VMEM, ANY),
        scratch_shapes=[dma, dma((3, 3, 4)), dma((3, 3, 4)), dma((3, 3, 6)), dma((3, 3, 6)), *reduce_scratch()],
        compiler_params=params(1), name="error",
    )(parts, base)


D = 3584
SPAN = 128
CHUNK = 896


def pick(sel, g, w, ws):
    for hh in range(2):
        ws[hh * SPAN : (hh + 1) * SPAN, :] = w[hh * 4 + sel[g, hh]]


def encode_kernel(sel, named, cen, w, bias, part, lat, mask, ws):
    g = pl.program_id(0)
    pick(sel, g, w, ws)
    pre = jnp.dot(ws[...], cen[0], preferred_element_type=jnp.float32)
    lane = lax.broadcasted_iota(jnp.int32, (SPAN, TOK), 1)
    for hh in range(2):
        rows = slice(hh * SPAN, (hh + 1) * SPAN)
        p = pre[rows] + bias[hh * 4 + sel[g, hh]]
        on = jnp.where(lane < SPAN, named[g, hh], named[g, 2 + hh])
        keep = (on > 0) & (p > 0)
        lat[0, rows] = jnp.where(keep, p, 0.0).astype(jnp.bfloat16)
        mask[0, rows] = jnp.where(keep, 1.0, 0.0).astype(jnp.bfloat16)
    for i in range(0, D, CHUNK):
        part[0, i : i + CHUNK] = lax.dot_general(
            ws[:, i : i + CHUNK], lat[0], (((0,), (0,)), ((), ())), preferred_element_type=jnp.float32
        ).astype(jnp.bfloat16)


def encode_call(sel, named, cen, w, bias):
    per = lambda *shape: pl.BlockSpec((1, *shape), lambda g, *_: (g, 0, 0))
    return pl.pallas_call(
        encode_kernel,
        out_shape=(
            jax.ShapeDtypeStruct((8, D, TOK), jnp.bfloat16),
            jax.ShapeDtypeStruct((8, 2 * SPAN, TOK), jnp.bfloat16),
            jax.ShapeDtypeStruct((8, 2 * SPAN, TOK), jnp.bfloat16),
        ),
        grid_spec=pltpu.PrefetchScalarGridSpec(
            num_scalar_prefetch=2, grid=(8,),
            in_specs=[per(D, TOK), VMEM, VMEM],
            out_specs=(per(D, TOK), per(2 * SPAN, TOK), per(2 * SPAN, TOK)),
            scratch_shapes=[pltpu.VMEM((2 * SPAN, D), jnp.bfloat16)],
        ),
        compiler_params=params(), name="encode",
    )(sel, named, cen, w, bias)


def grad_kernel(sel, err, cen, lat, mask, w, own, other, gb, ws, acc):
    g = pl.program_id(0)

    @pl.when(g == 0)
    def _():
        own[...] = jnp.zeros_like(own)
        acc[...] = jnp.zeros_like(acc)
        gb[...] = jnp.zeros_like(gb)

    pick(sel, g, w, ws)
    back = jnp.dot(ws[...], err[0], preferred_element_type=jnp.float32)
    slope = jnp.where(mask[0] > 0, back, 0.0).astype(jnp.bfloat16)
    ones = jnp.ones((TOK, SPAN), jnp.bfloat16)
    sums = jnp.dot(slope, ones, preferred_element_type=jnp.float32).astype(jnp.bfloat16).astype(jnp.float32)
    for hh in range(2):
        gb[hh * 4 + sel[g, hh]] += sums[hh * SPAN : (hh + 1) * SPAN]
    for i in range(0, D, CHUNK):
        nt = (((1,), (1,)), ((), ()))
        t = lax.dot_general(lat[0], err[0, i : i + CHUNK], nt, preferred_element_type=jnp.float32)
        t = t + lax.dot_general(slope, cen[0, i : i + CHUNK], nt, preferred_element_type=jnp.float32)
        t = t.astype(jnp.bfloat16).astype(jnp.float32)
        own[sel[g, 0], :, i : i + CHUNK] += t[:SPAN]
        acc[sel[g, 1], :, i : i + CHUNK] += t[SPAN:]

    @pl.when(g == 7)
    def _():
        for b in range(4):
            other[b] = acc[b].astype(jnp.bfloat16)


def grad_call(sel, err, cen, lat, mask, w):
    per = lambda *shape: pl.BlockSpec((1, *shape), lambda g, *_: (g, 0, 0))
    return pl.pallas_call(
        grad_kernel,
        out_shape=(
            jax.ShapeDtypeStruct((4, SPAN, D), jnp.float32),
            jax.ShapeDtypeStruct((4, SPAN, D), jnp.bfloat16),
            jax.ShapeDtypeStruct((8, SPAN, SPAN), jnp.float32),
        ),
        grid_spec=pltpu.PrefetchScalarGridSpec(
            num_scalar_prefetch=1, grid=(8,),
            in_specs=[per(D, TOK), per(D, TOK), per(2 * SPAN, TOK), per(2 * SPAN, TOK), VMEM],
            out_specs=(VMEM, VMEM, VMEM),
            scratch_shapes=[pltpu.VMEM((2 * SPAN, D), jnp.bfloat16), pltpu.VMEM((4, SPAN, D), jnp.float32)],
        ),
        compiler_params=params(), name="grad",
    )(sel, err, cen, lat, mask, w)


NAMES = ("x", "zh", "zl", "y", "c")
SWAP = [(0, 1), (1, 0)]


def step(activations, dictionary, enc_bias, dec_bias, block_codes):
    d = lax.axis_index("x") * 2 + lax.axis_index("zh")
    c = lax.axis_index("c")
    chip = lax.axis_index("zl") * 4 + lax.axis_index("y")
    mine = dictionary.reshape(4, SPAN, D)
    theirs = lax.ppermute(mine, "c", SWAP)
    bias_theirs = lax.ppermute(enc_bias, "c", SWAP)
    codes = lax.dynamic_index_in_dim(block_codes, d, axis=1, keepdims=False)
    codes = lax.all_gather(codes, ("zl", "y"), axis=0)
    act_t = activations.T.astype(jnp.float32)
    dec = lax.dynamic_slice_in_dim(dec_bias, d * ROWS, ROWS)[:, None]
    cen = gather_call((act_t - dec).astype(jnp.bfloat16)).reshape(8, D, TOK)
    first = d * 64 + (chip * 2 + jnp.stack([c, 1 - c])) * 4
    local = codes[:, :, None, :] - first[:, None]
    hit = (codes[:, :, None, :] >= 0) & (local >= 0) & (local < 4)
    named = jnp.any(hit, axis=3).astype(jnp.int32).reshape(8, 4)
    sel = jnp.max(jnp.where(hit, local, 0), axis=(1, 3)).astype(jnp.int32)
    w = jnp.concatenate([mine, theirs])
    bias = jnp.concatenate([enc_bias, bias_theirs]).astype(jnp.float32).reshape(8, SPAN, 1)
    part, lat, mask = encode_call(sel, named, cen, w, bias)
    err_own, err = error_call(part.reshape(PIECES), dec - act_t)
    own, other, gb = grad_call(sel, err.reshape(8, D, TOK), cen, lat, mask, w)
    gb = gb[:, :, 0]
    grad_w = own + lax.ppermute(other, "c", SWAP).astype(jnp.float32)
    grad_b = gb[:4] + lax.ppermute(gb[4:], "c", SWAP)
    return err_own.T, grad_w.reshape(4 * SPAN, D), grad_b.reshape(4 * SPAN)


def solution(mesh):
    split = Mesh(mesh.devices.reshape(4, 2, 2, 4, 2), NAMES)
    dict_, dp = ("x", "zh"), ("zl", "y", "c")
    rows = P((*dict_, *dp))
    return jax.shard_map(
        step, mesh=split,
        in_specs=(P(dp, dict_), P((*dict_, *dp), None), rows, P(), P(dp, None, None)),
        out_specs=(P(dp, dict_), P((*dict_, *dp), None), rows),
        check_vma=False,
    )
```

```python
import functools
import jax, jax.numpy as jnp
from jax import lax
from jax.experimental import pallas as pl
from jax.experimental.pallas import tpu as pltpu
from jax.sharding import Mesh, PartitionSpec as P

ROWS, TOK = 448, 256
C0 = (0, 144, 288)
CN = (144, 144, 160)
CH = (80, 64, 80)
ORDER = (("x", "y", "z"), ("y", "z", "x"), ("z", "x", "y"))


def coords():
    x, y = lax.axis_index("x"), lax.axis_index("y")
    z = lax.axis_index("zh") * 2 + lax.axis_index("zl")
    return {"x": x, "y": y, "z": z}


def shift(me, dim, by):
    return lax.rem(me[dim] + (by + 4), 4)


def device(dim, value):
    if dim == "z":
        return {"zh": value // 2, "zl": lax.rem(value, 2)}
    return {dim: value}


def region(ref, at, lo, n):
    z = at["z"]
    zl = slice(None) if z is None else lax.rem(z, 2)
    zh = slice(None) if z is None else z // 2
    y = slice(None) if at["y"] is None else at["y"]
    x = slice(None) if at["x"] is None else at["x"]
    return ref.at[zl, y, x, zh, pl.ds(lo, n), :]


def remote(src, dst, send, recv, dim, value):
    return pltpu.make_async_remote_copy(
        src_ref=src, dst_ref=dst, send_sem=send, recv_sem=recv,
        device_id=device(dim, value), device_id_type=pl.DeviceIdType.MESH)


def barrier(me):
    sem = pltpu.get_barrier_semaphore()
    for dim in ("x", "y", "z"):
        for by in (-1, 1):
            pl.semaphore_signal(sem, inc=1, device_id=device(dim, shift(me, dim, by)),
                                device_id_type=pl.DeviceIdType.MESH)
    pl.semaphore_wait(sem, 6)


NEAR = ((0, 1), (1, -1))


def gather(me, own, out, local, send, recv, beside=iter(())):
    mine = pltpu.make_async_copy(own, region(out, me, 0, ROWS), local)
    mine.start()
    copies = [{} for _ in range(3)]

    def go(k, phase, name, at, by, lo=0, n=None, src=None):
        order = ORDER[k]
        where = {d: (None if i < phase - 1 else shift(me, d, at.get(i, 0))) for i, d in enumerate(order)}
        part = region(out, where, C0[k] + lo, CN[k] if n is None else n)
        dim = order[phase]
        i = len(copies[k])
        c = remote(part if src is None else src, part, send.at[k, i], recv.at[k, i], dim, shift(me, dim, by))
        c.start()
        copies[k][(phase, *name)] = c

    def got(k, *name):
        copies[k][name].wait_recv()

    for k in range(3):
        src = own.at[pl.ds(C0[k], CN[k]), :]
        for s, by in NEAR:
            go(k, 0, ("near", s), {}, by, src=src)
        for s, by in NEAR:
            go(k, 1, ("near", 0, s), {}, by, src=src)
    next(beside, None)
    for k in range(3):
        for s, by in NEAR:
            got(k, 0, "near", s)
            lo, n = (0, CH[k]) if s == 0 else (CH[k], CN[k] - CH[k])
            go(k, 0, ("far", s), {0: -by}, by, lo, n)
        for j in (-1, 1):
            for s, by in NEAR:
                go(k, 1, ("near", j, s), {0: j}, by)
    mine.wait()
    next(beside, None)
    for k in range(3):
        got(k, 0, "far", 0)
        got(k, 0, "far", 1)
        for s, by in NEAR:
            go(k, 1, ("near", 2, s), {0: 2}, by)
        for s, by in NEAR:
            go(k, 2, ("near", 0, s), {1: 0}, by)
    for phase in (1, 2):
        next(beside, None)
        for j in (0, -1, 1, 2):
            for k in range(3):
                for s, by in NEAR:
                    got(k, phase, "near", j, s)
                    if (j in (0, 1)) == (s == 0):
                        go(k, phase, ("far", j), {phase - 1: j, phase: -by}, by)
        if phase == 1:
            for k in range(3):
                for j in (-1, 1):
                    for s, by in NEAR:
                        go(k, 2, ("near", j, s), {1: j}, by)
        for k in range(3):
            for j in (0, -1, 1, 2):
                got(k, phase, "far", j)
            if phase == 1:
                for s, by in NEAR:
                    go(k, 2, ("near", 2, s), {1: 2}, by)
    for k in range(3):
        for c in copies[k].values():
            c.wait_send()


def gather_codes(me, own, out, send, recv):
    zl = lax.rem(me["z"], 2)
    out[zl, me["y"]] = own[...]
    copies = []

    def go(src, dst, device_id):
        i = len(copies)
        c = pltpu.make_async_remote_copy(src_ref=src, dst_ref=dst, send_sem=send.at[i], recv_sem=recv.at[i],
                                         device_id=device_id, device_id_type=pl.DeviceIdType.MESH)
        c.start()
        copies.append(c)

    for by in (1, -1):
        go(own, out.at[zl, me["y"]], device("y", shift(me, "y", by)))
    yield
    copies[0].wait_recv()
    back = out.at[zl, shift(me, "y", -1)]
    go(back, back, device("y", shift(me, "y", 1)))
    yield
    copies[1].wait_recv()
    copies[2].wait_recv()
    go(out.at[zl], out.at[zl], {"zl": 1 - zl})
    yield
    copies[3].wait_recv()
    for c in copies:
        c.wait_send()


def held(ref, dims, at, lo, n):
    index = []
    for name in ("zl", "y", "x", "zh"):
        dim = name[0]
        if dim not in dims:
            continue
        value = at[dim]
        if value is None:
            index.append(slice(None))
        elif name == "zl":
            index.append(lax.rem(value, 2))
        elif name == "zh":
            index.append(value // 2)
        else:
            index.append(value)
    return ref.at[(*index, pl.ds(lo, n), slice(None))]


def lead(dims):
    return tuple(s for name, s in (("zl", 2), ("y", 4), ("x", 4), ("zh", 2)) if name[0] in dims)


def each(shape, body):
    total = 1
    for s in shape:
        total *= s
    if total == 1:
        body(())
        return

    def step(i, carry):
        index = []
        for s in reversed(shape):
            index.append(lax.rem(i, s))
            i = i // s
        body(tuple(reversed(index)))
        return carry

    lax.fori_loop(0, total, step, 0)


def reduce_scratch():
    shapes = []
    for k in range(3):
        n, h = CN[k], CH[k]
        for q in range(3):
            dims = lead(ORDER[k][: 2 - q])
            for rows in (h, n - h, h, n - h, h, n - h):
                shapes.append(pltpu.VMEM((*dims, rows, TOK), jnp.bfloat16))
            if q < 2:
                shapes.append(pltpu.VMEM((*dims, n, TOK), jnp.bfloat16))
    return shapes


def reduce_error(me, parts, base, err, slots, send, recv):
    slots = list(slots)
    table = []
    for k in range(3):
        row = []
        for q in range(3):
            row.append([slots.pop(0) for _ in range(7 if q < 2 else 6)])
        table.append(row)
    started = []

    def source(k, q, at, lo, n):
        if q == 0:
            return region(parts, at, C0[k] + lo, n)
        return held(table[k][q - 1][6], ORDER[k][: 3 - q], at, lo, n)

    for q in range(3):
        first = []
        for k in range(3):
            dim, rest = ORDER[k][2 - q], ORDER[k][: 2 - q]
            n, h = CN[k], CH[k]
            at = {d: (None if d in rest else me[d]) for d in me}
            far = {**at, dim: shift(me, dim, 2)}
            up, down = shift(me, dim, 1), shift(me, dim, -1)
            opp_p, opp_m, sum_p, raw_p, raw_m, sum_m = table[k][q][:6]
            copies = [
                remote(source(k, q, far, 0, h), opp_p, send.at[k, q, 0], recv.at[k, q, 0], dim, up),
                remote(source(k, q, far, h, n - h), opp_m, send.at[k, q, 1], recv.at[k, q, 1], dim, down),
                remote(source(k, q, {**at, dim: up}, h, n - h), raw_p, send.at[k, q, 2], recv.at[k, q, 2], dim, up),
                remote(source(k, q, {**at, dim: down}, 0, h), raw_m, send.at[k, q, 3], recv.at[k, q, 3], dim, down),
            ]
            for c in copies:
                c.start()
            first.append(copies)
            started += copies
        second = []
        for k in range(3):
            dim, rest = ORDER[k][2 - q], ORDER[k][: 2 - q]
            n, h = CN[k], CH[k]
            at = {d: (None if d in rest else me[d]) for d in me}
            up, down = shift(me, dim, 1), shift(me, dim, -1)
            opp_p, opp_m, sum_p, raw_p, raw_m, sum_m = table[k][q][:6]
            copies = []
            for s, (slot, to, lo, rows, into) in enumerate(((opp_p, up, 0, h, sum_p), (opp_m, down, h, n - h, sum_m))):
                first[k][s].wait_recv()
                own = source(k, q, {**at, dim: to}, lo, rows)

                def add(index, slot=slot, own=own):
                    a = slot[index].astype(jnp.float32) + own[index].astype(jnp.float32)
                    slot[index] = a.astype(jnp.bfloat16)

                each(lead(rest), add)
                c = remote(slot, into, send.at[k, q, 4 + s], recv.at[k, q, 4 + s], dim, to)
                c.start()
                copies.append(c)
            second.append(copies)
            started += copies
        for k in range(3):
            dim, rest = ORDER[k][2 - q], ORDER[k][: 2 - q]
            n, h = CN[k], CH[k]
            at = {d: (None if d in rest else me[d]) for d in me}
            opp_p, opp_m, sum_p, raw_p, raw_m, sum_m = table[k][q][:6]
            first[k][2].wait_recv()
            first[k][3].wait_recv()
            second[k][0].wait_recv()
            second[k][1].wait_recv()
            for lo, rows, a, b in ((0, h, sum_p, raw_m), (h, n - h, raw_p, sum_m)):
                own = source(k, q, at, lo, rows)

                def add(index, own=own, a=a, b=b, lo=lo, rows=rows):
                    total = own[index].astype(jnp.float32) + a[index].astype(jnp.float32) + b[index].astype(jnp.float32)
                    if q < 2:
                        table[k][q][6][(*index, pl.ds(lo, rows), slice(None))] = total.astype(jnp.bfloat16)
                    else:
                        at_rows = pl.ds(C0[k] + lo, rows)
                        err[at_rows, :] = (total + base[at_rows, :]).astype(jnp.bfloat16)

                each(lead(rest), add)
    return started


def params(collective=None):
    return pltpu.CompilerParams(collective_id=collective, has_side_effects=collective is not None,
                                vmem_limit_bytes=60 * 1024 * 1024)


PIECES = (2, 4, 4, 2, ROWS, TOK)
VMEM = pl.BlockSpec(memory_space=pltpu.VMEM)
ANY = pl.BlockSpec(memory_space=pl.ANY)


def gather_kernel(own, codes, out, all_codes, local, send, recv, csend, crecv):
    me = coords()
    barrier(me)
    gather(me, own, out, local, send, recv, gather_codes(me, codes, all_codes, csend, crecv))


DMA = pltpu.SemaphoreType.DMA
COPIES = 28


def gather_call(x, codes):
    return pl.pallas_call(
        gather_kernel,
        out_shape=(jax.ShapeDtypeStruct(PIECES, jnp.bfloat16), jax.ShapeDtypeStruct((2, 4, 8, 128), jnp.int32)),
        in_specs=[VMEM, VMEM], out_specs=(ANY, VMEM),
        scratch_shapes=[DMA, DMA((3, COPIES)), DMA((3, COPIES)), DMA((4,)), DMA((4,))],
        compiler_params=params(0), name="gather",
        cost_estimate=pl.CostEstimate(flops=0, bytes_accessed=150_000_000, transcendentals=0),
    )(x, codes)


def error_kernel(parts, base, err, out, local, send, recv, rsend, rrecv, *slots):
    me = coords()
    barrier(me)
    started = reduce_error(me, parts, base, err, slots, rsend, rrecv)
    gather(me, err, out, local, send, recv)
    for c in started:
        c.wait_send()


def error_call(parts, base):
    return pl.pallas_call(
        error_kernel,
        out_shape=(jax.ShapeDtypeStruct((ROWS, TOK), jnp.bfloat16), jax.ShapeDtypeStruct(PIECES, jnp.bfloat16)),
        in_specs=[VMEM, VMEM], out_specs=(VMEM, ANY),
        scratch_shapes=[DMA, DMA((3, COPIES)), DMA((3, COPIES)), DMA((3, 3, 6)), DMA((3, 3, 6)), *reduce_scratch()],
        compiler_params=params(1), name="error",
    )(parts, base)


D = 3584
SPAN = 128
CHUNK = 896


def pick(sel, g, mine, theirs, ws):
    ws[:SPAN, :] = mine[sel[g, 0]]
    ws[SPAN:, :] = theirs[sel[g, 1]]


def encode_kernel(sel, named, cen, mine, theirs, bias, part, lat, mask, ws):
    g = pl.program_id(0)
    pick(sel, g, mine, theirs, ws)
    pre = jnp.dot(ws[...], cen[0], preferred_element_type=jnp.float32)
    lane = lax.broadcasted_iota(jnp.int32, (SPAN, TOK), 1)
    for hh in range(2):
        rows = slice(hh * SPAN, (hh + 1) * SPAN)
        p = pre[rows] + bias[hh * 4 + sel[g, hh]]
        on = jnp.where(lane < SPAN, named[g, hh], named[g, 2 + hh])
        keep = (on > 0) & (p > 0)
        lat[0, rows] = jnp.where(keep, p, 0.0).astype(jnp.bfloat16)
        mask[0, rows] = jnp.where(keep, 1.0, 0.0).astype(jnp.bfloat16)
    for i in range(0, D, CHUNK):
        part[0, i : i + CHUNK] = lax.dot_general(
            ws[:, i : i + CHUNK], lat[0], (((0,), (0,)), ((), ())), preferred_element_type=jnp.float32
        ).astype(jnp.bfloat16)


def encode_call(sel, named, cen, mine, theirs, bias):
    per = lambda *shape: pl.BlockSpec((1, *shape), lambda g, *_: (g, 0, 0))
    return pl.pallas_call(
        encode_kernel,
        out_shape=(
            jax.ShapeDtypeStruct((8, D, TOK), jnp.bfloat16),
            jax.ShapeDtypeStruct((8, 2 * SPAN, TOK), jnp.bfloat16),
            jax.ShapeDtypeStruct((8, 2 * SPAN, TOK), jnp.bfloat16),
        ),
        grid_spec=pltpu.PrefetchScalarGridSpec(
            num_scalar_prefetch=2, grid=(8,),
            in_specs=[per(D, TOK), VMEM, VMEM, VMEM],
            out_specs=(per(D, TOK), per(2 * SPAN, TOK), per(2 * SPAN, TOK)),
            scratch_shapes=[pltpu.VMEM((2 * SPAN, D), jnp.bfloat16)],
        ),
        compiler_params=params(), name="encode",
    )(sel, named, cen, mine, theirs, bias)


def grad_kernel(sel, err, cen, lat, mask, mine, theirs, own, other, gb, ws, acc):
    g = pl.program_id(0)

    @pl.when(g == 0)
    def _():
        own[...] = jnp.zeros_like(own)
        acc[...] = jnp.zeros_like(acc)
        gb[...] = jnp.zeros_like(gb)

    pick(sel, g, mine, theirs, ws)
    back = jnp.dot(ws[...], err[0], preferred_element_type=jnp.float32)
    slope = jnp.where(mask[0] > 0, back, 0.0).astype(jnp.bfloat16)
    ones = jnp.ones((TOK, SPAN), jnp.bfloat16)
    sums = jnp.dot(slope, ones, preferred_element_type=jnp.float32).astype(jnp.bfloat16).astype(jnp.float32)
    for hh in range(2):
        gb[hh * 4 + sel[g, hh]] += sums[hh * SPAN : (hh + 1) * SPAN]
    for i in range(0, D, CHUNK):
        nt = (((1,), (1,)), ((), ()))
        t = lax.dot_general(lat[0], err[0, i : i + CHUNK], nt, preferred_element_type=jnp.float32)
        t = t + lax.dot_general(slope, cen[0, i : i + CHUNK], nt, preferred_element_type=jnp.float32)
        t = t.astype(jnp.bfloat16).astype(jnp.float32)
        own[sel[g, 0], :, i : i + CHUNK] += t[:SPAN]
        acc[sel[g, 1], :, i : i + CHUNK] += t[SPAN:]

    @pl.when(g == 7)
    def _():
        for b in range(4):
            other[b] = acc[b].astype(jnp.bfloat16)


def grad_call(sel, err, cen, lat, mask, mine, theirs):
    per = lambda *shape: pl.BlockSpec((1, *shape), lambda g, *_: (g, 0, 0))
    return pl.pallas_call(
        grad_kernel,
        out_shape=(
            jax.ShapeDtypeStruct((4, SPAN, D), jnp.float32),
            jax.ShapeDtypeStruct((4, SPAN, D), jnp.bfloat16),
            jax.ShapeDtypeStruct((8, SPAN, SPAN), jnp.float32),
        ),
        grid_spec=pltpu.PrefetchScalarGridSpec(
            num_scalar_prefetch=1, grid=(8,),
            in_specs=[per(D, TOK), per(D, TOK), per(2 * SPAN, TOK), per(2 * SPAN, TOK), VMEM, VMEM],
            out_specs=(VMEM, VMEM, VMEM),
            scratch_shapes=[pltpu.VMEM((2 * SPAN, D), jnp.bfloat16), pltpu.VMEM((4, SPAN, D), jnp.float32)],
        ),
        compiler_params=params(), name="grad",
    )(sel, err, cen, lat, mask, mine, theirs)


NAMES = ("x", "zh", "zl", "y", "c")
SWAP = [(0, 1), (1, 0)]


def step(activations, dictionary, enc_bias, dec_bias, block_codes):
    d = lax.axis_index("x") * 2 + lax.axis_index("zh")
    c = lax.axis_index("c")
    chip = lax.axis_index("zl") * 4 + lax.axis_index("y")
    mine = dictionary.reshape(4, SPAN, D)
    theirs = lax.ppermute(mine, "c", SWAP)
    bias_theirs = lax.ppermute(enc_bias, "c", SWAP)
    codes = lax.dynamic_index_in_dim(block_codes, d, axis=1, keepdims=False)
    codes = jnp.pad(codes.reshape(1, 32), ((0, 7), (0, 96)), constant_values=-1)
    act_t = activations.T.astype(jnp.float32)
    dec = lax.dynamic_slice_in_dim(dec_bias, d * ROWS, ROWS)[:, None]
    cen, codes = gather_call((act_t - dec).astype(jnp.bfloat16), codes)
    cen = cen.reshape(8, D, TOK)
    codes = codes.reshape(8, 8, 128)[:, 0, :32].reshape(8, 2, 16)
    first = d * 64 + (chip * 2 + jnp.stack([c, 1 - c])) * 4
    local = codes[:, :, None, :] - first[:, None]
    hit = (codes[:, :, None, :] >= 0) & (local >= 0) & (local < 4)
    named = jnp.any(hit, axis=3).astype(jnp.int32).reshape(8, 4)
    sel = jnp.max(jnp.where(hit, local, 0), axis=(1, 3)).astype(jnp.int32)
    bias = jnp.concatenate([enc_bias, bias_theirs]).astype(jnp.float32).reshape(8, SPAN, 1)
    part, lat, mask = encode_call(sel, named, cen, mine, theirs, bias)
    err_own, err = error_call(part.reshape(PIECES), dec - act_t)
    own, other, gb = grad_call(sel, err.reshape(8, D, TOK), cen, lat, mask, mine, theirs)
    gb = gb[:, :, 0]
    grad_w = own + lax.ppermute(other, "c", SWAP).astype(jnp.float32)
    grad_b = gb[:4] + lax.ppermute(gb[4:], "c", SWAP)
    return err_own.T, grad_w.reshape(4 * SPAN, D), grad_b.reshape(4 * SPAN)


def solution(mesh):
    split = Mesh(mesh.devices.reshape(4, 2, 2, 4, 2), NAMES)
    dict_, dp = ("x", "zh"), ("zl", "y", "c")
    rows = P((*dict_, *dp))
    return jax.shard_map(
        step, mesh=split,
        in_specs=(P(dp, dict_), P((*dict_, *dp), None), rows, P(), P(dp, None, None)),
        out_specs=(P(dp, dict_), P((*dict_, *dp), None), rows),
        check_vma=False,
    )
```

```python
import functools
import jax, jax.numpy as jnp
from jax import lax
from jax.experimental import pallas as pl
from jax.experimental.pallas import tpu as pltpu
from jax.sharding import Mesh, PartitionSpec as P

ROWS, TOK = 448, 256
D, SPAN = 3584, 128
C0 = (0, 144, 288)
CN = (144, 144, 160)
CH = (80, 64, 80)
ORDER = (("x", "y", "z"), ("y", "z", "x"), ("z", "x", "y"))


def coords():
    x, y = lax.axis_index("x"), lax.axis_index("y")
    z = lax.axis_index("zh") * 2 + lax.axis_index("zl")
    return {"x": x, "y": y, "z": z}


def shift(me, dim, by):
    return lax.rem(me[dim] + (by + 4), 4)


def device(dim, value):
    if dim == "z":
        return {"zh": value // 2, "zl": lax.rem(value, 2)}
    return {dim: value}


def region(ref, at, lo, n):
    z = at["z"]
    zl = slice(None) if z is None else lax.rem(z, 2)
    zh = slice(None) if z is None else z // 2
    y = slice(None) if at["y"] is None else at["y"]
    x = slice(None) if at["x"] is None else at["x"]
    return ref.at[zl, y, x, zh, pl.ds(lo, n), :]


def remote(src, dst, send, recv, dim, value):
    return pltpu.make_async_remote_copy(
        src_ref=src, dst_ref=dst, send_sem=send, recv_sem=recv,
        device_id=device(dim, value), device_id_type=pl.DeviceIdType.MESH)


def barrier(me, cores=False):
    sem = pltpu.get_barrier_semaphore()
    for dim in ("x", "y", "z"):
        for by in (-1, 1):
            pl.semaphore_signal(sem, inc=1, device_id=device(dim, shift(me, dim, by)),
                                device_id_type=pl.DeviceIdType.MESH)
    if cores:
        pl.semaphore_signal(sem, inc=1, device_id={"c": 1 - lax.axis_index("c")}, device_id_type=pl.DeviceIdType.MESH)
    pl.semaphore_wait(sem, 7 if cores else 6)


NEAR = ((0, 1), (1, -1))


def gather(me, own, out, local, send, recv, beside=iter(())):
    mine = pltpu.make_async_copy(own, region(out, me, 0, ROWS), local)
    mine.start()
    copies = [{} for _ in range(3)]

    def go(k, phase, name, at, by, lo=0, n=None, src=None):
        order = ORDER[k]
        where = {d: (None if i < phase - 1 else shift(me, d, at.get(i, 0))) for i, d in enumerate(order)}
        part = region(out, where, C0[k] + lo, CN[k] if n is None else n)
        dim = order[phase]
        i = len(copies[k])
        c = remote(part if src is None else src, part, send.at[k, i], recv.at[k, i], dim, shift(me, dim, by))
        c.start()
        copies[k][(phase, *name)] = c

    def got(k, *name):
        copies[k][name].wait_recv()

    for k in range(3):
        src = own.at[pl.ds(C0[k], CN[k]), :]
        for s, by in NEAR:
            go(k, 0, ("near", s), {}, by, src=src)
        for s, by in NEAR:
            go(k, 1, ("near", 0, s), {}, by, src=src)
    next(beside, None)
    for k in range(3):
        for s, by in NEAR:
            got(k, 0, "near", s)
            lo, n = (0, CH[k]) if s == 0 else (CH[k], CN[k] - CH[k])
            go(k, 0, ("far", s), {0: -by}, by, lo, n)
        for j in (-1, 1):
            for s, by in NEAR:
                go(k, 1, ("near", j, s), {0: j}, by)
    mine.wait()
    next(beside, None)
    for k in range(3):
        got(k, 0, "far", 0)
        got(k, 0, "far", 1)
        for s, by in NEAR:
            go(k, 1, ("near", 2, s), {0: 2}, by)
        for s, by in NEAR:
            go(k, 2, ("near", 0, s), {1: 0}, by)
    for phase in (1, 2):
        next(beside, None)
        for j in (0, -1, 1, 2):
            for k in range(3):
                for s, by in NEAR:
                    got(k, phase, "near", j, s)
                    if (j in (0, 1)) == (s == 0):
                        go(k, phase, ("far", j), {phase - 1: j, phase: -by}, by)
        if phase == 1:
            for k in range(3):
                for j in (-1, 1):
                    for s, by in NEAR:
                        go(k, 2, ("near", j, s), {1: j}, by)
        next(beside, None)
        for k in range(3):
            for j in (0, -1, 1, 2):
                got(k, phase, "far", j)
            if phase == 1:
                for s, by in NEAR:
                    go(k, 2, ("near", 2, s), {1: 2}, by)
    for k in range(3):
        for c in copies[k].values():
            c.wait_send()


def gather_codes(me, own, out, send, recv):
    zl = lax.rem(me["z"], 2)
    out[zl, me["y"]] = own[...]
    copies = []

    def go(src, dst, device_id):
        i = len(copies)
        c = pltpu.make_async_remote_copy(src_ref=src, dst_ref=dst, send_sem=send.at[i], recv_sem=recv.at[i],
                                         device_id=device_id, device_id_type=pl.DeviceIdType.MESH)
        c.start()
        copies.append(c)

    for by in (1, -1):
        go(own, out.at[zl, me["y"]], device("y", shift(me, "y", by)))
    yield
    copies[0].wait_recv()
    back = out.at[zl, shift(me, "y", -1)]
    go(back, back, device("y", shift(me, "y", 1)))
    yield
    copies[1].wait_recv()
    copies[2].wait_recv()
    go(out.at[zl], out.at[zl], {"zl": 1 - zl})
    yield
    copies[3].wait_recv()
    for c in copies:
        c.wait_send()


def held(ref, dims, at, lo, n):
    index = []
    for name in ("zl", "y", "x", "zh"):
        dim = name[0]
        if dim not in dims:
            continue
        value = at[dim]
        if value is None:
            index.append(slice(None))
        elif name == "zl":
            index.append(lax.rem(value, 2))
        elif name == "zh":
            index.append(value // 2)
        else:
            index.append(value)
    return ref.at[(*index, pl.ds(lo, n), slice(None))]


def lead(dims):
    return tuple(s for name, s in (("zl", 2), ("y", 4), ("x", 4), ("zh", 2)) if name[0] in dims)


def each(shape, body):
    total = 1
    for s in shape:
        total *= s
    if total == 1:
        body(())
        return

    def step(i, carry):
        index = []
        for s in reversed(shape):
            index.append(lax.rem(i, s))
            i = i // s
        body(tuple(reversed(index)))
        return carry

    lax.fori_loop(0, total, step, 0)


def reduce_scratch():
    shapes = []
    for k in range(3):
        n, h = CN[k], CH[k]
        for q in range(3):
            dims = lead(ORDER[k][: 2 - q])
            for rows in (h, n - h, h, n - h, h, n - h):
                shapes.append(pltpu.VMEM((*dims, rows, TOK), jnp.bfloat16))
            if q < 2:
                shapes.append(pltpu.VMEM((*dims, n, TOK), jnp.bfloat16))
    return shapes


def fill(k, at, sel, wt, lat, parts):
    dims = [d for d in ("z", "y", "x") if at[d] is None]
    lo, n = C0[k], CN[k]

    def one(index):
        where = {**at, **dict(zip(dims, index, strict=True))}
        zl, zh = lax.rem(where["z"], 2), where["z"] // 2
        g = zl * 4 + where["y"]
        rows = pl.ds(pl.multiple_of((where["x"] * 2 + zh) * ROWS + lo, 16), n)
        w = jnp.concatenate([wt[sel[g, 0], rows, :], wt[4 + sel[g, 1], rows, :]], axis=1)
        part = jnp.dot(w, lat[g], preferred_element_type=jnp.float32)
        parts[zl, where["y"], where["x"], zh, pl.ds(lo, n), :] = part.astype(jnp.bfloat16)

    each((4,) * len(dims), one)


def reduce_error(me, make, parts, base, err, slots, send, recv):
    slots = list(slots)
    table = []
    for k in range(3):
        row = []
        for q in range(3):
            row.append([slots.pop(0) for _ in range(7 if q < 2 else 6)])
        table.append(row)
    started = []

    def source(k, q, at, lo, n):
        if q == 0:
            return region(parts, at, C0[k] + lo, n)
        return held(table[k][q - 1][6], ORDER[k][: 3 - q], at, lo, n)

    for q in range(3):
        first = []
        for k in range(3):
            dim, rest = ORDER[k][2 - q], ORDER[k][: 2 - q]
            n, h = CN[k], CH[k]
            at = {d: (None if d in rest else me[d]) for d in me}
            far = {**at, dim: shift(me, dim, 2)}
            up, down = shift(me, dim, 1), shift(me, dim, -1)
            opp_p, opp_m, sum_p, raw_p, raw_m, sum_m = table[k][q][:6]
            if q == 0:
                make(k, far)
            copies = [
                remote(source(k, q, far, 0, h), opp_p, send.at[k, q, 0], recv.at[k, q, 0], dim, up),
                remote(source(k, q, far, h, n - h), opp_m, send.at[k, q, 1], recv.at[k, q, 1], dim, down),
            ]
            for c in copies:
                c.start()
            first.append(copies)
        for k in range(3):
            dim, rest = ORDER[k][2 - q], ORDER[k][: 2 - q]
            n, h = CN[k], CH[k]
            at = {d: (None if d in rest else me[d]) for d in me}
            up, down = shift(me, dim, 1), shift(me, dim, -1)
            opp_p, opp_m, sum_p, raw_p, raw_m, sum_m = table[k][q][:6]
            if q == 0:
                make(k, {**at, dim: up})
                make(k, {**at, dim: down})
            copies = [
                remote(source(k, q, {**at, dim: up}, h, n - h), raw_p, send.at[k, q, 2], recv.at[k, q, 2], dim, up),
                remote(source(k, q, {**at, dim: down}, 0, h), raw_m, send.at[k, q, 3], recv.at[k, q, 3], dim, down),
            ]
            for c in copies:
                c.start()
            first[k] += copies
            started += first[k]
        if q == 0:
            for k in range(3):
                make(k, {d: (None if d in ORDER[k][:2] else me[d]) for d in me})
        second = []
        for k in range(3):
            dim, rest = ORDER[k][2 - q], ORDER[k][: 2 - q]
            n, h = CN[k], CH[k]
            at = {d: (None if d in rest else me[d]) for d in me}
            up, down = shift(me, dim, 1), shift(me, dim, -1)
            opp_p, opp_m, sum_p, raw_p, raw_m, sum_m = table[k][q][:6]
            copies = []
            for s, (slot, to, lo, rows, into) in enumerate(((opp_p, up, 0, h, sum_p), (opp_m, down, h, n - h, sum_m))):
                first[k][s].wait_recv()
                own = source(k, q, {**at, dim: to}, lo, rows)

                def add(index, slot=slot, own=own):
                    a = slot[index].astype(jnp.float32) + own[index].astype(jnp.float32)
                    slot[index] = a.astype(jnp.bfloat16)

                each(lead(rest), add)
                c = remote(slot, into, send.at[k, q, 4 + s], recv.at[k, q, 4 + s], dim, to)
                c.start()
                copies.append(c)
            second.append(copies)
            started += copies
        for k in range(3):
            dim, rest = ORDER[k][2 - q], ORDER[k][: 2 - q]
            n, h = CN[k], CH[k]
            at = {d: (None if d in rest else me[d]) for d in me}
            opp_p, opp_m, sum_p, raw_p, raw_m, sum_m = table[k][q][:6]
            first[k][2].wait_recv()
            first[k][3].wait_recv()
            second[k][0].wait_recv()
            second[k][1].wait_recv()
            for lo, rows, a, b in ((0, h, sum_p, raw_m), (h, n - h, raw_p, sum_m)):
                own = source(k, q, at, lo, rows)

                def add(index, own=own, a=a, b=b, lo=lo, rows=rows):
                    total = own[index].astype(jnp.float32) + a[index].astype(jnp.float32) + b[index].astype(jnp.float32)
                    if q < 2:
                        table[k][q][6][(*index, pl.ds(lo, rows), slice(None))] = total.astype(jnp.bfloat16)
                    else:
                        at_rows = pl.ds(C0[k] + lo, rows)
                        err[at_rows, :] = (total + base[at_rows, :]).astype(jnp.bfloat16)

                each(lead(rest), add)
    return started


def params(collective=None):
    return pltpu.CompilerParams(collective_id=collective, has_side_effects=collective is not None,
                                vmem_limit_bytes=60 * 1024 * 1024)


PIECES = (2, 4, 4, 2, ROWS, TOK)
VMEM = pl.BlockSpec(memory_space=pltpu.VMEM)
ANY = pl.BlockSpec(memory_space=pl.ANY)


def turn(mine, wt, held_w, turned, sems, send, recv):
    load = pltpu.make_async_copy(mine, held_w, sems.at[0])
    load.start()
    yield
    yield
    yield
    load.wait()
    yield

    def block(i, carry):
        b, j = i // (D // SPAN), pl.multiple_of(lax.rem(i, D // SPAN) * SPAN, SPAN)
        turned[b, pl.ds(j, SPAN), :] = held_w[b, :, pl.ds(j, SPAN)].T
        return carry

    lax.fori_loop(0, 4 * (D // SPAN), block, 0)
    yield
    keep = pltpu.make_async_copy(turned, wt.at[pl.ds(0, 4)], sems.at[1])
    give = pltpu.make_async_remote_copy(
        src_ref=turned, dst_ref=wt.at[pl.ds(4, 4)], send_sem=send, recv_sem=recv,
        device_id={"c": 1 - lax.axis_index("c")}, device_id_type=pl.DeviceIdType.MESH)
    keep.start()
    give.start()
    yield
    keep.wait()
    give.wait()


def both(*steps):
    while True:
        done = [next(s, "end") for s in steps]
        if all(d == "end" for d in done):
            return
        yield


def gather_kernel(own, codes, mine, out, all_codes, wt, local, send, recv, csend, crecv, held_w, turned, sems, wsend, wrecv):
    me = coords()
    barrier(me, True)
    steps = both(gather_codes(me, codes, all_codes, csend, crecv), turn(mine, wt, held_w, turned, sems, wsend, wrecv))
    gather(me, own, out, local, send, recv, steps)
    for _ in steps:
        pass


DMA = pltpu.SemaphoreType.DMA
COPIES = 28


def gather_call(x, codes, mine):
    return pl.pallas_call(
        gather_kernel,
        out_shape=(
            jax.ShapeDtypeStruct(PIECES, jnp.bfloat16),
            jax.ShapeDtypeStruct((2, 4, 8, 128), jnp.int32),
            jax.ShapeDtypeStruct((8, D, SPAN), jnp.bfloat16),
        ),
        in_specs=[VMEM, VMEM, ANY], out_specs=(ANY, VMEM, ANY),
        scratch_shapes=[
            DMA, DMA((3, COPIES)), DMA((3, COPIES)), DMA((4,)), DMA((4,)),
            pltpu.VMEM((4, SPAN, D), jnp.bfloat16), pltpu.VMEM((4, D, SPAN), jnp.bfloat16), DMA((2,)), DMA, DMA,
        ],
        compiler_params=params(0), name="gather",
        cost_estimate=pl.CostEstimate(flops=0, bytes_accessed=150_000_000, transcendentals=0),
    )(x, codes, mine)


def error_kernel(sel, wt_hbm, lat, base, err, out, local, send, recv, rsend, rrecv, wt, wt_sem, parts, *slots):
    me = coords()
    load = pltpu.make_async_copy(wt_hbm, wt, wt_sem)
    load.start()
    barrier(me)
    load.wait()

    def make(k, at):
        fill(k, at, sel, wt, lat, parts)

    started = reduce_error(me, make, parts, base, err, slots, rsend, rrecv)
    gather(me, err, out, local, send, recv)
    for c in started:
        c.wait_send()


def error_call(sel, wt, lat, base):
    return pl.pallas_call(
        error_kernel,
        out_shape=(jax.ShapeDtypeStruct((ROWS, TOK), jnp.bfloat16), jax.ShapeDtypeStruct(PIECES, jnp.bfloat16)),
        in_specs=[pl.BlockSpec(memory_space=pltpu.SMEM), ANY, VMEM, VMEM], out_specs=(VMEM, ANY),
        scratch_shapes=[
            DMA, DMA((3, COPIES)), DMA((3, COPIES)), DMA((3, 3, 6)), DMA((3, 3, 6)),
            pltpu.VMEM((8, D, SPAN), jnp.bfloat16), DMA, pltpu.VMEM(PIECES, jnp.bfloat16), *reduce_scratch(),
        ],
        compiler_params=params(1), name="error",
    )(sel, wt, lat, base)


CHUNK = 896


def pick(sel, g, mine, theirs, ws):
    ws[:SPAN, :] = mine[sel[g, 0]]
    ws[SPAN:, :] = theirs[sel[g, 1]]


def encode_kernel(sel, named, cen, mine, theirs, bias, lat, mask, ws):
    g = pl.program_id(0)
    pick(sel, g, mine, theirs, ws)
    pre = jnp.dot(ws[...], cen[0], preferred_element_type=jnp.float32)
    lane = lax.broadcasted_iota(jnp.int32, (SPAN, TOK), 1)
    for hh in range(2):
        rows = slice(hh * SPAN, (hh + 1) * SPAN)
        p = pre[rows] + bias[hh * 4 + sel[g, hh]]
        on = jnp.where(lane < SPAN, named[g, hh], named[g, 2 + hh])
        keep = (on > 0) & (p > 0)
        lat[0, rows] = jnp.where(keep, p, 0.0).astype(jnp.bfloat16)
        mask[0, rows] = jnp.where(keep, 1.0, 0.0).astype(jnp.bfloat16)


def encode_call(sel, named, cen, mine, theirs, bias):
    per = lambda *shape: pl.BlockSpec((1, *shape), lambda g, *_: (g, 0, 0))
    return pl.pallas_call(
        encode_kernel,
        out_shape=(
            jax.ShapeDtypeStruct((8, 2 * SPAN, TOK), jnp.bfloat16),
            jax.ShapeDtypeStruct((8, 2 * SPAN, TOK), jnp.bfloat16),
        ),
        grid_spec=pltpu.PrefetchScalarGridSpec(
            num_scalar_prefetch=2, grid=(8,),
            in_specs=[per(D, TOK), VMEM, VMEM, VMEM],
            out_specs=(per(2 * SPAN, TOK), per(2 * SPAN, TOK)),
            scratch_shapes=[pltpu.VMEM((2 * SPAN, D), jnp.bfloat16)],
        ),
        compiler_params=params(), name="encode",
    )(sel, named, cen, mine, theirs, bias)


def grad_kernel(sel, err, cen, lat, mask, mine, theirs, own, other, gb, ws, acc):
    g = pl.program_id(0)

    @pl.when(g == 0)
    def _():
        own[...] = jnp.zeros_like(own)
        acc[...] = jnp.zeros_like(acc)
        gb[...] = jnp.zeros_like(gb)

    pick(sel, g, mine, theirs, ws)
    back = jnp.dot(ws[...], err[0], preferred_element_type=jnp.float32)
    slope = jnp.where(mask[0] > 0, back, 0.0).astype(jnp.bfloat16)
    ones = jnp.ones((TOK, SPAN), jnp.bfloat16)
    sums = jnp.dot(slope, ones, preferred_element_type=jnp.float32).astype(jnp.bfloat16).astype(jnp.float32)
    for hh in range(2):
        gb[hh * 4 + sel[g, hh]] += sums[hh * SPAN : (hh + 1) * SPAN]
    for i in range(0, D, CHUNK):
        nt = (((1,), (1,)), ((), ()))
        t = lax.dot_general(lat[0], err[0, i : i + CHUNK], nt, preferred_element_type=jnp.float32)
        t = t + lax.dot_general(slope, cen[0, i : i + CHUNK], nt, preferred_element_type=jnp.float32)
        t = t.astype(jnp.bfloat16).astype(jnp.float32)
        own[sel[g, 0], :, i : i + CHUNK] += t[:SPAN]
        acc[sel[g, 1], :, i : i + CHUNK] += t[SPAN:]

    @pl.when(g == 7)
    def _():
        for b in range(4):
            other[b] = acc[b].astype(jnp.bfloat16)


def grad_call(sel, err, cen, lat, mask, mine, theirs):
    per = lambda *shape: pl.BlockSpec((1, *shape), lambda g, *_: (g, 0, 0))
    return pl.pallas_call(
        grad_kernel,
        out_shape=(
            jax.ShapeDtypeStruct((4, SPAN, D), jnp.float32),
            jax.ShapeDtypeStruct((4, SPAN, D), jnp.bfloat16),
            jax.ShapeDtypeStruct((8, SPAN, SPAN), jnp.float32),
        ),
        grid_spec=pltpu.PrefetchScalarGridSpec(
            num_scalar_prefetch=1, grid=(8,),
            in_specs=[per(D, TOK), per(D, TOK), per(2 * SPAN, TOK), per(2 * SPAN, TOK), VMEM, VMEM],
            out_specs=(VMEM, VMEM, VMEM),
            scratch_shapes=[pltpu.VMEM((2 * SPAN, D), jnp.bfloat16), pltpu.VMEM((4, SPAN, D), jnp.float32)],
        ),
        compiler_params=params(), name="grad",
    )(sel, err, cen, lat, mask, mine, theirs)


NAMES = ("x", "zh", "zl", "y", "c")
SWAP = [(0, 1), (1, 0)]


def step(activations, dictionary, enc_bias, dec_bias, block_codes):
    d = lax.axis_index("x") * 2 + lax.axis_index("zh")
    c = lax.axis_index("c")
    chip = lax.axis_index("zl") * 4 + lax.axis_index("y")
    mine = dictionary.reshape(4, SPAN, D)
    theirs = lax.ppermute(mine, "c", SWAP)
    bias_theirs = lax.ppermute(enc_bias, "c", SWAP)
    codes = lax.dynamic_index_in_dim(block_codes, d, axis=1, keepdims=False)
    codes = jnp.pad(codes.reshape(1, 32), ((0, 7), (0, 96)), constant_values=-1)
    act_t = activations.T.astype(jnp.float32)
    dec = lax.dynamic_slice_in_dim(dec_bias, d * ROWS, ROWS)[:, None]
    cen, codes, wt = gather_call((act_t - dec).astype(jnp.bfloat16), codes, mine)
    cen = cen.reshape(8, D, TOK)
    codes = codes.reshape(8, 8, 128)[:, 0, :32].reshape(8, 2, 16)
    first = d * 64 + (chip * 2 + jnp.stack([c, 1 - c])) * 4
    local = codes[:, :, None, :] - first[:, None]
    hit = (codes[:, :, None, :] >= 0) & (local >= 0) & (local < 4)
    named = jnp.any(hit, axis=3).astype(jnp.int32).reshape(8, 4)
    sel = jnp.max(jnp.where(hit, local, 0), axis=(1, 3)).astype(jnp.int32)
    bias = jnp.concatenate([enc_bias, bias_theirs]).astype(jnp.float32).reshape(8, SPAN, 1)
    lat, mask = encode_call(sel, named, cen, mine, theirs, bias)
    err_own, err = error_call(sel, wt, lat, dec - act_t)
    own, other, gb = grad_call(sel, err.reshape(8, D, TOK), cen, lat, mask, mine, theirs)
    gb = gb[:, :, 0]
    grad_w = own + lax.ppermute(other, "c", SWAP).astype(jnp.float32)
    grad_b = gb[:4] + lax.ppermute(gb[4:], "c", SWAP)
    return err_own.T, grad_w.reshape(4 * SPAN, D), grad_b.reshape(4 * SPAN)


def solution(mesh):
    split = Mesh(mesh.devices.reshape(4, 2, 2, 4, 2), NAMES)
    dict_, dp = ("x", "zh"), ("zl", "y", "c")
    rows = P((*dict_, *dp))
    return jax.shard_map(
        step, mesh=split,
        in_specs=(P(dp, dict_), P((*dict_, *dp), None), rows, P(), P(dp, None, None)),
        out_specs=(P(dp, dict_), P((*dict_, *dp), None), rows),
        check_vma=False,
    )
```

```python
import functools
import jax, jax.numpy as jnp
from jax import lax
from jax.experimental import pallas as pl
from jax.experimental.pallas import tpu as pltpu
from jax.sharding import Mesh, PartitionSpec as P

ROWS, TOK = 448, 256
D, SPAN = 3584, 128
C0 = (0, 144, 288)
CN = (144, 144, 160)
CH = (80, 64, 80)
ORDER = (("x", "y", "z"), ("y", "z", "x"), ("z", "x", "y"))


def coords():
    x, y = lax.axis_index("x"), lax.axis_index("y")
    z = lax.axis_index("zh") * 2 + lax.axis_index("zl")
    return {"x": x, "y": y, "z": z}


def shift(me, dim, by):
    return lax.rem(me[dim] + (by + 4), 4)


def device(dim, value):
    if dim == "z":
        return {"zh": value // 2, "zl": lax.rem(value, 2)}
    return {dim: value}


def region(ref, at, lo, n):
    z = at["z"]
    zl = slice(None) if z is None else lax.rem(z, 2)
    zh = slice(None) if z is None else z // 2
    y = slice(None) if at["y"] is None else at["y"]
    x = slice(None) if at["x"] is None else at["x"]
    return ref.at[zl, y, x, zh, pl.ds(lo, n), :]


def remote(src, dst, send, recv, dim, value):
    return pltpu.make_async_remote_copy(
        src_ref=src, dst_ref=dst, send_sem=send, recv_sem=recv,
        device_id=device(dim, value), device_id_type=pl.DeviceIdType.MESH)


def barrier(me, cores=False):
    sem = pltpu.get_barrier_semaphore()
    for dim in ("x", "y", "z"):
        for by in (-1, 1):
            pl.semaphore_signal(sem, inc=1, device_id=device(dim, shift(me, dim, by)),
                                device_id_type=pl.DeviceIdType.MESH)
    if cores:
        pl.semaphore_signal(sem, inc=1, device_id={"c": 1 - lax.axis_index("c")}, device_id_type=pl.DeviceIdType.MESH)
    pl.semaphore_wait(sem, 7 if cores else 6)


NEAR = ((0, 1), (1, -1))


def gather(me, own, out, local, send, recv, beside=iter(())):
    mine = pltpu.make_async_copy(own, region(out, me, 0, ROWS), local)
    mine.start()
    copies = [{} for _ in range(3)]

    def go(k, phase, name, at, by, lo=0, n=None, src=None):
        order = ORDER[k]
        where = {d: (None if i < phase - 1 else shift(me, d, at.get(i, 0))) for i, d in enumerate(order)}
        part = region(out, where, C0[k] + lo, CN[k] if n is None else n)
        dim = order[phase]
        i = len(copies[k])
        c = remote(part if src is None else src, part, send.at[k, i], recv.at[k, i], dim, shift(me, dim, by))
        c.start()
        copies[k][(phase, *name)] = c

    def got(k, *name):
        copies[k][name].wait_recv()

    for k in range(3):
        src = own.at[pl.ds(C0[k], CN[k]), :]
        for s, by in NEAR:
            go(k, 0, ("near", s), {}, by, src=src)
        for s, by in NEAR:
            go(k, 1, ("near", 0, s), {}, by, src=src)
    next(beside, None)
    for k in range(3):
        for s, by in NEAR:
            got(k, 0, "near", s)
            lo, n = (0, CH[k]) if s == 0 else (CH[k], CN[k] - CH[k])
            go(k, 0, ("far", s), {0: -by}, by, lo, n)
        for j in (-1, 1):
            for s, by in NEAR:
                go(k, 1, ("near", j, s), {0: j}, by)
    mine.wait()
    next(beside, None)
    for k in range(3):
        got(k, 0, "far", 0)
        got(k, 0, "far", 1)
        for s, by in NEAR:
            go(k, 1, ("near", 2, s), {0: 2}, by)
        for s, by in NEAR:
            go(k, 2, ("near", 0, s), {1: 0}, by)
    for phase in (1, 2):
        next(beside, None)
        for j in (0, -1, 1, 2):
            for k in range(3):
                for s, by in NEAR:
                    got(k, phase, "near", j, s)
                    if (j in (0, 1)) == (s == 0):
                        go(k, phase, ("far", j), {phase - 1: j, phase: -by}, by)
        if phase == 1:
            for k in range(3):
                for j in (-1, 1):
                    for s, by in NEAR:
                        go(k, 2, ("near", j, s), {1: j}, by)
        next(beside, None)
        for k in range(3):
            for j in (0, -1, 1, 2):
                got(k, phase, "far", j)
            if phase == 1:
                for s, by in NEAR:
                    go(k, 2, ("near", 2, s), {1: 2}, by)
    for k in range(3):
        for c in copies[k].values():
            c.wait_send()


def gather_codes(me, own, out, send, recv):
    zl = lax.rem(me["z"], 2)
    out[zl, me["y"]] = own[...]
    copies = []

    def go(src, dst, device_id):
        i = len(copies)
        c = pltpu.make_async_remote_copy(src_ref=src, dst_ref=dst, send_sem=send.at[i], recv_sem=recv.at[i],
                                         device_id=device_id, device_id_type=pl.DeviceIdType.MESH)
        c.start()
        copies.append(c)

    for by in (1, -1):
        go(own, out.at[zl, me["y"]], device("y", shift(me, "y", by)))
    yield
    copies[0].wait_recv()
    back = out.at[zl, shift(me, "y", -1)]
    go(back, back, device("y", shift(me, "y", 1)))
    yield
    copies[1].wait_recv()
    copies[2].wait_recv()
    go(out.at[zl], out.at[zl], {"zl": 1 - zl})
    yield
    copies[3].wait_recv()
    for c in copies:
        c.wait_send()


def held(ref, dims, at, lo, n):
    index = []
    for name in ("zl", "y", "x", "zh"):
        dim = name[0]
        if dim not in dims:
            continue
        value = at[dim]
        if value is None:
            index.append(slice(None))
        elif name == "zl":
            index.append(lax.rem(value, 2))
        elif name == "zh":
            index.append(value // 2)
        else:
            index.append(value)
    return ref.at[(*index, pl.ds(lo, n), slice(None))]


def lead(dims):
    return tuple(s for name, s in (("zl", 2), ("y", 4), ("x", 4), ("zh", 2)) if name[0] in dims)


def each(shape, body):
    total = 1
    for s in shape:
        total *= s
    if total == 1:
        body(())
        return

    def step(i, carry):
        index = []
        for s in reversed(shape):
            index.append(lax.rem(i, s))
            i = i // s
        body(tuple(reversed(index)))
        return carry

    lax.fori_loop(0, total, step, 0)


def reduce_scratch():
    shapes = []
    for k in range(3):
        n, h = CN[k], CH[k]
        for q in range(3):
            dims = lead(ORDER[k][: 2 - q])
            for rows in (h, n - h, h, n - h, h, n - h):
                shapes.append(pltpu.VMEM((*dims, rows, TOK), jnp.bfloat16))
            if q < 2:
                shapes.append(pltpu.VMEM((*dims, n, TOK), jnp.bfloat16))
    return shapes


def fill(k, at, sel, wt, lat, parts):
    lo, n = C0[k], CN[k]

    def group(index):
        index = list(index)
        zl = index.pop(0) if at["z"] is None else lax.rem(at["z"], 2)
        y = index.pop(0) if at["y"] is None else at["y"]
        g = zl * 4 + y
        for zh in (0, 1) if at["z"] is None else (at["z"] // 2,):
            for x in range(4) if at["x"] is None else (at["x"],):
                rows = pl.ds(pl.multiple_of((x * 2 + zh) * ROWS + lo, 16), n)
                w = jnp.concatenate([wt[sel[g, 0], rows, :], wt[4 + sel[g, 1], rows, :]], axis=1)
                part = jnp.dot(w, lat[g], preferred_element_type=jnp.float32)
                parts[zl, y, x, zh, pl.ds(lo, n), :] = part.astype(jnp.bfloat16)

    each((2,) * (at["z"] is None) + (4,) * (at["y"] is None), group)


def reduce_error(me, make, parts, base, err, slots, send, recv):
    slots = list(slots)
    table = []
    for k in range(3):
        row = []
        for q in range(3):
            row.append([slots.pop(0) for _ in range(7 if q < 2 else 6)])
        table.append(row)
    started = []

    def source(k, q, at, lo, n):
        if q == 0:
            return region(parts, at, C0[k] + lo, n)
        return held(table[k][q - 1][6], ORDER[k][: 3 - q], at, lo, n)

    for q in range(3):
        first = []
        for k in range(3):
            dim, rest = ORDER[k][2 - q], ORDER[k][: 2 - q]
            n, h = CN[k], CH[k]
            at = {d: (None if d in rest else me[d]) for d in me}
            far = {**at, dim: shift(me, dim, 2)}
            up, down = shift(me, dim, 1), shift(me, dim, -1)
            opp_p, opp_m, sum_p, raw_p, raw_m, sum_m = table[k][q][:6]
            if q == 0:
                make(k, far)
            copies = [
                remote(source(k, q, far, 0, h), opp_p, send.at[k, q, 0], recv.at[k, q, 0], dim, up),
                remote(source(k, q, far, h, n - h), opp_m, send.at[k, q, 1], recv.at[k, q, 1], dim, down),
            ]
            for c in copies:
                c.start()
            first.append(copies)
        for k in range(3):
            dim, rest = ORDER[k][2 - q], ORDER[k][: 2 - q]
            n, h = CN[k], CH[k]
            at = {d: (None if d in rest else me[d]) for d in me}
            up, down = shift(me, dim, 1), shift(me, dim, -1)
            opp_p, opp_m, sum_p, raw_p, raw_m, sum_m = table[k][q][:6]
            if q == 0:
                make(k, {**at, dim: up})
                make(k, {**at, dim: down})
            copies = [
                remote(source(k, q, {**at, dim: up}, h, n - h), raw_p, send.at[k, q, 2], recv.at[k, q, 2], dim, up),
                remote(source(k, q, {**at, dim: down}, 0, h), raw_m, send.at[k, q, 3], recv.at[k, q, 3], dim, down),
            ]
            for c in copies:
                c.start()
            first[k] += copies
            started += first[k]
        second = []
        for k in range(3):
            dim, rest = ORDER[k][2 - q], ORDER[k][: 2 - q]
            n, h = CN[k], CH[k]
            at = {d: (None if d in rest else me[d]) for d in me}
            up, down = shift(me, dim, 1), shift(me, dim, -1)
            opp_p, opp_m, sum_p, raw_p, raw_m, sum_m = table[k][q][:6]
            copies = []
            for s, (slot, to, lo, rows, into) in enumerate(((opp_p, up, 0, h, sum_p), (opp_m, down, h, n - h, sum_m))):
                first[k][s].wait_recv()
                own = source(k, q, {**at, dim: to}, lo, rows)

                def add(index, slot=slot, own=own):
                    a = slot[index].astype(jnp.float32) + own[index].astype(jnp.float32)
                    slot[index] = a.astype(jnp.bfloat16)

                each(lead(rest), add)
                c = remote(slot, into, send.at[k, q, 4 + s], recv.at[k, q, 4 + s], dim, to)
                c.start()
                copies.append(c)
            second.append(copies)
            started += copies
        for k in range(3) if q == 0 else ():
            make(k, {d: (None if d in ORDER[k][:2] else me[d]) for d in me})
        for k in range(3):
            dim, rest = ORDER[k][2 - q], ORDER[k][: 2 - q]
            n, h = CN[k], CH[k]
            at = {d: (None if d in rest else me[d]) for d in me}
            opp_p, opp_m, sum_p, raw_p, raw_m, sum_m = table[k][q][:6]
            first[k][2].wait_recv()
            first[k][3].wait_recv()
            second[k][0].wait_recv()
            second[k][1].wait_recv()
            for lo, rows, a, b in ((0, h, sum_p, raw_m), (h, n - h, raw_p, sum_m)):
                own = source(k, q, at, lo, rows)

                def add(index, own=own, a=a, b=b, lo=lo, rows=rows):
                    total = own[index].astype(jnp.float32) + a[index].astype(jnp.float32) + b[index].astype(jnp.float32)
                    if q < 2:
                        table[k][q][6][(*index, pl.ds(lo, rows), slice(None))] = total.astype(jnp.bfloat16)
                    else:
                        at_rows = pl.ds(C0[k] + lo, rows)
                        err[at_rows, :] = (total + base[at_rows, :]).astype(jnp.bfloat16)

                each(lead(rest), add)
    return started


def params(collective=None):
    return pltpu.CompilerParams(collective_id=collective, has_side_effects=collective is not None,
                                vmem_limit_bytes=60 * 1024 * 1024)


PIECES = (2, 4, 4, 2, ROWS, TOK)
VMEM = pl.BlockSpec(memory_space=pltpu.VMEM)
ANY = pl.BlockSpec(memory_space=pl.ANY)


def turn(mine, bias, theirs, biases, wt, held_w, turned, sems, send, recv):
    def give(i, src, dst):
        c = pltpu.make_async_remote_copy(
            src_ref=src, dst_ref=dst, send_sem=send.at[i], recv_sem=recv.at[i],
            device_id={"c": 1 - lax.axis_index("c")}, device_id_type=pl.DeviceIdType.MESH)
        c.start()
        return c

    load = pltpu.make_async_copy(mine, held_w, sems.at[0])
    load.start()
    given = [give(0, mine, theirs), give(1, bias, biases.at[1])]
    biases[0] = bias[...]
    yield
    yield
    yield
    load.wait()
    yield

    def block(i, carry):
        b, j = i // (D // SPAN), pl.multiple_of(lax.rem(i, D // SPAN) * SPAN, SPAN)
        turned[b, pl.ds(j, SPAN), :] = held_w[b, :, pl.ds(j, SPAN)].T
        return carry

    lax.fori_loop(0, 4 * (D // SPAN), block, 0)
    yield
    keep = pltpu.make_async_copy(turned, wt.at[pl.ds(0, 4)], sems.at[1])
    keep.start()
    given.append(give(2, turned, wt.at[pl.ds(4, 4)]))
    yield
    keep.wait()
    for c in given:
        c.wait()


def both(*steps):
    while True:
        done = [next(s, "end") for s in steps]
        if all(d == "end" for d in done):
            return
        yield


def gather_kernel(own, codes, bias, mine, out, all_codes, biases, theirs, wt, local, send, recv, csend, crecv, held_w, turned, sems, wsend, wrecv):
    me = coords()
    barrier(me, True)
    steps = both(gather_codes(me, codes, all_codes, csend, crecv), turn(mine, bias, theirs, biases, wt, held_w, turned, sems, wsend, wrecv))
    gather(me, own, out, local, send, recv, steps)
    for _ in steps:
        pass


DMA = pltpu.SemaphoreType.DMA
COPIES = 28


def gather_call(x, codes, bias, mine):
    return pl.pallas_call(
        gather_kernel,
        out_shape=(
            jax.ShapeDtypeStruct(PIECES, jnp.bfloat16),
            jax.ShapeDtypeStruct((2, 4, 8, 128), jnp.int32),
            jax.ShapeDtypeStruct((2, 8, SPAN), jnp.float32),
            jax.ShapeDtypeStruct((4, SPAN, D), jnp.bfloat16),
            jax.ShapeDtypeStruct((8, D, SPAN), jnp.bfloat16),
        ),
        in_specs=[VMEM, VMEM, VMEM, ANY], out_specs=(ANY, VMEM, VMEM, ANY, ANY),
        scratch_shapes=[
            DMA, DMA((3, COPIES)), DMA((3, COPIES)), DMA((4,)), DMA((4,)),
            pltpu.VMEM((4, SPAN, D), jnp.bfloat16), pltpu.VMEM((4, D, SPAN), jnp.bfloat16), DMA((2,)), DMA((3,)), DMA((3,)),
        ],
        compiler_params=params(0), name="gather",
        cost_estimate=pl.CostEstimate(flops=0, bytes_accessed=150_000_000, transcendentals=0),
    )(x, codes, bias, mine)


def error_kernel(sel, wt_hbm, lat, base, err, out, local, send, recv, rsend, rrecv, wt, wt_sem, parts, *slots):
    me = coords()
    load = pltpu.make_async_copy(wt_hbm, wt, wt_sem)
    load.start()
    barrier(me)
    load.wait()

    def make(k, at):
        fill(k, at, sel, wt, lat, parts)

    started = reduce_error(me, make, parts, base, err, slots, rsend, rrecv)
    gather(me, err, out, local, send, recv)
    for c in started:
        c.wait_send()


def error_call(sel, wt, lat, base):
    return pl.pallas_call(
        error_kernel,
        out_shape=(jax.ShapeDtypeStruct((ROWS, TOK), jnp.bfloat16), jax.ShapeDtypeStruct(PIECES, jnp.bfloat16)),
        in_specs=[pl.BlockSpec(memory_space=pltpu.SMEM), ANY, VMEM, VMEM], out_specs=(VMEM, ANY),
        scratch_shapes=[
            DMA, DMA((3, COPIES)), DMA((3, COPIES)), DMA((3, 3, 6)), DMA((3, 3, 6)),
            pltpu.VMEM((8, D, SPAN), jnp.bfloat16), DMA, pltpu.VMEM(PIECES, jnp.bfloat16), *reduce_scratch(),
        ],
        compiler_params=params(1), name="error",
    )(sel, wt, lat, base)


CHUNK = 896


def pick(mine, theirs, ws):
    ws[:SPAN, :] = mine[0]
    ws[SPAN:, :] = theirs[0]


def encode_kernel(table, cen, mine, theirs, bias, lat, mask, ws):
    g = pl.program_id(0)
    pick(mine, theirs, ws)
    pre = jnp.dot(ws[...], cen[0], preferred_element_type=jnp.float32)
    lane = lax.broadcasted_iota(jnp.int32, (SPAN, TOK), 1)
    for hh in range(2):
        rows = slice(hh * SPAN, (hh + 1) * SPAN)
        chosen = lax.broadcasted_iota(jnp.int32, (8, TOK), 0) == table[g, hh]
        p = pre[rows] + lax.dot_general(
            bias[hh].astype(jnp.bfloat16), jnp.where(chosen, 1.0, 0.0).astype(jnp.bfloat16),
            (((0,), (0,)), ((), ())), preferred_element_type=jnp.float32)
        on = jnp.where(lane < SPAN, table[g, 2 + hh], table[g, 4 + hh])
        keep = (on > 0) & (p > 0)
        lat[0, rows] = jnp.where(keep, p, 0.0).astype(jnp.bfloat16)
        mask[0, rows] = jnp.where(keep, 1.0, 0.0).astype(jnp.bfloat16)


def encode_call(table, cen, mine, theirs, bias):
    per = lambda *shape: pl.BlockSpec((1, *shape), lambda g, *_: (g, 0, 0))
    block = lambda hh: pl.BlockSpec((1, SPAN, D), lambda g, t: (t[g, hh], 0, 0))
    return pl.pallas_call(
        encode_kernel,
        out_shape=(
            jax.ShapeDtypeStruct((8, 2 * SPAN, TOK), jnp.bfloat16),
            jax.ShapeDtypeStruct((8, 2 * SPAN, TOK), jnp.bfloat16),
        ),
        grid_spec=pltpu.PrefetchScalarGridSpec(
            num_scalar_prefetch=1, grid=(8,),
            in_specs=[per(D, TOK), block(0), block(1), VMEM],
            out_specs=(per(2 * SPAN, TOK), per(2 * SPAN, TOK)),
            scratch_shapes=[pltpu.VMEM((2 * SPAN, D), jnp.bfloat16)],
        ),
        compiler_params=params(), name="encode",
    )(table, cen, mine, theirs, bias)


def grad_kernel(sel, err, cen, lat, mask, mine, theirs, own, other, gb, ws, acc):
    g = pl.program_id(0)

    @pl.when(g == 0)
    def _():
        own[...] = jnp.zeros_like(own)
        acc[...] = jnp.zeros_like(acc)
        gb[...] = jnp.zeros_like(gb)

    pick(mine, theirs, ws)
    back = jnp.dot(ws[...], err[0], preferred_element_type=jnp.float32)
    slope = jnp.where(mask[0] > 0, back, 0.0).astype(jnp.bfloat16)
    sums = lax.dot_general(jnp.ones((8, TOK), jnp.bfloat16), slope, (((1,), (1,)), ((), ())), preferred_element_type=jnp.float32)
    sums = sums.astype(jnp.bfloat16).astype(jnp.float32)
    row = lax.broadcasted_iota(jnp.int32, (8, SPAN), 0)
    for hh in range(2):
        gb[hh] += jnp.where(row == sel[g, hh], sums[:, hh * SPAN : (hh + 1) * SPAN], 0.0)
    for i in range(0, D, CHUNK):
        nt = (((1,), (1,)), ((), ()))
        t = lax.dot_general(lat[0], err[0, i : i + CHUNK], nt, preferred_element_type=jnp.float32)
        t = t + lax.dot_general(slope, cen[0, i : i + CHUNK], nt, preferred_element_type=jnp.float32)
        t = t.astype(jnp.bfloat16).astype(jnp.float32)
        own[sel[g, 0], :, i : i + CHUNK] += t[:SPAN]
        acc[sel[g, 1], :, i : i + CHUNK] += t[SPAN:]

    @pl.when(g == 7)
    def _():
        for b in range(4):
            other[b] = acc[b].astype(jnp.bfloat16)


def grad_call(sel, err, cen, lat, mask, mine, theirs):
    per = lambda *shape: pl.BlockSpec((1, *shape), lambda g, *_: (g, 0, 0))
    block = lambda hh: pl.BlockSpec((1, SPAN, D), lambda g, t: (t[g, hh], 0, 0))
    return pl.pallas_call(
        grad_kernel,
        out_shape=(
            jax.ShapeDtypeStruct((4, SPAN, D), jnp.float32),
            jax.ShapeDtypeStruct((4, SPAN, D), jnp.bfloat16),
            jax.ShapeDtypeStruct((2, 8, SPAN), jnp.float32),
        ),
        grid_spec=pltpu.PrefetchScalarGridSpec(
            num_scalar_prefetch=1, grid=(8,),
            in_specs=[per(D, TOK), per(D, TOK), per(2 * SPAN, TOK), per(2 * SPAN, TOK), block(0), block(1)],
            out_specs=(VMEM, VMEM, VMEM),
            scratch_shapes=[pltpu.VMEM((2 * SPAN, D), jnp.bfloat16), pltpu.VMEM((4, SPAN, D), jnp.float32)],
        ),
        compiler_params=params(), name="grad",
    )(sel, err, cen, lat, mask, mine, theirs)


NAMES = ("x", "zh", "zl", "y", "c")
SWAP = [(0, 1), (1, 0)]


def step(activations, dictionary, enc_bias, dec_bias, block_codes):
    d = lax.axis_index("x") * 2 + lax.axis_index("zh")
    c = lax.axis_index("c")
    chip = lax.axis_index("zl") * 4 + lax.axis_index("y")
    mine = dictionary.reshape(4, SPAN, D)
    codes = lax.dynamic_index_in_dim(block_codes, d, axis=1, keepdims=False)
    codes = jnp.pad(codes.reshape(1, 32), ((0, 7), (0, 96)), constant_values=-1)
    act_t = activations.T.astype(jnp.float32)
    dec = lax.dynamic_slice_in_dim(dec_bias, d * ROWS, ROWS)[:, None]
    bias = jnp.pad(enc_bias.astype(jnp.float32).reshape(4, SPAN), ((0, 4), (0, 0)))
    cen, codes, biases, theirs, wt = gather_call((act_t - dec).astype(jnp.bfloat16), codes, bias, mine)
    cen = cen.reshape(8, D, TOK)
    codes = codes.reshape(8, 8, 128)[:, 0, :32].reshape(8, 2, 16)
    first = d * 64 + (chip * 2 + jnp.stack([c, 1 - c])) * 4
    local = codes[:, :, None, :] - first[:, None]
    hit = (codes[:, :, None, :] >= 0) & (local >= 0) & (local < 4)
    local = jnp.max(jnp.where(hit, local, -1), axis=3)
    table = jnp.concatenate([jnp.maximum(jnp.max(local, axis=1), 0), (local >= 0).astype(jnp.int32).reshape(8, 4)], axis=1)
    lat, mask = encode_call(table, cen, mine, theirs, biases)
    err_own, err = error_call(table, wt, lat, dec - act_t)
    own, other, gb = grad_call(table, err.reshape(8, D, TOK), cen, lat, mask, mine, theirs)
    grad_w = own + lax.ppermute(other, "c", SWAP).astype(jnp.float32)
    grad_b = (gb[0] + lax.ppermute(gb[1], "c", SWAP))[:4]
    return err_own.T, grad_w.reshape(4 * SPAN, D), grad_b.reshape(4 * SPAN)


def solution(mesh):
    split = Mesh(mesh.devices.reshape(4, 2, 2, 4, 2), NAMES)
    dict_, dp = ("x", "zh"), ("zl", "y", "c")
    rows = P((*dict_, *dp))
    return jax.shard_map(
        step, mesh=split,
        in_specs=(P(dp, dict_), P((*dict_, *dp), None), rows, P(), P(dp, None, None)),
        out_specs=(P(dp, dict_), P((*dict_, *dp), None), rows),
        check_vma=False,
    )
```

```python
import functools
import jax, jax.numpy as jnp
from jax import lax
from jax.experimental import pallas as pl
from jax.experimental.pallas import tpu as pltpu
from jax.sharding import Mesh, PartitionSpec as P

ROWS, TOK = 448, 256
D, SPAN = 3584, 128
C0 = (0, 144, 288)
CN = (144, 144, 160)
CH = (80, 64, 80)
ORDER = (("x", "y", "z"), ("y", "z", "x"), ("z", "x", "y"))


def coords():
    x, y = lax.axis_index("x"), lax.axis_index("y")
    z = lax.axis_index("zh") * 2 + lax.axis_index("zl")
    return {"x": x, "y": y, "z": z}


def shift(me, dim, by):
    return lax.rem(me[dim] + (by + 4), 4)


def device(dim, value):
    if dim == "z":
        return {"zh": value // 2, "zl": lax.rem(value, 2)}
    return {dim: value}


def region(ref, at, lo, n):
    z = at["z"]
    zl = slice(None) if z is None else lax.rem(z, 2)
    zh = slice(None) if z is None else z // 2
    y = slice(None) if at["y"] is None else at["y"]
    x = slice(None) if at["x"] is None else at["x"]
    return ref.at[zl, y, x, zh, pl.ds(lo, n), :]


def remote(src, dst, send, recv, dim, value):
    return pltpu.make_async_remote_copy(
        src_ref=src, dst_ref=dst, send_sem=send, recv_sem=recv,
        device_id=device(dim, value), device_id_type=pl.DeviceIdType.MESH)


def barrier(me, cores=False):
    sem = pltpu.get_barrier_semaphore()
    for dim in ("x", "y", "z"):
        for by in (-1, 1):
            pl.semaphore_signal(sem, inc=1, device_id=device(dim, shift(me, dim, by)),
                                device_id_type=pl.DeviceIdType.MESH)
    if cores:
        pl.semaphore_signal(sem, inc=1, device_id={"c": 1 - lax.axis_index("c")}, device_id_type=pl.DeviceIdType.MESH)
    pl.semaphore_wait(sem, 7 if cores else 6)


NEAR = ((0, 1), (1, -1))


def gather(me, own, out, local, send, recv, beside=iter(()), ready=lambda k: None):
    mine = pltpu.make_async_copy(own, region(out, me, 0, ROWS), local)
    copies = [{} for _ in range(3)]

    def go(k, phase, name, at, by, lo=0, n=None, src=None):
        order = ORDER[k]
        where = {d: (None if i < phase - 1 else shift(me, d, at.get(i, 0))) for i, d in enumerate(order)}
        part = region(out, where, C0[k] + lo, CN[k] if n is None else n)
        dim = order[phase]
        i = len(copies[k])
        c = remote(part if src is None else src, part, send.at[k, i], recv.at[k, i], dim, shift(me, dim, by))
        c.start()
        copies[k][(phase, *name)] = c

    def got(k, *name):
        copies[k][name].wait_recv()

    for k in range(3):
        ready(k)
        src = own.at[pl.ds(C0[k], CN[k]), :]
        for s, by in NEAR:
            go(k, 0, ("near", s), {}, by, src=src)
        for s, by in NEAR:
            go(k, 1, ("near", 0, s), {}, by, src=src)
    mine.start()
    next(beside, None)
    for k in range(3):
        for s, by in NEAR:
            got(k, 0, "near", s)
            lo, n = (0, CH[k]) if s == 0 else (CH[k], CN[k] - CH[k])
            go(k, 0, ("far", s), {0: -by}, by, lo, n)
        for j in (-1, 1):
            for s, by in NEAR:
                go(k, 1, ("near", j, s), {0: j}, by)
    mine.wait()
    next(beside, None)
    for k in range(3):
        got(k, 0, "far", 0)
        got(k, 0, "far", 1)
        for s, by in NEAR:
            go(k, 1, ("near", 2, s), {0: 2}, by)
        for s, by in NEAR:
            go(k, 2, ("near", 0, s), {1: 0}, by)
    for phase in (1, 2):
        next(beside, None)
        for j in (0, -1, 1, 2):
            for k in range(3):
                for s, by in NEAR:
                    got(k, phase, "near", j, s)
                    if (j in (0, 1)) == (s == 0):
                        go(k, phase, ("far", j), {phase - 1: j, phase: -by}, by)
        if phase == 1:
            for k in range(3):
                for j in (-1, 1):
                    for s, by in NEAR:
                        go(k, 2, ("near", j, s), {1: j}, by)
        next(beside, None)
        for k in range(3):
            for j in (0, -1, 1, 2):
                got(k, phase, "far", j)
            if phase == 1:
                for s, by in NEAR:
                    go(k, 2, ("near", 2, s), {1: 2}, by)
    for k in range(3):
        for c in copies[k].values():
            c.wait_send()


def gather_codes(me, own, out, send, recv):
    zl = lax.rem(me["z"], 2)
    out[zl, me["y"]] = own[...]
    copies = []

    def go(src, dst, device_id):
        i = len(copies)
        c = pltpu.make_async_remote_copy(src_ref=src, dst_ref=dst, send_sem=send.at[i], recv_sem=recv.at[i],
                                         device_id=device_id, device_id_type=pl.DeviceIdType.MESH)
        c.start()
        copies.append(c)

    for by in (1, -1):
        go(own, out.at[zl, me["y"]], device("y", shift(me, "y", by)))
    yield
    copies[0].wait_recv()
    back = out.at[zl, shift(me, "y", -1)]
    go(back, back, device("y", shift(me, "y", 1)))
    yield
    copies[1].wait_recv()
    copies[2].wait_recv()
    go(out.at[zl], out.at[zl], {"zl": 1 - zl})
    yield
    copies[3].wait_recv()
    for c in copies:
        c.wait_send()


def lead(dims):
    return tuple(s for name, s in (("zl", 2), ("y", 4), ("x", 4), ("zh", 2)) if name[0] in dims)


def each(shape, body):
    total = 1
    for s in shape:
        total *= s
    if total == 1:
        body(())
        return

    def step(i, carry):
        index = []
        for s in reversed(shape):
            index.append(lax.rem(i, s))
            i = i // s
        body(tuple(reversed(index)))
        return carry

    lax.fori_loop(0, total, step, 0)


SUBS = (2, -1, 1, 0)


def reduce_scratch():
    shapes = []
    for k in range(3):
        n, h = CN[k], CH[k]
        for q in (0, 0, 0, 0, 1, 2):
            dims = lead(ORDER[k][:1] if q < 2 else ())
            for rows in (h, n - h, h, n - h, h, n - h):
                shapes.append(pltpu.VMEM((*dims, rows, TOK), jnp.bfloat16))
    return shapes


class Reduction:
    def __init__(self, me, k, dim, at, parts, slots, send, recv, base):
        self.me, self.k, self.dim, self.at, self.parts, self.slots = me, k, dim, at, parts, slots
        self.send, self.recv, self.base = send, recv, base
        self.copies = {}
        self.lead = lead(tuple(d for d in at if d != dim and at[d] is None))
        self.halves = ((0, CH[k]), (CH[k], CN[k] - CH[k]))

    def source(self, by, half):
        lo, n = self.halves[half]
        return region(self.parts, {**self.at, self.dim: shift(self.me, self.dim, by)}, C0[self.k] + lo, n)

    def go(self, i, src, by):
        c = remote(src, self.slots[i], self.send.at[self.k, self.base + i], self.recv.at[self.k, self.base + i],
                   self.dim, shift(self.me, self.dim, by))
        c.start()
        self.copies[i] = c

    def far(self):
        self.go(0, self.source(2, 0), 1)
        self.go(1, self.source(2, 1), -1)

    def near(self):
        self.go(3, self.source(1, 1), 1)
        self.go(4, self.source(-1, 0), -1)

    def forward(self):
        for i, by in ((0, 1), (1, -1)):
            self.copies[i].wait_recv()
            slot, own = self.slots[i], self.source(by, i)

            def add(index, slot=slot, own=own):
                a = slot[index].astype(jnp.float32) + own[index].astype(jnp.float32)
                slot[index] = a.astype(jnp.bfloat16)

            each(self.lead, add)
            self.go(2 if i == 0 else 5, slot, by)

    def finish(self, store=None):
        for i in (3, 4, 2, 5):
            self.copies[i].wait_recv()
        for half, (i, j) in enumerate(((2, 4), (3, 5))):
            a, b, own = self.slots[i], self.slots[j], self.source(0, half)

            def add(index, a=a, b=b, own=own, half=half):
                total = own[index].astype(jnp.float32) + a[index].astype(jnp.float32) + b[index].astype(jnp.float32)
                if store is None:
                    own[index] = total.astype(jnp.bfloat16)
                else:
                    store(self.halves[half], total)

            each(self.lead, add)

    def drain(self):
        for c in self.copies.values():
            c.wait_send()


def fill(k, at, sel, wt, lat, parts):
    lo, n = C0[k], CN[k]

    def group(index):
        index = list(index)
        zl = index.pop(0) if at["z"] is None else lax.rem(at["z"], 2)
        y = index.pop(0) if at["y"] is None else at["y"]
        g = zl * 4 + y
        for zh in (0, 1) if at["z"] is None else (at["z"] // 2,):
            for x in range(4) if at["x"] is None else (at["x"],):
                rows = pl.ds(pl.multiple_of((x * 2 + zh) * ROWS + lo, 16), n)
                w = jnp.concatenate([wt[sel[g, 0], rows, :], wt[4 + sel[g, 1], rows, :]], axis=1)
                part = jnp.dot(w, lat[g], preferred_element_type=jnp.float32)
                parts[zl, y, x, zh, pl.ds(lo, n), :] = part.astype(jnp.bfloat16)

    each((2,) * (at["z"] is None) + (4,) * (at["y"] is None), group)


def reduce_error(me, make, parts, base, err, slots, send, recv):
    first, second, third = [], [], []
    for k in range(3):
        a, b, c = ORDER[k]
        mine = slots[36 * k : 36 * (k + 1)]
        at = {a: None, b: me[b], c: me[c]}

        def new(dim, at, i, k=k, mine=mine):
            return Reduction(me, k, dim, at, parts, mine[6 * i : 6 * i + 6], send, recv, 6 * i)

        first.append({m: new(c, {**at, b: shift(me, b, m)}, i) for i, m in enumerate(SUBS)})
        second.append(new(b, at, 4))
        third.append(new(a, {**at, a: me[a]}, 5))

    def whole(k, by):
        a, b, c = ORDER[k]
        make(k, {a: None, b: None, c: shift(me, c, by)})

    for k in range(3):
        whole(k, 2)
        for m in SUBS:
            first[k][m].far()
    for k in range(3):
        whole(k, 1)
        whole(k, -1)
        for m in SUBS:
            first[k][m].near()
    for m in SUBS:
        for k in range(3):
            first[k][m].forward()
    for k in range(3):
        whole(k, 0)
    for m in SUBS:
        for k in range(3):
            first[k][m].finish()
            if m == 2:
                second[k].far()
            elif m == 1:
                second[k].near()
    for k in range(3):
        second[k].forward()
    for k in range(3):
        second[k].finish()
        third[k].far()
        third[k].near()
    for k in range(3):
        third[k].forward()

    def last(k):
        def store(half, total):
            rows = pl.ds(C0[k] + half[0], half[1])
            err[rows, :] = (total + base[rows, :]).astype(jnp.bfloat16)

        third[k].finish(store)

    return last, [r for k in range(3) for r in (*first[k].values(), second[k], third[k])]


def params(collective=None):
    return pltpu.CompilerParams(collective_id=collective, has_side_effects=collective is not None,
                                vmem_limit_bytes=60 * 1024 * 1024)


PIECES = (2, 4, 4, 2, ROWS, TOK)
VMEM = pl.BlockSpec(memory_space=pltpu.VMEM)
ANY = pl.BlockSpec(memory_space=pl.ANY)


def turn(mine, bias, theirs, biases, wt, held_w, turned, sems, send, recv):
    def give(i, src, dst):
        c = pltpu.make_async_remote_copy(
            src_ref=src, dst_ref=dst, send_sem=send.at[i], recv_sem=recv.at[i],
            device_id={"c": 1 - lax.axis_index("c")}, device_id_type=pl.DeviceIdType.MESH)
        c.start()
        return c

    load = pltpu.make_async_copy(mine, held_w, sems.at[0])
    load.start()
    given = [give(0, mine, theirs), give(1, bias, biases.at[1])]
    biases[0] = bias[...]
    yield
    yield
    yield
    load.wait()
    yield

    def block(i, carry):
        b, j = i // (D // SPAN), pl.multiple_of(lax.rem(i, D // SPAN) * SPAN, SPAN)
        turned[b, pl.ds(j, SPAN), :] = held_w[b, :, pl.ds(j, SPAN)].T
        return carry

    lax.fori_loop(0, 4 * (D // SPAN), block, 0)
    yield
    keep = pltpu.make_async_copy(turned, wt.at[pl.ds(0, 4)], sems.at[1])
    keep.start()
    given.append(give(2, turned, wt.at[pl.ds(4, 4)]))
    yield
    keep.wait()
    for c in given:
        c.wait()


def both(*steps):
    while True:
        done = [next(s, "end") for s in steps]
        if all(d == "end" for d in done):
            return
        yield


def gather_kernel(own, codes, bias, mine, out, all_codes, biases, theirs, wt, local, send, recv, csend, crecv, held_w, turned, sems, wsend, wrecv):
    me = coords()
    barrier(me, True)
    steps = both(gather_codes(me, codes, all_codes, csend, crecv), turn(mine, bias, theirs, biases, wt, held_w, turned, sems, wsend, wrecv))
    gather(me, own, out, local, send, recv, steps)
    for _ in steps:
        pass


DMA = pltpu.SemaphoreType.DMA
COPIES = 28


def gather_call(x, codes, bias, mine):
    return pl.pallas_call(
        gather_kernel,
        out_shape=(
            jax.ShapeDtypeStruct(PIECES, jnp.bfloat16),
            jax.ShapeDtypeStruct((2, 4, 8, 128), jnp.int32),
            jax.ShapeDtypeStruct((2, 8, SPAN), jnp.float32),
            jax.ShapeDtypeStruct((4, SPAN, D), jnp.bfloat16),
            jax.ShapeDtypeStruct((8, D, SPAN), jnp.bfloat16),
        ),
        in_specs=[VMEM, VMEM, VMEM, ANY], out_specs=(ANY, VMEM, VMEM, ANY, ANY),
        scratch_shapes=[
            DMA, DMA((3, COPIES)), DMA((3, COPIES)), DMA((4,)), DMA((4,)),
            pltpu.VMEM((4, SPAN, D), jnp.bfloat16), pltpu.VMEM((4, D, SPAN), jnp.bfloat16), DMA((2,)), DMA((3,)), DMA((3,)),
        ],
        compiler_params=params(0), name="gather",
        cost_estimate=pl.CostEstimate(flops=0, bytes_accessed=150_000_000, transcendentals=0),
    )(x, codes, bias, mine)


def error_kernel(sel, wt_hbm, lat, base, err, out, local, send, recv, rsend, rrecv, wt, wt_sem, parts, *slots):
    me = coords()
    load = pltpu.make_async_copy(wt_hbm, wt, wt_sem)
    load.start()
    barrier(me)
    load.wait()

    def make(k, at):
        fill(k, at, sel, wt, lat, parts)

    last, reductions = reduce_error(me, make, parts, base, err, slots, rsend, rrecv)
    gather(me, err, out, local, send, recv, ready=last)
    for r in reductions:
        r.drain()


def error_call(sel, wt, lat, base):
    return pl.pallas_call(
        error_kernel,
        out_shape=(jax.ShapeDtypeStruct((ROWS, TOK), jnp.bfloat16), jax.ShapeDtypeStruct(PIECES, jnp.bfloat16)),
        in_specs=[pl.BlockSpec(memory_space=pltpu.SMEM), ANY, VMEM, VMEM], out_specs=(VMEM, ANY),
        scratch_shapes=[
            DMA, DMA((3, COPIES)), DMA((3, COPIES)), DMA((3, 36)), DMA((3, 36)),
            pltpu.VMEM((8, D, SPAN), jnp.bfloat16), DMA, pltpu.VMEM(PIECES, jnp.bfloat16), *reduce_scratch(),
        ],
        compiler_params=params(1), name="error",
    )(sel, wt, lat, base)


CHUNK = 896


def pick(mine, theirs, ws):
    ws[:SPAN, :] = mine[0]
    ws[SPAN:, :] = theirs[0]


def encode_kernel(table, cen, mine, theirs, bias, lat, mask, ws):
    g = pl.program_id(0)
    pick(mine, theirs, ws)
    pre = jnp.dot(ws[...], cen[0], preferred_element_type=jnp.float32)
    lane = lax.broadcasted_iota(jnp.int32, (SPAN, TOK), 1)
    for hh in range(2):
        rows = slice(hh * SPAN, (hh + 1) * SPAN)
        chosen = lax.broadcasted_iota(jnp.int32, (8, TOK), 0) == table[g, hh]
        p = pre[rows] + lax.dot_general(
            bias[hh].astype(jnp.bfloat16), jnp.where(chosen, 1.0, 0.0).astype(jnp.bfloat16),
            (((0,), (0,)), ((), ())), preferred_element_type=jnp.float32)
        on = jnp.where(lane < SPAN, table[g, 2 + hh], table[g, 4 + hh])
        keep = (on > 0) & (p > 0)
        lat[0, rows] = jnp.where(keep, p, 0.0).astype(jnp.bfloat16)
        mask[0, rows] = jnp.where(keep, 1.0, 0.0).astype(jnp.bfloat16)


def encode_call(table, cen, mine, theirs, bias):
    per = lambda *shape: pl.BlockSpec((1, *shape), lambda g, *_: (g, 0, 0))
    block = lambda hh: pl.BlockSpec((1, SPAN, D), lambda g, t: (t[g, hh], 0, 0))
    return pl.pallas_call(
        encode_kernel,
        out_shape=(
            jax.ShapeDtypeStruct((8, 2 * SPAN, TOK), jnp.bfloat16),
            jax.ShapeDtypeStruct((8, 2 * SPAN, TOK), jnp.bfloat16),
        ),
        grid_spec=pltpu.PrefetchScalarGridSpec(
            num_scalar_prefetch=1, grid=(8,),
            in_specs=[per(D, TOK), block(0), block(1), VMEM],
            out_specs=(per(2 * SPAN, TOK), per(2 * SPAN, TOK)),
            scratch_shapes=[pltpu.VMEM((2 * SPAN, D), jnp.bfloat16)],
        ),
        compiler_params=params(), name="encode",
    )(table, cen, mine, theirs, bias)


def grad_kernel(sel, err, cen, lat, mask, mine, theirs, own, other, gb, ws, mine_acc, acc):
    g = pl.program_id(0)

    @pl.when(g == 0)
    def _():
        mine_acc[...] = jnp.zeros_like(mine_acc)
        acc[...] = jnp.zeros_like(acc)
        gb[...] = jnp.zeros_like(gb)

    pick(mine, theirs, ws)
    back = jnp.dot(ws[...], err[0], preferred_element_type=jnp.float32)
    slope = jnp.where(mask[0] > 0, back, 0.0).astype(jnp.bfloat16)
    sums = lax.dot_general(jnp.ones((8, TOK), jnp.bfloat16), slope, (((1,), (1,)), ((), ())), preferred_element_type=jnp.float32)
    sums = sums.astype(jnp.bfloat16).astype(jnp.float32)
    row = lax.broadcasted_iota(jnp.int32, (8, SPAN), 0)
    for hh in range(2):
        gb[hh] += jnp.where(row == sel[g, hh], sums[:, hh * SPAN : (hh + 1) * SPAN], 0.0)
    for i in range(0, D, CHUNK):
        nt = (((1,), (1,)), ((), ()))
        t = lax.dot_general(lat[0], err[0, i : i + CHUNK], nt, preferred_element_type=jnp.float32)
        t = t + lax.dot_general(slope, cen[0, i : i + CHUNK], nt, preferred_element_type=jnp.float32)
        t = t.astype(jnp.bfloat16).astype(jnp.float32)
        mine_acc[sel[g, 0], :, i : i + CHUNK] += t[:SPAN]
        acc[sel[g, 1], :, i : i + CHUNK] += t[SPAN:]

    @pl.when(g == 7)
    def _():
        for b in range(4):
            own[b] = mine_acc[b].astype(jnp.bfloat16)
            other[b] = acc[b].astype(jnp.bfloat16)


def grad_call(sel, err, cen, lat, mask, mine, theirs):
    per = lambda *shape: pl.BlockSpec((1, *shape), lambda g, *_: (g, 0, 0))
    block = lambda hh: pl.BlockSpec((1, SPAN, D), lambda g, t: (t[g, hh], 0, 0))
    return pl.pallas_call(
        grad_kernel,
        out_shape=(
            jax.ShapeDtypeStruct((4, SPAN, D), jnp.bfloat16),
            jax.ShapeDtypeStruct((4, SPAN, D), jnp.bfloat16),
            jax.ShapeDtypeStruct((2, 8, SPAN), jnp.float32),
        ),
        grid_spec=pltpu.PrefetchScalarGridSpec(
            num_scalar_prefetch=1, grid=(8,),
            in_specs=[per(D, TOK), per(D, TOK), per(2 * SPAN, TOK), per(2 * SPAN, TOK), block(0), block(1)],
            out_specs=(VMEM, VMEM, VMEM),
            scratch_shapes=[pltpu.VMEM((2 * SPAN, D), jnp.bfloat16)] + [pltpu.VMEM((4, SPAN, D), jnp.float32)] * 2,
        ),
        compiler_params=params(), name="grad",
    )(sel, err, cen, lat, mask, mine, theirs)


NAMES = ("x", "zh", "zl", "y", "c")
SWAP = [(0, 1), (1, 0)]


def step(activations, dictionary, enc_bias, dec_bias, block_codes):
    d = lax.axis_index("x") * 2 + lax.axis_index("zh")
    c = lax.axis_index("c")
    chip = lax.axis_index("zl") * 4 + lax.axis_index("y")
    mine = dictionary.reshape(4, SPAN, D)
    codes = lax.dynamic_index_in_dim(block_codes, d, axis=1, keepdims=False)
    codes = jnp.pad(codes.reshape(1, 32), ((0, 7), (0, 96)), constant_values=-1)
    act_t = activations.T.astype(jnp.float32)
    dec = lax.dynamic_slice_in_dim(dec_bias, d * ROWS, ROWS)[:, None]
    bias = jnp.pad(enc_bias.astype(jnp.float32).reshape(4, SPAN), ((0, 4), (0, 0)))
    cen, codes, biases, theirs, wt = gather_call((act_t - dec).astype(jnp.bfloat16), codes, bias, mine)
    cen = cen.reshape(8, D, TOK)
    codes = codes.reshape(8, 8, 128)[:, 0, :32].reshape(8, 2, 16)
    first = d * 64 + (chip * 2 + jnp.stack([c, 1 - c])) * 4
    local = codes[:, :, None, :] - first[:, None]
    hit = (codes[:, :, None, :] >= 0) & (local >= 0) & (local < 4)
    local = jnp.max(jnp.where(hit, local, -1), axis=3)
    table = jnp.concatenate([jnp.maximum(jnp.max(local, axis=1), 0), (local >= 0).astype(jnp.int32).reshape(8, 4)], axis=1)
    lat, mask = encode_call(table, cen, mine, theirs, biases)
    err_own, err = error_call(table, wt, lat, dec - act_t)
    own, other, gb = grad_call(table, err.reshape(8, D, TOK), cen, lat, mask, mine, theirs)
    grad_w = own.astype(jnp.float32) + lax.ppermute(other, "c", SWAP).astype(jnp.float32)
    grad_b = (gb[0] + lax.ppermute(gb[1], "c", SWAP))[:4]
    return err_own.T, grad_w.reshape(4 * SPAN, D), grad_b.reshape(4 * SPAN)


def solution(mesh):
    split = Mesh(mesh.devices.reshape(4, 2, 2, 4, 2), NAMES)
    dict_, dp = ("x", "zh"), ("zl", "y", "c")
    rows = P((*dict_, *dp))
    return jax.shard_map(
        step, mesh=split,
        in_specs=(P(dp, dict_), P((*dict_, *dp), None), rows, P(), P(dp, None, None)),
        out_specs=(P(dp, dict_), P((*dict_, *dp), None), rows),
        check_vma=False,
    )
```

```python
import functools
import jax, jax.numpy as jnp
from jax import lax
from jax.experimental import pallas as pl
from jax.experimental.pallas import tpu as pltpu
from jax.sharding import Mesh, PartitionSpec as P

ROWS, TOK = 448, 256
D, SPAN = 3584, 128
C0 = (0, 144, 288)
CN = (144, 144, 160)
CH = (80, 64, 80)
ORDER = (("x", "y", "z"), ("y", "z", "x"), ("z", "x", "y"))


def coords():
    x, y = lax.axis_index("x"), lax.axis_index("y")
    z = lax.axis_index("zh") * 2 + lax.axis_index("zl")
    return {"x": x, "y": y, "z": z}


def shift(me, dim, by):
    return lax.rem(me[dim] + (by + 4), 4)


def device(dim, value):
    if dim == "z":
        return {"zh": value // 2, "zl": lax.rem(value, 2)}
    return {dim: value}


def region(ref, at, lo, n):
    z = at["z"]
    zl = slice(None) if z is None else lax.rem(z, 2)
    zh = slice(None) if z is None else z // 2
    y = slice(None) if at["y"] is None else at["y"]
    x = slice(None) if at["x"] is None else at["x"]
    return ref.at[zl, y, x, zh, pl.ds(lo, n), :]


def remote(src, dst, send, recv, dim, value):
    return pltpu.make_async_remote_copy(
        src_ref=src, dst_ref=dst, send_sem=send, recv_sem=recv,
        device_id=device(dim, value), device_id_type=pl.DeviceIdType.MESH)


def barrier(me, cores=False):
    sem = pltpu.get_barrier_semaphore()
    for dim in ("x", "y", "z"):
        for by in (-1, 1):
            pl.semaphore_signal(sem, inc=1, device_id=device(dim, shift(me, dim, by)),
                                device_id_type=pl.DeviceIdType.MESH)
    if cores:
        pl.semaphore_signal(sem, inc=1, device_id={"c": 1 - lax.axis_index("c")}, device_id_type=pl.DeviceIdType.MESH)
    pl.semaphore_wait(sem, 7 if cores else 6)


NEAR = ((0, 1), (1, -1))


def gather(me, own, out, local, send, recv, beside=iter(()), ready=lambda k: None):
    mine = pltpu.make_async_copy(own, region(out, me, 0, ROWS), local)
    copies = [{} for _ in range(3)]

    def go(k, phase, name, at, by, lo=0, n=None, src=None):
        order = ORDER[k]
        where = {d: (None if i < phase - 1 else shift(me, d, at.get(i, 0))) for i, d in enumerate(order)}
        part = region(out, where, C0[k] + lo, CN[k] if n is None else n)
        dim = order[phase]
        i = len(copies[k])
        c = remote(part if src is None else src, part, send.at[k, i], recv.at[k, i], dim, shift(me, dim, by))
        c.start()
        copies[k][(phase, *name)] = c

    def got(k, *name):
        copies[k][name].wait_recv()

    for k in range(3):
        ready(k)
        src = own.at[pl.ds(C0[k], CN[k]), :]
        for s, by in NEAR:
            go(k, 0, ("near", s), {}, by, src=src)
        for s, by in NEAR:
            go(k, 1, ("near", 0, s), {}, by, src=src)
    mine.start()
    next(beside, None)
    for k in range(3):
        for s, by in NEAR:
            got(k, 0, "near", s)
            lo, n = (0, CH[k]) if s == 0 else (CH[k], CN[k] - CH[k])
            go(k, 0, ("far", s), {0: -by}, by, lo, n)
        for j in (-1, 1):
            for s, by in NEAR:
                go(k, 1, ("near", j, s), {0: j}, by)
    mine.wait()
    next(beside, None)
    for k in range(3):
        got(k, 0, "far", 0)
        got(k, 0, "far", 1)
        for s, by in NEAR:
            go(k, 1, ("near", 2, s), {0: 2}, by)
        for s, by in NEAR:
            go(k, 2, ("near", 0, s), {1: 0}, by)
    for phase in (1, 2):
        next(beside, None)
        for j in (0, -1, 1, 2):
            for k in range(3):
                for s, by in NEAR:
                    got(k, phase, "near", j, s)
                    if (j in (0, 1)) == (s == 0):
                        go(k, phase, ("far", j), {phase - 1: j, phase: -by}, by)
        if phase == 1:
            for k in range(3):
                for j in (-1, 1):
                    for s, by in NEAR:
                        go(k, 2, ("near", j, s), {1: j}, by)
        next(beside, None)
        for k in range(3):
            for j in (0, -1, 1, 2):
                got(k, phase, "far", j)
            if phase == 1:
                for s, by in NEAR:
                    go(k, 2, ("near", 2, s), {1: 2}, by)
    for k in range(3):
        for c in copies[k].values():
            c.wait_send()


def gather_codes(me, own, out, send, recv):
    zl = lax.rem(me["z"], 2)
    out[zl, me["y"]] = own[...]
    copies = []

    def go(src, dst, device_id):
        i = len(copies)
        c = pltpu.make_async_remote_copy(src_ref=src, dst_ref=dst, send_sem=send.at[i], recv_sem=recv.at[i],
                                         device_id=device_id, device_id_type=pl.DeviceIdType.MESH)
        c.start()
        copies.append(c)

    for by in (1, -1):
        go(own, out.at[zl, me["y"]], device("y", shift(me, "y", by)))
    yield
    copies[0].wait_recv()
    back = out.at[zl, shift(me, "y", -1)]
    go(back, back, device("y", shift(me, "y", 1)))
    yield
    copies[1].wait_recv()
    copies[2].wait_recv()
    go(out.at[zl], out.at[zl], {"zl": 1 - zl})
    yield
    copies[3].wait_recv()
    for c in copies:
        c.wait_send()


def lead(dims):
    return tuple(s for name, s in (("zl", 2), ("y", 4), ("x", 4), ("zh", 2)) if name[0] in dims)


def each(shape, body):
    total = 1
    for s in shape:
        total *= s
    if total == 1:
        body(())
        return

    def step(i, carry):
        index = []
        for s in reversed(shape):
            index.append(lax.rem(i, s))
            i = i // s
        body(tuple(reversed(index)))
        return carry

    lax.fori_loop(0, total, step, 0)


SUBS = (2, -1, 1, 0)


def reduce_scratch():
    shapes = []
    for k in range(3):
        n, h = CN[k], CH[k]
        for q in (0, 0, 0, 0, 1, 2):
            dims = lead(ORDER[k][:1] if q < 2 else ())
            for rows in (h, n - h, h, n - h, h, n - h):
                shapes.append(pltpu.VMEM((*dims, rows, TOK), jnp.bfloat16))
    return shapes


class Reduction:
    def __init__(self, me, k, dim, at, parts, slots, send, recv, base):
        self.me, self.k, self.dim, self.at, self.parts, self.slots = me, k, dim, at, parts, slots
        self.send, self.recv, self.base = send, recv, base
        self.copies = {}
        self.lead = lead(tuple(d for d in at if d != dim and at[d] is None))
        self.halves = ((0, CH[k]), (CH[k], CN[k] - CH[k]))

    def source(self, by, half):
        lo, n = self.halves[half]
        return region(self.parts, {**self.at, self.dim: shift(self.me, self.dim, by)}, C0[self.k] + lo, n)

    def go(self, i, src, by):
        c = remote(src, self.slots[i], self.send.at[self.k, self.base + i], self.recv.at[self.k, self.base + i],
                   self.dim, shift(self.me, self.dim, by))
        c.start()
        self.copies[i] = c

    def far(self):
        self.go(0, self.source(2, 0), 1)
        self.go(1, self.source(2, 1), -1)

    def near(self):
        self.go(3, self.source(1, 1), 1)
        self.go(4, self.source(-1, 0), -1)

    def forward(self):
        for i, by in ((0, 1), (1, -1)):
            self.copies[i].wait_recv()
            slot, own = self.slots[i], self.source(by, i)

            def add(index, slot=slot, own=own):
                a = slot[index].astype(jnp.float32) + own[index].astype(jnp.float32)
                slot[index] = a.astype(jnp.bfloat16)

            each(self.lead, add)
            self.go(2 if i == 0 else 5, slot, by)

    def finish(self, store=None):
        for i in (3, 4, 2, 5):
            self.copies[i].wait_recv()
        for half, (i, j) in enumerate(((2, 4), (3, 5))):
            a, b, own = self.slots[i], self.slots[j], self.source(0, half)

            def add(index, a=a, b=b, own=own, half=half):
                total = own[index].astype(jnp.float32) + a[index].astype(jnp.float32) + b[index].astype(jnp.float32)
                if store is None:
                    own[index] = total.astype(jnp.bfloat16)
                else:
                    store(self.halves[half], total)

            each(self.lead, add)

    def drain(self):
        for c in self.copies.values():
            c.wait_send()


def fill(k, at, sel, wt, lat, parts):
    lo, n = C0[k], CN[k]

    def group(index):
        index = list(index)
        zl = index.pop(0) if at["z"] is None else lax.rem(at["z"], 2)
        y = index.pop(0) if at["y"] is None else at["y"]
        g = zl * 4 + y
        for zh in (0, 1) if at["z"] is None else (at["z"] // 2,):
            for x in range(4) if at["x"] is None else (at["x"],):
                rows = pl.ds(pl.multiple_of((x * 2 + zh) * ROWS + lo, 16), n)
                w = jnp.concatenate([wt[sel[g, 0], rows, :], wt[4 + sel[g, 1], rows, :]], axis=1)
                part = jnp.dot(w, lat[g], preferred_element_type=jnp.float32)
                parts[zl, y, x, zh, pl.ds(lo, n), :] = part.astype(jnp.bfloat16)

    each((2,) * (at["z"] is None) + (4,) * (at["y"] is None), group)


def reduce_error(me, make, parts, base, err, slots, send, recv):
    first, second, third = [], [], []
    for k in range(3):
        a, b, c = ORDER[k]
        mine = slots[36 * k : 36 * (k + 1)]
        at = {a: None, b: me[b], c: me[c]}

        def new(dim, at, i, k=k, mine=mine):
            return Reduction(me, k, dim, at, parts, mine[6 * i : 6 * i + 6], send, recv, 6 * i)

        first.append({m: new(c, {**at, b: shift(me, b, m)}, i) for i, m in enumerate(SUBS)})
        second.append(new(b, at, 4))
        third.append(new(a, {**at, a: me[a]}, 5))

    def whole(k, by):
        a, b, c = ORDER[k]
        make(k, {a: None, b: None, c: shift(me, c, by)})

    def push(m):
        for k in range(3):
            first[k][m].near()
            first[k][m].forward()

    for m in SUBS:
        for k in range(3):
            a, b, c = ORDER[k]
            make(k, {a: None, b: shift(me, b, m), c: shift(me, c, 2)})
            first[k][m].far()
    for k in range(3):
        whole(k, 1)
        whole(k, -1)
    push(2)
    push(-1)
    for k in range(3):
        whole(k, 0)
    for k in range(3):
        first[k][2].finish()
        second[k].far()
    push(1)
    for k in range(3):
        first[k][-1].finish()
    push(0)
    for k in range(3):
        first[k][1].finish()
        second[k].near()
    for k in range(3):
        second[k].forward()
    for k in range(3):
        first[k][0].finish()
    for k in range(3):
        second[k].finish()
        third[k].far()
        third[k].near()
    for k in range(3):
        third[k].forward()

    def last(k):
        def store(half, total):
            rows = pl.ds(C0[k] + half[0], half[1])
            err[rows, :] = (total + base[rows, :]).astype(jnp.bfloat16)

        third[k].finish(store)

    return last, [r for k in range(3) for r in (*first[k].values(), second[k], third[k])]


def params(collective=None):
    return pltpu.CompilerParams(collective_id=collective, has_side_effects=collective is not None,
                                vmem_limit_bytes=60 * 1024 * 1024)


PIECES = (2, 4, 4, 2, ROWS, TOK)
VMEM = pl.BlockSpec(memory_space=pltpu.VMEM)
ANY = pl.BlockSpec(memory_space=pl.ANY)


def turn(mine, bias, theirs, biases, wt, held_w, turned, sems, send, recv):
    def give(i, src, dst):
        c = pltpu.make_async_remote_copy(
            src_ref=src, dst_ref=dst, send_sem=send.at[i], recv_sem=recv.at[i],
            device_id={"c": 1 - lax.axis_index("c")}, device_id_type=pl.DeviceIdType.MESH)
        c.start()
        return c

    load = pltpu.make_async_copy(mine, held_w, sems.at[0])
    load.start()
    given = [give(0, mine, theirs), give(1, bias, biases.at[1])]
    biases[0] = bias[...]
    yield
    yield
    yield
    load.wait()
    yield

    def block(i, carry):
        b, j = i // (D // SPAN), pl.multiple_of(lax.rem(i, D // SPAN) * SPAN, SPAN)
        turned[b, pl.ds(j, SPAN), :] = held_w[b, :, pl.ds(j, SPAN)].T
        return carry

    lax.fori_loop(0, 4 * (D // SPAN), block, 0)
    yield
    keep = pltpu.make_async_copy(turned, wt.at[pl.ds(0, 4)], sems.at[1])
    keep.start()
    given.append(give(2, turned, wt.at[pl.ds(4, 4)]))
    yield
    keep.wait()
    for c in given:
        c.wait()


def both(*steps):
    while True:
        done = [next(s, "end") for s in steps]
        if all(d == "end" for d in done):
            return
        yield


def gather_kernel(own, codes, bias, mine, out, all_codes, biases, theirs, wt, local, send, recv, csend, crecv, held_w, turned, sems, wsend, wrecv):
    me = coords()
    barrier(me, True)
    steps = both(gather_codes(me, codes, all_codes, csend, crecv), turn(mine, bias, theirs, biases, wt, held_w, turned, sems, wsend, wrecv))
    gather(me, own, out, local, send, recv, steps)
    for _ in steps:
        pass


DMA = pltpu.SemaphoreType.DMA
COPIES = 28


def gather_call(x, codes, bias, mine):
    return pl.pallas_call(
        gather_kernel,
        out_shape=(
            jax.ShapeDtypeStruct(PIECES, jnp.bfloat16),
            jax.ShapeDtypeStruct((2, 4, 2, 8, 16), jnp.int32),
            jax.ShapeDtypeStruct((2, 8, SPAN), jnp.float32),
            jax.ShapeDtypeStruct((4, SPAN, D), jnp.bfloat16),
            jax.ShapeDtypeStruct((8, D, SPAN), jnp.bfloat16),
        ),
        in_specs=[VMEM, VMEM, VMEM, ANY], out_specs=(ANY, VMEM, VMEM, ANY, ANY),
        scratch_shapes=[
            DMA, DMA((3, COPIES)), DMA((3, COPIES)), DMA((4,)), DMA((4,)),
            pltpu.VMEM((4, SPAN, D), jnp.bfloat16), pltpu.VMEM((4, D, SPAN), jnp.bfloat16), DMA((2,)), DMA((3,)), DMA((3,)),
        ],
        compiler_params=params(0), name="gather",
        cost_estimate=pl.CostEstimate(flops=0, bytes_accessed=150_000_000, transcendentals=0),
    )(x, codes, bias, mine)


def error_kernel(sel, wt_hbm, lat, base, err, out, local, send, recv, rsend, rrecv, wt, wt_sem, parts, *slots):
    me = coords()
    loads = [pltpu.make_async_copy(wt_hbm.at[i], wt.at[i], wt_sem.at[i]) for i in range(8)]
    for c in loads:
        c.start()
    barrier(me)
    for c in loads:
        c.wait()

    def make(k, at):
        fill(k, at, sel, wt, lat, parts)

    last, reductions = reduce_error(me, make, parts, base, err, slots, rsend, rrecv)
    gather(me, err, out, local, send, recv, ready=last)
    for r in reductions:
        r.drain()


def error_call(sel, wt, lat, base):
    return pl.pallas_call(
        error_kernel,
        out_shape=(jax.ShapeDtypeStruct((ROWS, TOK), jnp.bfloat16), jax.ShapeDtypeStruct(PIECES, jnp.bfloat16)),
        in_specs=[pl.BlockSpec(memory_space=pltpu.SMEM), ANY, VMEM, VMEM], out_specs=(VMEM, ANY),
        scratch_shapes=[
            DMA, DMA((3, COPIES)), DMA((3, COPIES)), DMA((3, 36)), DMA((3, 36)),
            pltpu.VMEM((8, D, SPAN), jnp.bfloat16), DMA((8,)), pltpu.VMEM(PIECES, jnp.bfloat16), *reduce_scratch(),
        ],
        compiler_params=params(1), name="error",
    )(sel, wt, lat, base)


CHUNK = 896


def pick(mine, theirs, ws):
    ws[:SPAN, :] = mine[0]
    ws[SPAN:, :] = theirs[0]


def encode_kernel(table, cen, mine, theirs, bias, lat, mask, ws):
    g = pl.program_id(0)
    pick(mine, theirs, ws)
    pre = jnp.dot(ws[...], cen[0], preferred_element_type=jnp.float32)
    lane = lax.broadcasted_iota(jnp.int32, (SPAN, TOK), 1)
    for hh in range(2):
        rows = slice(hh * SPAN, (hh + 1) * SPAN)
        chosen = lax.broadcasted_iota(jnp.int32, (8, TOK), 0) == table[g, hh]
        p = pre[rows] + lax.dot_general(
            bias[hh].astype(jnp.bfloat16), jnp.where(chosen, 1.0, 0.0).astype(jnp.bfloat16),
            (((0,), (0,)), ((), ())), preferred_element_type=jnp.float32)
        on = jnp.where(lane < SPAN, table[g, 2 + hh], table[g, 4 + hh])
        keep = (on > 0) & (p > 0)
        lat[0, rows] = jnp.where(keep, p, 0.0).astype(jnp.bfloat16)
        mask[0, rows] = jnp.where(keep, 1.0, 0.0).astype(jnp.bfloat16)


def encode_call(table, cen, mine, theirs, bias):
    per = lambda *shape: pl.BlockSpec((1, *shape), lambda g, *_: (g, 0, 0))
    block = lambda hh: pl.BlockSpec((1, SPAN, D), lambda g, t: (t[g, hh], 0, 0))
    return pl.pallas_call(
        encode_kernel,
        out_shape=(
            jax.ShapeDtypeStruct((8, 2 * SPAN, TOK), jnp.bfloat16),
            jax.ShapeDtypeStruct((8, 2 * SPAN, TOK), jnp.bfloat16),
        ),
        grid_spec=pltpu.PrefetchScalarGridSpec(
            num_scalar_prefetch=1, grid=(8,),
            in_specs=[per(D, TOK), block(0), block(1), VMEM],
            out_specs=(per(2 * SPAN, TOK), per(2 * SPAN, TOK)),
            scratch_shapes=[pltpu.VMEM((2 * SPAN, D), jnp.bfloat16)],
        ),
        compiler_params=params(), name="encode",
    )(table, cen, mine, theirs, bias)


def grad_kernel(sel, err, cen, lat, mask, mine, theirs, own, other, own_b, other_b, ws, mine_acc, acc):
    g = pl.program_id(0)

    @pl.when(g == 0)
    def _():
        mine_acc[...] = jnp.zeros_like(mine_acc)
        acc[...] = jnp.zeros_like(acc)
        own_b[...] = jnp.zeros_like(own_b)
        other_b[...] = jnp.zeros_like(other_b)

    pick(mine, theirs, ws)
    back = jnp.dot(ws[...], err[0], preferred_element_type=jnp.float32)
    slope = jnp.where(mask[0] > 0, back, 0.0).astype(jnp.bfloat16)
    sums = lax.dot_general(jnp.ones((8, TOK), jnp.bfloat16), slope, (((1,), (1,)), ((), ())), preferred_element_type=jnp.float32)
    sums = sums.astype(jnp.bfloat16).astype(jnp.float32)
    row = lax.broadcasted_iota(jnp.int32, (8, SPAN), 0)
    for hh, into in enumerate((own_b, other_b)):
        into[...] += jnp.where(row == sel[g, hh], sums[:, hh * SPAN : (hh + 1) * SPAN], 0.0)
    for i in range(0, D, CHUNK):
        nt = (((1,), (1,)), ((), ()))
        t = lax.dot_general(lat[0], err[0, i : i + CHUNK], nt, preferred_element_type=jnp.float32)
        t = t + lax.dot_general(slope, cen[0, i : i + CHUNK], nt, preferred_element_type=jnp.float32)
        t = t.astype(jnp.bfloat16).astype(jnp.float32)
        mine_acc[sel[g, 0], :, i : i + CHUNK] += t[:SPAN]
        acc[sel[g, 1], :, i : i + CHUNK] += t[SPAN:]

    @pl.when(g == 7)
    def _():
        for b in range(4):
            own[b] = mine_acc[b].astype(jnp.bfloat16)
            other[b] = acc[b].astype(jnp.bfloat16)


def grad_call(sel, err, cen, lat, mask, mine, theirs):
    per = lambda *shape: pl.BlockSpec((1, *shape), lambda g, *_: (g, 0, 0))
    block = lambda hh: pl.BlockSpec((1, SPAN, D), lambda g, t: (t[g, hh], 0, 0))
    return pl.pallas_call(
        grad_kernel,
        out_shape=(
            jax.ShapeDtypeStruct((4, SPAN, D), jnp.bfloat16),
            jax.ShapeDtypeStruct((4, SPAN, D), jnp.bfloat16),
            jax.ShapeDtypeStruct((8, SPAN), jnp.float32),
            jax.ShapeDtypeStruct((8, SPAN), jnp.float32),
        ),
        grid_spec=pltpu.PrefetchScalarGridSpec(
            num_scalar_prefetch=1, grid=(8,),
            in_specs=[per(D, TOK), per(D, TOK), per(2 * SPAN, TOK), per(2 * SPAN, TOK), block(0), block(1)],
            out_specs=(VMEM, VMEM, VMEM, VMEM),
            scratch_shapes=[pltpu.VMEM((2 * SPAN, D), jnp.bfloat16)] + [pltpu.VMEM((4, SPAN, D), jnp.float32)] * 2,
        ),
        compiler_params=params(), name="grad",
    )(sel, err, cen, lat, mask, mine, theirs)


NAMES = ("x", "zh", "zl", "y", "c")
SWAP = [(0, 1), (1, 0)]


def step(activations, dictionary, enc_bias, dec_bias, block_codes):
    d = lax.axis_index("x") * 2 + lax.axis_index("zh")
    c = lax.axis_index("c")
    chip = lax.axis_index("zl") * 4 + lax.axis_index("y")
    mine = dictionary.reshape(4, SPAN, D)
    act_t = activations.T.astype(jnp.float32)
    dec = lax.dynamic_slice_in_dim(dec_bias, d * ROWS, ROWS)[:, None]
    bias = jnp.pad(enc_bias.astype(jnp.float32).reshape(4, SPAN), ((0, 4), (0, 0)))
    cen, codes, biases, theirs, wt = gather_call((act_t - dec).astype(jnp.bfloat16), block_codes, bias, mine)
    cen = cen.reshape(8, D, TOK)
    codes = lax.dynamic_index_in_dim(codes.reshape(8, 2, 8, 16), d, axis=2, keepdims=False)
    first = d * 64 + (chip * 2 + jnp.stack([c, 1 - c])) * 4
    local = codes[:, :, None, :] - first[:, None]
    hit = (codes[:, :, None, :] >= 0) & (local >= 0) & (local < 4)
    local = jnp.max(jnp.where(hit, local, -1), axis=3)
    table = jnp.concatenate([jnp.maximum(jnp.max(local, axis=1), 0), (local >= 0).astype(jnp.int32).reshape(8, 4)], axis=1)
    lat, mask = encode_call(table, cen, mine, theirs, biases)
    err_own, err = error_call(table, wt, lat, dec - act_t)
    own, other, own_b, other_b = grad_call(table, err.reshape(8, D, TOK), cen, lat, mask, mine, theirs)
    grad_w = own.astype(jnp.float32) + lax.ppermute(other, "c", SWAP).astype(jnp.float32)
    grad_b = (own_b + lax.ppermute(other_b, "c", SWAP))[:4]
    return err_own.T, grad_w.reshape(4 * SPAN, D), grad_b.reshape(4 * SPAN)


def solution(mesh):
    split = Mesh(mesh.devices.reshape(4, 2, 2, 4, 2), NAMES)
    dict_, dp = ("x", "zh"), ("zl", "y", "c")
    rows = P((*dict_, *dp))
    return jax.shard_map(
        step, mesh=split,
        in_specs=(P(dp, dict_), P((*dict_, *dp), None), rows, P(), P(dp, None, None)),
        out_specs=(P(dp, dict_), P((*dict_, *dp), None), rows),
        check_vma=False,
    )
```

```python
import functools
import jax, jax.numpy as jnp
from jax import lax
from jax.experimental import pallas as pl
from jax.experimental.pallas import tpu as pltpu
from jax.sharding import Mesh, PartitionSpec as P

ROWS, TOK = 448, 256
D, SPAN = 3584, 128
C0 = (0, 144, 288)
CN = (144, 144, 160)
CH = (80, 64, 80)
ORDER = (("x", "y", "z"), ("y", "z", "x"), ("z", "x", "y"))


def coords():
    x, y = lax.axis_index("x"), lax.axis_index("y")
    z = lax.axis_index("zh") * 2 + lax.axis_index("zl")
    return {"x": x, "y": y, "z": z}


def shift(me, dim, by):
    return lax.rem(me[dim] + (by + 4), 4)


def device(dim, value):
    if dim == "z":
        return {"zh": value // 2, "zl": lax.rem(value, 2)}
    return {dim: value}


def region(ref, at, lo, n):
    z = at["z"]
    zl = slice(None) if z is None else lax.rem(z, 2)
    zh = slice(None) if z is None else z // 2
    y = slice(None) if at["y"] is None else at["y"]
    x = slice(None) if at["x"] is None else at["x"]
    return ref.at[zl, y, x, zh, pl.ds(lo, n), :]


def remote(src, dst, send, recv, dim, value):
    return pltpu.make_async_remote_copy(
        src_ref=src, dst_ref=dst, send_sem=send, recv_sem=recv,
        device_id=device(dim, value), device_id_type=pl.DeviceIdType.MESH)


def barrier(me, cores=False):
    sem = pltpu.get_barrier_semaphore()
    for dim in ("x", "y", "z"):
        for by in (-1, 1):
            pl.semaphore_signal(sem, inc=1, device_id=device(dim, shift(me, dim, by)),
                                device_id_type=pl.DeviceIdType.MESH)
    if cores:
        pl.semaphore_signal(sem, inc=1, device_id={"c": 1 - lax.axis_index("c")}, device_id_type=pl.DeviceIdType.MESH)
    pl.semaphore_wait(sem, 7 if cores else 6)


NEAR = ((0, 1), (1, -1))


def gather(me, own, out, local, send, recv, beside=iter(()), ready=lambda k: None, use=None):
    mine = pltpu.make_async_copy(own, region(out, me, 0, ROWS), local)
    copies = [{} for _ in range(3)]

    def arrived(k, by_b, by_c=0):
        if use is not None:
            a, b, c = ORDER[k]
            use.arrived(k, {a: None, b: shift(me, b, by_b), c: shift(me, c, by_c)})

    def work():
        if use is not None:
            use.work()

    def go(k, phase, name, at, by, lo=0, n=None, src=None):
        order = ORDER[k]
        where = {d: (None if i < phase - 1 else shift(me, d, at.get(i, 0))) for i, d in enumerate(order)}
        part = region(out, where, C0[k] + lo, CN[k] if n is None else n)
        dim = order[phase]
        i = len(copies[k])
        c = remote(part if src is None else src, part, send.at[k, i], recv.at[k, i], dim, shift(me, dim, by))
        c.start()
        copies[k][(phase, *name)] = c

    def got(k, *name):
        copies[k][name].wait_recv()

    for k in range(3):
        ready(k)
        src = own.at[pl.ds(C0[k], CN[k]), :]
        for s, by in NEAR:
            go(k, 0, ("near", s), {}, by, src=src)
        for s, by in NEAR:
            go(k, 1, ("near", 0, s), {}, by, src=src)
    mine.start()
    next(beside, None)
    for k in range(3):
        for s, by in NEAR:
            got(k, 0, "near", s)
            lo, n = (0, CH[k]) if s == 0 else (CH[k], CN[k] - CH[k])
            go(k, 0, ("far", s), {0: -by}, by, lo, n)
        for j in (-1, 1):
            for s, by in NEAR:
                go(k, 1, ("near", j, s), {0: j}, by)
    mine.wait()
    next(beside, None)
    for k in range(3):
        got(k, 0, "far", 0)
        got(k, 0, "far", 1)
        for s, by in NEAR:
            go(k, 1, ("near", 2, s), {0: 2}, by)
        for s, by in NEAR:
            go(k, 2, ("near", 0, s), {1: 0}, by)
        arrived(k, 0)
    for phase in (1, 2):
        next(beside, None)
        for j in (0, -1, 1, 2):
            for k in range(3):
                for s, by in NEAR:
                    got(k, phase, "near", j, s)
                    if (j in (0, 1)) == (s == 0):
                        go(k, phase, ("far", j), {phase - 1: j, phase: -by}, by)
                    if phase == 2:
                        arrived(k, j, -by)
            if phase == 2:
                work()
        if phase == 1:
            for k in range(3):
                for j in (-1, 1):
                    for s, by in NEAR:
                        go(k, 2, ("near", j, s), {1: j}, by)
                    arrived(k, j)
        next(beside, None)
        for j in (0, -1, 1, 2):
            for k in range(3):
                got(k, phase, "far", j)
                if phase == 2:
                    arrived(k, j, 2)
            if phase == 2:
                work()
        if phase == 1:
            for k in range(3):
                for s, by in NEAR:
                    go(k, 2, ("near", 2, s), {1: 2}, by)
                arrived(k, 2)
            work()
    work()
    work()
    for k in range(3):
        for c in copies[k].values():
            c.wait_send()


def gather_codes(me, own, out, send, recv):
    zl = lax.rem(me["z"], 2)
    out[zl, me["y"]] = own[...]
    copies = []

    def go(src, dst, device_id):
        i = len(copies)
        c = pltpu.make_async_remote_copy(src_ref=src, dst_ref=dst, send_sem=send.at[i], recv_sem=recv.at[i],
                                         device_id=device_id, device_id_type=pl.DeviceIdType.MESH)
        c.start()
        copies.append(c)

    for by in (1, -1):
        go(own, out.at[zl, me["y"]], device("y", shift(me, "y", by)))
    yield
    copies[0].wait_recv()
    back = out.at[zl, shift(me, "y", -1)]
    go(back, back, device("y", shift(me, "y", 1)))
    yield
    copies[1].wait_recv()
    copies[2].wait_recv()
    go(out.at[zl], out.at[zl], {"zl": 1 - zl})
    yield
    copies[3].wait_recv()
    for c in copies:
        c.wait_send()


def lead(dims):
    return tuple(s for name, s in (("zl", 2), ("y", 4), ("x", 4), ("zh", 2)) if name[0] in dims)


def each(shape, body):
    total = 1
    for s in shape:
        total *= s
    if total == 1:
        body(())
        return

    def step(i, carry):
        index = []
        for s in reversed(shape):
            index.append(lax.rem(i, s))
            i = i // s
        body(tuple(reversed(index)))
        return carry

    lax.fori_loop(0, total, step, 0)


SUBS = (2, -1, 1, 0)


def reduce_scratch():
    shapes = []
    for k in range(3):
        n, h = CN[k], CH[k]
        for q in (0, 0, 0, 0, 1, 2):
            dims = lead(ORDER[k][:1] if q < 2 else ())
            for rows in (h, n - h, h, n - h, h, n - h):
                shapes.append(pltpu.VMEM((*dims, rows, TOK), jnp.bfloat16))
    return shapes


class Reduction:
    def __init__(self, me, k, dim, at, parts, slots, send, recv, base):
        self.me, self.k, self.dim, self.at, self.parts, self.slots = me, k, dim, at, parts, slots
        self.send, self.recv, self.base = send, recv, base
        self.copies = {}
        self.lead = lead(tuple(d for d in at if d != dim and at[d] is None))
        self.halves = ((0, CH[k]), (CH[k], CN[k] - CH[k]))

    def source(self, by, half):
        lo, n = self.halves[half]
        return region(self.parts, {**self.at, self.dim: shift(self.me, self.dim, by)}, C0[self.k] + lo, n)

    def go(self, i, src, by):
        c = remote(src, self.slots[i], self.send.at[self.k, self.base + i], self.recv.at[self.k, self.base + i],
                   self.dim, shift(self.me, self.dim, by))
        c.start()
        self.copies[i] = c

    def far(self):
        self.go(0, self.source(2, 0), 1)
        self.go(1, self.source(2, 1), -1)

    def near(self):
        self.go(3, self.source(1, 1), 1)
        self.go(4, self.source(-1, 0), -1)

    def forward(self):
        for i, by in ((0, 1), (1, -1)):
            self.copies[i].wait_recv()
            slot, own = self.slots[i], self.source(by, i)

            def add(index, slot=slot, own=own):
                a = slot[index].astype(jnp.float32) + own[index].astype(jnp.float32)
                slot[index] = a.astype(jnp.bfloat16)

            each(self.lead, add)
            self.go(2 if i == 0 else 5, slot, by)

    def finish(self, store=None):
        for i in (3, 4, 2, 5):
            self.copies[i].wait_recv()
        for half, (i, j) in enumerate(((2, 4), (3, 5))):
            a, b, own = self.slots[i], self.slots[j], self.source(0, half)

            def add(index, a=a, b=b, own=own, half=half):
                total = own[index].astype(jnp.float32) + a[index].astype(jnp.float32) + b[index].astype(jnp.float32)
                if store is None:
                    own[index] = total.astype(jnp.bfloat16)
                else:
                    store(self.halves[half], total)

            each(self.lead, add)

    def drain(self):
        for c in self.copies.values():
            c.wait_send()


def pieces(at, body):
    def group(index):
        index = list(index)
        zl = index.pop(0) if at["z"] is None else lax.rem(at["z"], 2)
        y = index.pop(0) if at["y"] is None else at["y"]
        body(zl * 4 + y, [
            (zl, y, x, zh)
            for zh in ((0, 1) if at["z"] is None else (at["z"] // 2,))
            for x in (range(4) if at["x"] is None else (at["x"],))
        ])

    each((2,) * (at["z"] is None) + (4,) * (at["y"] is None), group)


def turned_rows(wt, sel, g, piece, lo, n):
    rows = pl.ds(pl.multiple_of((piece[2] * 2 + piece[3]) * ROWS + lo, 16), n)
    return jnp.concatenate([wt[sel[g, 0], rows, :], wt[4 + sel[g, 1], rows, :]], axis=1)


class Back:
    def __init__(self, sel, wt, out, held_e, back, sems):
        self.sel, self.wt, self.out, self.held, self.back, self.sems = sel, wt, out, held_e, back, sems
        self.count, self.old, self.new = 0, [], []

    def arrived(self, k, at):
        src, dst = (region(r, at, C0[k], CN[k]) for r in (self.out, self.held))
        copy = pltpu.make_async_copy(src, dst, self.sems.at[self.count])
        self.count += 1
        copy.start()
        self.new.append((k, at, copy))

    def work(self):
        todo, self.old, self.new = self.old, self.new, []
        for k, at, copy in todo:
            copy.wait()
            rows = pl.ds(C0[k], CN[k])

            def add(g, group, k=k, rows=rows):
                w = jnp.concatenate([turned_rows(self.wt, self.sel, g, piece, C0[k], CN[k]) for piece in group], axis=0)
                e = jnp.concatenate([self.held[(*piece, rows, slice(None))] for piece in group], axis=0)
                self.back[g] += lax.dot_general(w, e, (((0,), (0,)), ((), ())), preferred_element_type=jnp.float32)

            pieces(at, add)


def fill(k, at, sel, wt, lat, parts):
    lo, n = C0[k], CN[k]

    def group(g, found):
        for piece in found:
            part = jnp.dot(turned_rows(wt, sel, g, piece, lo, n), lat[g], preferred_element_type=jnp.float32)
            parts[(*piece, pl.ds(lo, n), slice(None))] = part.astype(jnp.bfloat16)

    pieces(at, group)


def reduce_error(me, make, parts, base, err, slots, send, recv):
    first, second, third = [], [], []
    for k in range(3):
        a, b, c = ORDER[k]
        mine = slots[36 * k : 36 * (k + 1)]
        at = {a: None, b: me[b], c: me[c]}

        def new(dim, at, i, k=k, mine=mine):
            return Reduction(me, k, dim, at, parts, mine[6 * i : 6 * i + 6], send, recv, 6 * i)

        first.append({m: new(c, {**at, b: shift(me, b, m)}, i) for i, m in enumerate(SUBS)})
        second.append(new(b, at, 4))
        third.append(new(a, {**at, a: me[a]}, 5))

    def whole(k, by):
        a, b, c = ORDER[k]
        make(k, {a: None, b: None, c: shift(me, c, by)})

    def push(m):
        for k in range(3):
            first[k][m].near()
            first[k][m].forward()

    for m in SUBS:
        for k in range(3):
            a, b, c = ORDER[k]
            make(k, {a: None, b: shift(me, b, m), c: shift(me, c, 2)})
            first[k][m].far()
    for k in range(3):
        whole(k, 1)
        whole(k, -1)
    push(2)
    push(-1)
    for k in range(3):
        whole(k, 0)
    for k in range(3):
        first[k][2].finish()
        second[k].far()
    push(1)
    for k in range(3):
        first[k][-1].finish()
    push(0)
    for k in range(3):
        first[k][1].finish()
        second[k].near()
    for k in range(3):
        second[k].forward()
    for k in range(3):
        first[k][0].finish()
    for k in range(3):
        second[k].finish()
        third[k].far()
        third[k].near()
    for k in range(3):
        third[k].forward()

    def last(k):
        def store(half, total):
            rows = pl.ds(C0[k] + half[0], half[1])
            err[rows, :] = (total + base[rows, :]).astype(jnp.bfloat16)

        third[k].finish(store)

    return last, [r for k in range(3) for r in (*first[k].values(), second[k], third[k])]


def params(collective=None):
    return pltpu.CompilerParams(collective_id=collective, has_side_effects=collective is not None,
                                vmem_limit_bytes=60 * 1024 * 1024)


PIECES = (2, 4, 4, 2, ROWS, TOK)
VMEM = pl.BlockSpec(memory_space=pltpu.VMEM)
ANY = pl.BlockSpec(memory_space=pl.ANY)


def turn(mine, bias, theirs, biases, wt, held_w, turned, sems, send, recv):
    def give(i, src, dst):
        c = pltpu.make_async_remote_copy(
            src_ref=src, dst_ref=dst, send_sem=send.at[i], recv_sem=recv.at[i],
            device_id={"c": 1 - lax.axis_index("c")}, device_id_type=pl.DeviceIdType.MESH)
        c.start()
        return c

    load = pltpu.make_async_copy(mine, held_w, sems.at[0])
    load.start()
    given = [give(0, mine, theirs), give(1, bias, biases.at[1])]
    biases[0] = bias[...]
    yield
    yield
    yield
    load.wait()
    yield

    def block(i, carry):
        b, j = i // (D // SPAN), pl.multiple_of(lax.rem(i, D // SPAN) * SPAN, SPAN)
        turned[b, pl.ds(j, SPAN), :] = held_w[b, :, pl.ds(j, SPAN)].T
        return carry

    lax.fori_loop(0, 4 * (D // SPAN), block, 0)
    yield
    keep = pltpu.make_async_copy(turned, wt.at[pl.ds(0, 4)], sems.at[1])
    keep.start()
    given.append(give(2, turned, wt.at[pl.ds(4, 4)]))
    yield
    keep.wait()
    for c in given:
        c.wait()


def both(*steps):
    while True:
        done = [next(s, "end") for s in steps]
        if all(d == "end" for d in done):
            return
        yield


def gather_kernel(own, codes, bias, mine, out, all_codes, biases, theirs, wt, local, send, recv, csend, crecv, held_w, turned, sems, wsend, wrecv):
    me = coords()
    barrier(me, True)
    steps = both(gather_codes(me, codes, all_codes, csend, crecv), turn(mine, bias, theirs, biases, wt, held_w, turned, sems, wsend, wrecv))
    gather(me, own, out, local, send, recv, steps)
    for _ in steps:
        pass


DMA = pltpu.SemaphoreType.DMA
COPIES = 28


def gather_call(x, codes, bias, mine):
    return pl.pallas_call(
        gather_kernel,
        out_shape=(
            jax.ShapeDtypeStruct(PIECES, jnp.bfloat16),
            jax.ShapeDtypeStruct((2, 4, 2, 8, 16), jnp.int32),
            jax.ShapeDtypeStruct((2, 8, SPAN), jnp.float32),
            jax.ShapeDtypeStruct((4, SPAN, D), jnp.bfloat16),
            jax.ShapeDtypeStruct((8, D, SPAN), jnp.bfloat16),
        ),
        in_specs=[VMEM, VMEM, VMEM, ANY], out_specs=(ANY, VMEM, VMEM, ANY, ANY),
        scratch_shapes=[
            DMA, DMA((3, COPIES)), DMA((3, COPIES)), DMA((4,)), DMA((4,)),
            pltpu.VMEM((4, SPAN, D), jnp.bfloat16), pltpu.VMEM((4, D, SPAN), jnp.bfloat16), DMA((2,)), DMA((3,)), DMA((3,)),
        ],
        compiler_params=params(0), name="gather",
        cost_estimate=pl.CostEstimate(flops=0, bytes_accessed=150_000_000, transcendentals=0),
    )(x, codes, bias, mine)


def error_kernel(sel, wt_hbm, lat, mask, base, err, out, slope, local, send, recv, rsend, rrecv, wt, wt_sem, parts, held_e, back, sems, *slots):
    me = coords()
    loads = [pltpu.make_async_copy(wt_hbm.at[i], wt.at[i], wt_sem.at[i]) for i in range(8)]
    for c in loads:
        c.start()
    barrier(me)
    for c in loads:
        c.wait()

    def make(k, at):
        fill(k, at, sel, wt, lat, parts)

    last, reductions = reduce_error(me, make, parts, base, err, slots, rsend, rrecv)
    back[...] = jnp.zeros_like(back)
    gather(me, err, out, local, send, recv, ready=last, use=Back(sel, wt, out, held_e, back, sems))

    def round_off(g, carry):
        slope[g] = jnp.where(mask[g] > 0, back[g], 0.0).astype(jnp.bfloat16)
        return carry

    lax.fori_loop(0, 8, round_off, 0)
    for r in reductions:
        r.drain()


def error_call(sel, wt, lat, mask, base):
    return pl.pallas_call(
        error_kernel,
        out_shape=(
            jax.ShapeDtypeStruct((ROWS, TOK), jnp.bfloat16),
            jax.ShapeDtypeStruct(PIECES, jnp.bfloat16),
            jax.ShapeDtypeStruct((8, 2 * SPAN, TOK), jnp.bfloat16),
        ),
        in_specs=[pl.BlockSpec(memory_space=pltpu.SMEM), ANY, VMEM, VMEM, VMEM], out_specs=(VMEM, ANY, VMEM),
        scratch_shapes=[
            DMA, DMA((3, COPIES)), DMA((3, COPIES)), DMA((3, 36)), DMA((3, 36)),
            pltpu.VMEM((8, D, SPAN), jnp.bfloat16), DMA((8,)), pltpu.VMEM(PIECES, jnp.bfloat16), pltpu.VMEM(PIECES, jnp.bfloat16),
            pltpu.VMEM((8, 2 * SPAN, TOK), jnp.float32), DMA((48,)), *reduce_scratch(),
        ],
        compiler_params=params(1), name="error",
    )(sel, wt, lat, mask, base)


CHUNK = 896


def pick(mine, theirs, ws):
    ws[:SPAN, :] = mine[0]
    ws[SPAN:, :] = theirs[0]


def encode_kernel(table, cen, mine, theirs, bias, lat, mask, ws):
    g = pl.program_id(0)
    pick(mine, theirs, ws)
    pre = jnp.dot(ws[...], cen[0], preferred_element_type=jnp.float32)
    lane = lax.broadcasted_iota(jnp.int32, (SPAN, TOK), 1)
    for hh in range(2):
        rows = slice(hh * SPAN, (hh + 1) * SPAN)
        chosen = lax.broadcasted_iota(jnp.int32, (8, TOK), 0) == table[g, hh]
        p = pre[rows] + lax.dot_general(
            bias[hh].astype(jnp.bfloat16), jnp.where(chosen, 1.0, 0.0).astype(jnp.bfloat16),
            (((0,), (0,)), ((), ())), preferred_element_type=jnp.float32)
        on = jnp.where(lane < SPAN, table[g, 2 + hh], table[g, 4 + hh])
        keep = (on > 0) & (p > 0)
        lat[0, rows] = jnp.where(keep, p, 0.0).astype(jnp.bfloat16)
        mask[0, rows] = jnp.where(keep, 1.0, 0.0).astype(jnp.bfloat16)


def encode_call(table, cen, mine, theirs, bias):
    per = lambda *shape: pl.BlockSpec((1, *shape), lambda g, *_: (g, 0, 0))
    block = lambda hh: pl.BlockSpec((1, SPAN, D), lambda g, t: (t[g, hh], 0, 0))
    return pl.pallas_call(
        encode_kernel,
        out_shape=(
            jax.ShapeDtypeStruct((8, 2 * SPAN, TOK), jnp.bfloat16),
            jax.ShapeDtypeStruct((8, 2 * SPAN, TOK), jnp.bfloat16),
        ),
        grid_spec=pltpu.PrefetchScalarGridSpec(
            num_scalar_prefetch=1, grid=(8,),
            in_specs=[per(D, TOK), block(0), block(1), VMEM],
            out_specs=(per(2 * SPAN, TOK), per(2 * SPAN, TOK)),
            scratch_shapes=[pltpu.VMEM((2 * SPAN, D), jnp.bfloat16)],
        ),
        compiler_params=params(), name="encode",
    )(table, cen, mine, theirs, bias)


def grad_kernel(sel, err, cen, lat, slopes, own, other, own_b, other_b, mine_acc, acc):
    g = pl.program_id(0)

    @pl.when(g == 0)
    def _():
        mine_acc[...] = jnp.zeros_like(mine_acc)
        acc[...] = jnp.zeros_like(acc)
        own_b[...] = jnp.zeros_like(own_b)
        other_b[...] = jnp.zeros_like(other_b)

    slope = slopes[0]
    sums = lax.dot_general(jnp.ones((8, TOK), jnp.bfloat16), slope, (((1,), (1,)), ((), ())), preferred_element_type=jnp.float32)
    sums = sums.astype(jnp.bfloat16).astype(jnp.float32)
    row = lax.broadcasted_iota(jnp.int32, (8, SPAN), 0)
    for hh, into in enumerate((own_b, other_b)):
        into[...] += jnp.where(row == sel[g, hh], sums[:, hh * SPAN : (hh + 1) * SPAN], 0.0)
    for i in range(0, D, CHUNK):
        nt = (((1,), (1,)), ((), ()))
        t = lax.dot_general(lat[0], err[0, i : i + CHUNK], nt, preferred_element_type=jnp.float32)
        t = t + lax.dot_general(slope, cen[0, i : i + CHUNK], nt, preferred_element_type=jnp.float32)
        t = t.astype(jnp.bfloat16).astype(jnp.float32)
        mine_acc[sel[g, 0], :, i : i + CHUNK] += t[:SPAN]
        acc[sel[g, 1], :, i : i + CHUNK] += t[SPAN:]

    @pl.when(g == 7)
    def _():
        for b in range(4):
            own[b] = mine_acc[b].astype(jnp.bfloat16)
            other[b] = acc[b].astype(jnp.bfloat16)


def grad_call(sel, err, cen, lat, slope):
    per = lambda *shape: pl.BlockSpec((1, *shape), lambda g, *_: (g, 0, 0))
    return pl.pallas_call(
        grad_kernel,
        out_shape=(
            jax.ShapeDtypeStruct((4, SPAN, D), jnp.bfloat16),
            jax.ShapeDtypeStruct((4, SPAN, D), jnp.bfloat16),
            jax.ShapeDtypeStruct((8, SPAN), jnp.float32),
            jax.ShapeDtypeStruct((8, SPAN), jnp.float32),
        ),
        grid_spec=pltpu.PrefetchScalarGridSpec(
            num_scalar_prefetch=1, grid=(8,),
            in_specs=[per(D, TOK), per(D, TOK), per(2 * SPAN, TOK), per(2 * SPAN, TOK)],
            out_specs=(VMEM, VMEM, VMEM, VMEM),
            scratch_shapes=[pltpu.VMEM((4, SPAN, D), jnp.float32)] * 2,
        ),
        compiler_params=params(), name="grad",
    )(sel, err, cen, lat, slope)


NAMES = ("x", "zh", "zl", "y", "c")
SWAP = [(0, 1), (1, 0)]


def step(activations, dictionary, enc_bias, dec_bias, block_codes):
    d = lax.axis_index("x") * 2 + lax.axis_index("zh")
    c = lax.axis_index("c")
    chip = lax.axis_index("zl") * 4 + lax.axis_index("y")
    mine = dictionary.reshape(4, SPAN, D)
    act_t = activations.T.astype(jnp.float32)
    dec = lax.dynamic_slice_in_dim(dec_bias, d * ROWS, ROWS)[:, None]
    bias = jnp.pad(enc_bias.astype(jnp.float32).reshape(4, SPAN), ((0, 4), (0, 0)))
    cen, codes, biases, theirs, wt = gather_call((act_t - dec).astype(jnp.bfloat16), block_codes, bias, mine)
    cen = cen.reshape(8, D, TOK)
    codes = lax.dynamic_index_in_dim(codes.reshape(8, 2, 8, 16), d, axis=2, keepdims=False)
    first = d * 64 + (chip * 2 + jnp.stack([c, 1 - c])) * 4
    local = codes[:, :, None, :] - first[:, None]
    hit = (codes[:, :, None, :] >= 0) & (local >= 0) & (local < 4)
    local = jnp.max(jnp.where(hit, local, -1), axis=3)
    table = jnp.concatenate([jnp.maximum(jnp.max(local, axis=1), 0), (local >= 0).astype(jnp.int32).reshape(8, 4)], axis=1)
    lat, mask = encode_call(table, cen, mine, theirs, biases)
    err_own, err, slope = error_call(table, wt, lat, mask, dec - act_t)
    own, other, own_b, other_b = grad_call(table, err.reshape(8, D, TOK), cen, lat, slope)
    grad_w = own.astype(jnp.float32) + lax.ppermute(other, "c", SWAP).astype(jnp.float32)
    grad_b = (own_b + lax.ppermute(other_b, "c", SWAP))[:4]
    return err_own.T, grad_w.reshape(4 * SPAN, D), grad_b.reshape(4 * SPAN)


def solution(mesh):
    split = Mesh(mesh.devices.reshape(4, 2, 2, 4, 2), NAMES)
    dict_, dp = ("x", "zh"), ("zl", "y", "c")
    rows = P((*dict_, *dp))
    return jax.shard_map(
        step, mesh=split,
        in_specs=(P(dp, dict_), P((*dict_, *dp), None), rows, P(), P(dp, None, None)),
        out_specs=(P(dp, dict_), P((*dict_, *dp), None), rows),
        check_vma=False,
    )
```

```python
import functools
import jax, jax.numpy as jnp
from jax import lax
from jax.experimental import pallas as pl
from jax.experimental.pallas import tpu as pltpu
from jax.sharding import Mesh, PartitionSpec as P

ROWS, TOK = 448, 256
D, SPAN = 3584, 128
C0 = (0, 144, 288)
CN = (144, 144, 160)
CH = (80, 64, 80)
ORDER = (("x", "y", "z"), ("y", "z", "x"), ("z", "x", "y"))


def coords():
    x, y = lax.axis_index("x"), lax.axis_index("y")
    z = lax.axis_index("zh") * 2 + lax.axis_index("zl")
    return {"x": x, "y": y, "z": z}


def shift(me, dim, by):
    return lax.rem(me[dim] + (by + 4), 4)


def device(dim, value):
    if dim == "z":
        return {"zh": value // 2, "zl": lax.rem(value, 2)}
    return {dim: value}


def region(ref, at, lo, n):
    z = at["z"]
    zl = slice(None) if z is None else lax.rem(z, 2)
    zh = slice(None) if z is None else z // 2
    y = slice(None) if at["y"] is None else at["y"]
    x = slice(None) if at["x"] is None else at["x"]
    return ref.at[zl, y, x, zh, pl.ds(lo, n), :]


def remote(src, dst, send, recv, dim, value):
    return pltpu.make_async_remote_copy(
        src_ref=src, dst_ref=dst, send_sem=send, recv_sem=recv,
        device_id=device(dim, value), device_id_type=pl.DeviceIdType.MESH)


def barrier(me, cores=False):
    sem = pltpu.get_barrier_semaphore()
    for dim in ("x", "y", "z"):
        for by in (-1, 1):
            pl.semaphore_signal(sem, inc=1, device_id=device(dim, shift(me, dim, by)),
                                device_id_type=pl.DeviceIdType.MESH)
    if cores:
        pl.semaphore_signal(sem, inc=1, device_id={"c": 1 - lax.axis_index("c")}, device_id_type=pl.DeviceIdType.MESH)
    pl.semaphore_wait(sem, 7 if cores else 6)


NEAR = ((0, 1), (1, -1))


def gather(me, own, out, local, send, recv, beside=iter(()), ready=lambda k: None, use=None):
    mine = pltpu.make_async_copy(own, region(out, me, 0, ROWS), local)
    copies = [{} for _ in range(3)]

    def arrived(k, by_b, by_c=0):
        if use is not None:
            a, b, c = ORDER[k]
            use.arrived(k, {a: None, b: shift(me, b, by_b), c: shift(me, c, by_c)})

    def work():
        if use is not None:
            use.work()

    def go(k, phase, name, at, by, lo=0, n=None, src=None):
        order = ORDER[k]
        where = {d: (None if i < phase - 1 else shift(me, d, at.get(i, 0))) for i, d in enumerate(order)}
        part = region(out, where, C0[k] + lo, CN[k] if n is None else n)
        dim = order[phase]
        i = len(copies[k])
        c = remote(part if src is None else src, part, send.at[k, i], recv.at[k, i], dim, shift(me, dim, by))
        c.start()
        copies[k][(phase, *name)] = c

    def got(k, *name):
        copies[k][name].wait_recv()

    for k in range(3):
        ready(k)
        src = own.at[pl.ds(C0[k], CN[k]), :]
        for s, by in NEAR:
            go(k, 0, ("near", s), {}, by, src=src)
        for s, by in NEAR:
            go(k, 1, ("near", 0, s), {}, by, src=src)
    mine.start()
    next(beside, None)
    for k in range(3):
        for s, by in NEAR:
            got(k, 0, "near", s)
            lo, n = (0, CH[k]) if s == 0 else (CH[k], CN[k] - CH[k])
            go(k, 0, ("far", s), {0: -by}, by, lo, n)
        for j in (-1, 1):
            for s, by in NEAR:
                go(k, 1, ("near", j, s), {0: j}, by)
    mine.wait()
    next(beside, None)
    for k in range(3):
        got(k, 0, "far", 0)
        got(k, 0, "far", 1)
        for s, by in NEAR:
            go(k, 1, ("near", 2, s), {0: 2}, by)
        for s, by in NEAR:
            go(k, 2, ("near", 0, s), {1: 0}, by)
        arrived(k, 0)
    for phase in (1, 2):
        next(beside, None)
        for j in (0, -1, 1, 2):
            for k in range(3):
                for s, by in NEAR:
                    got(k, phase, "near", j, s)
                    if (j in (0, 1)) == (s == 0):
                        go(k, phase, ("far", j), {phase - 1: j, phase: -by}, by)
                    if phase == 2:
                        arrived(k, j, -by)
            if phase == 2:
                work()
        if phase == 1:
            for k in range(3):
                for j in (-1, 1):
                    for s, by in NEAR:
                        go(k, 2, ("near", j, s), {1: j}, by)
                    arrived(k, j)
        next(beside, None)
        for j in (0, -1, 1, 2):
            for k in range(3):
                got(k, phase, "far", j)
                if phase == 2:
                    arrived(k, j, 2)
            if phase == 2:
                work()
        if phase == 1:
            for k in range(3):
                for s, by in NEAR:
                    go(k, 2, ("near", 2, s), {1: 2}, by)
                arrived(k, 2)
            work()
    work()
    work()
    for k in range(3):
        for c in copies[k].values():
            c.wait_send()


def gather_codes(me, own, out, send, recv):
    zl = lax.rem(me["z"], 2)
    out[zl, me["y"]] = own[...]
    copies = []

    def go(src, dst, device_id):
        i = len(copies)
        c = pltpu.make_async_remote_copy(src_ref=src, dst_ref=dst, send_sem=send.at[i], recv_sem=recv.at[i],
                                         device_id=device_id, device_id_type=pl.DeviceIdType.MESH)
        c.start()
        copies.append(c)

    for by in (1, -1):
        go(own, out.at[zl, me["y"]], device("y", shift(me, "y", by)))
    yield
    copies[0].wait_recv()
    back = out.at[zl, shift(me, "y", -1)]
    go(back, back, device("y", shift(me, "y", 1)))
    yield
    copies[1].wait_recv()
    copies[2].wait_recv()
    go(out.at[zl], out.at[zl], {"zl": 1 - zl})
    yield
    copies[3].wait_recv()
    for c in copies:
        c.wait_send()


def lead(dims):
    return tuple(s for name, s in (("zl", 2), ("y", 4), ("x", 4), ("zh", 2)) if name[0] in dims)


def each(shape, body):
    total = 1
    for s in shape:
        total *= s
    if total == 1:
        body(())
        return

    def step(i, carry):
        index = []
        for s in reversed(shape):
            index.append(lax.rem(i, s))
            i = i // s
        body(tuple(reversed(index)))
        return carry

    lax.fori_loop(0, total, step, 0)


SUBS = (2, -1, 1, 0)


def reduce_scratch():
    shapes = []
    for k in range(3):
        n, h = CN[k], CH[k]
        for q in (0, 0, 0, 0, 1, 2):
            dims = lead(ORDER[k][:1] if q < 2 else ())
            for rows in (h, n - h, h, n - h, h, n - h):
                shapes.append(pltpu.VMEM((*dims, rows, TOK), jnp.bfloat16))
    return shapes


class Reduction:
    def __init__(self, me, k, dim, at, parts, slots, send, recv, base):
        self.me, self.k, self.dim, self.at, self.parts, self.slots = me, k, dim, at, parts, slots
        self.send, self.recv, self.base = send, recv, base
        self.copies = {}
        self.lead = lead(tuple(d for d in at if d != dim and at[d] is None))
        self.halves = ((0, CH[k]), (CH[k], CN[k] - CH[k]))

    def source(self, by, half):
        lo, n = self.halves[half]
        return region(self.parts, {**self.at, self.dim: shift(self.me, self.dim, by)}, C0[self.k] + lo, n)

    def go(self, i, src, by):
        c = remote(src, self.slots[i], self.send.at[self.k, self.base + i], self.recv.at[self.k, self.base + i],
                   self.dim, shift(self.me, self.dim, by))
        c.start()
        self.copies[i] = c

    def far(self):
        self.go(0, self.source(2, 0), 1)
        self.go(1, self.source(2, 1), -1)

    def near(self):
        self.go(3, self.source(1, 1), 1)
        self.go(4, self.source(-1, 0), -1)

    def forward(self):
        for i, by in ((0, 1), (1, -1)):
            self.copies[i].wait_recv()
            slot, own = self.slots[i], self.source(by, i)

            def add(index, slot=slot, own=own):
                a = slot[index].astype(jnp.float32) + own[index].astype(jnp.float32)
                slot[index] = a.astype(jnp.bfloat16)

            each(self.lead, add)
            self.go(2 if i == 0 else 5, slot, by)

    def finish(self, store=None):
        for i in (3, 4, 2, 5):
            self.copies[i].wait_recv()
        for half, (i, j) in enumerate(((2, 4), (3, 5))):
            a, b, own = self.slots[i], self.slots[j], self.source(0, half)

            def add(index, a=a, b=b, own=own, half=half):
                total = own[index].astype(jnp.float32) + a[index].astype(jnp.float32) + b[index].astype(jnp.float32)
                if store is None:
                    own[index] = total.astype(jnp.bfloat16)
                else:
                    store(self.halves[half], total)

            each(self.lead, add)

    def drain(self):
        for c in self.copies.values():
            c.wait_send()


def pieces(at, body):
    def group(index):
        index = list(index)
        zl = index.pop(0) if at["z"] is None else lax.rem(at["z"], 2)
        y = index.pop(0) if at["y"] is None else at["y"]
        body(zl * 4 + y, [
            (zl, y, x, zh)
            for zh in ((0, 1) if at["z"] is None else (at["z"] // 2,))
            for x in (range(4) if at["x"] is None else (at["x"],))
        ])

    each((2,) * (at["z"] is None) + (4,) * (at["y"] is None), group)


def turned_rows(wt, sel, g, piece, lo, n):
    rows = pl.ds(pl.multiple_of((piece[2] * 2 + piece[3]) * ROWS + lo, 16), n)
    return jnp.concatenate([wt[sel[g, 0], rows, :], wt[4 + sel[g, 1], rows, :]], axis=1)


class Back:
    def __init__(self, sel, wt, out, held_e, back, sems):
        self.sel, self.wt, self.out, self.held, self.back, self.sems = sel, wt, out, held_e, back, sems
        self.count, self.old, self.new = 0, [], []

    def arrived(self, k, at):
        src, dst = (region(r, at, C0[k], CN[k]) for r in (self.out, self.held))
        copy = pltpu.make_async_copy(src, dst, self.sems.at[self.count])
        self.count += 1
        copy.start()
        self.new.append((k, at, copy))

    def work(self):
        todo, self.old, self.new = self.old, self.new, []
        for k, at, copy in todo:
            copy.wait()
            rows = pl.ds(C0[k], CN[k])

            def add(g, group, k=k, rows=rows):
                w = jnp.concatenate([turned_rows(self.wt, self.sel, g, piece, C0[k], CN[k]) for piece in group], axis=0)
                e = jnp.concatenate([self.held[(*piece, rows, slice(None))] for piece in group], axis=0)
                self.back[g] += lax.dot_general(w, e, (((0,), (0,)), ((), ())), preferred_element_type=jnp.float32)

            pieces(at, add)


def fill(k, at, sel, wt, lat, parts):
    lo, n = C0[k], CN[k]

    def group(g, found):
        for piece in found:
            part = jnp.dot(turned_rows(wt, sel, g, piece, lo, n), lat[g], preferred_element_type=jnp.float32)
            parts[(*piece, pl.ds(lo, n), slice(None))] = part.astype(jnp.bfloat16)

    pieces(at, group)


def reduce_error(me, make, parts, base, err, slots, send, recv):
    first, second, third = [], [], []
    for k in range(3):
        a, b, c = ORDER[k]
        mine = slots[36 * k : 36 * (k + 1)]
        at = {a: None, b: me[b], c: me[c]}

        def new(dim, at, i, k=k, mine=mine):
            return Reduction(me, k, dim, at, parts, mine[6 * i : 6 * i + 6], send, recv, 6 * i)

        first.append({m: new(c, {**at, b: shift(me, b, m)}, i) for i, m in enumerate(SUBS)})
        second.append(new(b, at, 4))
        third.append(new(a, {**at, a: me[a]}, 5))

    def whole(k, by):
        a, b, c = ORDER[k]
        make(k, {a: None, b: None, c: shift(me, c, by)})

    def push(m):
        for k in range(3):
            first[k][m].near()
            first[k][m].forward()

    for m in SUBS:
        for k in range(3):
            a, b, c = ORDER[k]
            make(k, {a: None, b: shift(me, b, m), c: shift(me, c, 2)})
            first[k][m].far()
    for k in range(3):
        whole(k, 1)
        whole(k, -1)
    push(2)
    push(-1)
    for k in range(3):
        whole(k, 0)
    for k in range(3):
        first[k][2].finish()
        second[k].far()
    push(1)
    for k in range(3):
        first[k][-1].finish()
    push(0)
    for k in range(3):
        first[k][1].finish()
        second[k].near()
    for k in range(3):
        second[k].forward()
    for k in range(3):
        first[k][0].finish()
    for k in range(3):
        second[k].finish()
        third[k].far()
        third[k].near()
    for k in range(3):
        third[k].forward()

    def last(k):
        def store(half, total):
            rows = pl.ds(C0[k] + half[0], half[1])
            err[rows, :] = (total + base[rows, :]).astype(jnp.bfloat16)

        third[k].finish(store)

    return last, [r for k in range(3) for r in (*first[k].values(), second[k], third[k])]


def params(collective=None):
    return pltpu.CompilerParams(collective_id=collective, has_side_effects=collective is not None,
                                vmem_limit_bytes=60 * 1024 * 1024)


PIECES = (2, 4, 4, 2, ROWS, TOK)
VMEM = pl.BlockSpec(memory_space=pltpu.VMEM)
ANY = pl.BlockSpec(memory_space=pl.ANY)


def turn(mine, bias, theirs, biases, wt, held_w, turned, sems, send, recv):
    def give(i, src, dst):
        c = pltpu.make_async_remote_copy(
            src_ref=src, dst_ref=dst, send_sem=send.at[i], recv_sem=recv.at[i],
            device_id={"c": 1 - lax.axis_index("c")}, device_id_type=pl.DeviceIdType.MESH)
        c.start()
        return c

    load = pltpu.make_async_copy(mine, held_w, sems.at[0])
    load.start()
    given = [give(0, mine, theirs), give(1, bias, biases.at[1])]
    biases[0] = bias[...]
    yield
    yield
    yield
    load.wait()
    yield

    def block(i, carry):
        b, j = i // (D // SPAN), pl.multiple_of(lax.rem(i, D // SPAN) * SPAN, SPAN)
        turned[b, pl.ds(j, SPAN), :] = held_w[b, :, pl.ds(j, SPAN)].T
        return carry

    lax.fori_loop(0, 4 * (D // SPAN), block, 0)
    yield
    keep = pltpu.make_async_copy(turned, wt.at[pl.ds(0, 4)], sems.at[1])
    keep.start()
    given.append(give(2, turned, wt.at[pl.ds(4, 4)]))
    yield
    keep.wait()
    for c in given:
        c.wait()


def both(*steps):
    while True:
        done = [next(s, "end") for s in steps]
        if all(d == "end" for d in done):
            return
        yield


def gather_kernel(own, codes, bias, mine, out, all_codes, biases, theirs, wt, local, send, recv, csend, crecv, held_w, turned, sems, wsend, wrecv):
    me = coords()
    barrier(me, True)
    steps = both(gather_codes(me, codes, all_codes, csend, crecv), turn(mine, bias, theirs, biases, wt, held_w, turned, sems, wsend, wrecv))
    gather(me, own, out, local, send, recv, steps)
    for _ in steps:
        pass


DMA = pltpu.SemaphoreType.DMA
COPIES = 28


def gather_call(x, codes, bias, mine):
    return pl.pallas_call(
        gather_kernel,
        out_shape=(
            jax.ShapeDtypeStruct(PIECES, jnp.bfloat16),
            jax.ShapeDtypeStruct((2, 4, 2, 8, 16), jnp.int32),
            jax.ShapeDtypeStruct((2, 8, SPAN), jnp.float32),
            jax.ShapeDtypeStruct((4, SPAN, D), jnp.bfloat16),
            jax.ShapeDtypeStruct((8, D, SPAN), jnp.bfloat16),
        ),
        in_specs=[VMEM, VMEM, VMEM, ANY], out_specs=(ANY, VMEM, VMEM, ANY, ANY),
        scratch_shapes=[
            DMA, DMA((3, COPIES)), DMA((3, COPIES)), DMA((4,)), DMA((4,)),
            pltpu.VMEM((4, SPAN, D), jnp.bfloat16), pltpu.VMEM((4, D, SPAN), jnp.bfloat16), DMA((2,)), DMA((3,)), DMA((3,)),
        ],
        compiler_params=params(0), name="gather",
        cost_estimate=pl.CostEstimate(flops=0, bytes_accessed=150_000_000, transcendentals=0),
    )(x, codes, bias, mine)


def error_kernel(sel, wt_hbm, lat, mask, base, err, out, slope, local, send, recv, rsend, rrecv, wt, wt_sem, parts, held_e, back, sems, *slots):
    me = coords()
    loads = [pltpu.make_async_copy(wt_hbm.at[i], wt.at[i], wt_sem.at[i]) for i in range(8)]
    for c in loads:
        c.start()
    back[...] = jnp.zeros_like(back)
    barrier(me)
    for c in loads:
        c.wait()

    def make(k, at):
        fill(k, at, sel, wt, lat, parts)

    last, reductions = reduce_error(me, make, parts, base, err, slots, rsend, rrecv)
    gather(me, err, out, local, send, recv, ready=last, use=Back(sel, wt, out, held_e, back, sems))

    def round_off(g, carry):
        slope[g] = jnp.where(mask[g] > 0, back[g], 0.0).astype(jnp.bfloat16)
        return carry

    lax.fori_loop(0, 8, round_off, 0)
    for r in reductions:
        r.drain()


def error_call(sel, wt, lat, mask, base):
    return pl.pallas_call(
        error_kernel,
        out_shape=(
            jax.ShapeDtypeStruct((ROWS, TOK), jnp.bfloat16),
            jax.ShapeDtypeStruct(PIECES, jnp.bfloat16),
            jax.ShapeDtypeStruct((8, 2 * SPAN, TOK), jnp.bfloat16),
        ),
        in_specs=[pl.BlockSpec(memory_space=pltpu.SMEM), ANY, VMEM, VMEM, VMEM], out_specs=(VMEM, ANY, VMEM),
        scratch_shapes=[
            DMA, DMA((3, COPIES)), DMA((3, COPIES)), DMA((3, 36)), DMA((3, 36)),
            pltpu.VMEM((8, D, SPAN), jnp.bfloat16), DMA((8,)), pltpu.VMEM(PIECES, jnp.bfloat16), pltpu.VMEM(PIECES, jnp.bfloat16),
            pltpu.VMEM((8, 2 * SPAN, TOK), jnp.float32), DMA((48,)), *reduce_scratch(),
        ],
        compiler_params=params(1), name="error",
    )(sel, wt, lat, mask, base)


CHUNK = DEPTH = 512


def encode_kernel(table, cen, mine, theirs, bias, lat, mask):
    g = pl.program_id(0)
    pre = jnp.zeros((2 * SPAN, TOK), jnp.float32)
    for i in range(0, D, DEPTH):
        w = jnp.concatenate([mine[0, :, i : i + DEPTH], theirs[0, :, i : i + DEPTH]], axis=0)
        pre = pre + jnp.dot(w, cen[0, i : i + DEPTH], preferred_element_type=jnp.float32)
    lane = lax.broadcasted_iota(jnp.int32, (SPAN, TOK), 1)
    for hh in range(2):
        rows = slice(hh * SPAN, (hh + 1) * SPAN)
        chosen = lax.broadcasted_iota(jnp.int32, (8, TOK), 0) == table[g, hh]
        p = pre[rows] + lax.dot_general(
            bias[hh].astype(jnp.bfloat16), jnp.where(chosen, 1.0, 0.0).astype(jnp.bfloat16),
            (((0,), (0,)), ((), ())), preferred_element_type=jnp.float32)
        on = jnp.where(lane < SPAN, table[g, 2 + hh], table[g, 4 + hh])
        keep = (on > 0) & (p > 0)
        lat[0, rows] = jnp.where(keep, p, 0.0).astype(jnp.bfloat16)
        mask[0, rows] = jnp.where(keep, 1.0, 0.0).astype(jnp.bfloat16)


def encode_call(table, cen, mine, theirs, bias):
    per = lambda *shape: pl.BlockSpec((1, *shape), lambda g, *_: (g, 0, 0))
    block = lambda hh: pl.BlockSpec((1, SPAN, D), lambda g, t: (t[g, hh], 0, 0))
    return pl.pallas_call(
        encode_kernel,
        out_shape=(
            jax.ShapeDtypeStruct((8, 2 * SPAN, TOK), jnp.bfloat16),
            jax.ShapeDtypeStruct((8, 2 * SPAN, TOK), jnp.bfloat16),
        ),
        grid_spec=pltpu.PrefetchScalarGridSpec(
            num_scalar_prefetch=1, grid=(8,),
            in_specs=[per(D, TOK), block(0), block(1), VMEM],
            out_specs=(per(2 * SPAN, TOK), per(2 * SPAN, TOK)),
        ),
        compiler_params=params(), name="encode",
    )(table, cen, mine, theirs, bias)


def grad_kernel(sel, err, cen, lat, slopes, own, other, own_b, other_b, mine_acc, acc):
    g = pl.program_id(0)

    @pl.when(g == 0)
    def _():
        mine_acc[...] = jnp.zeros_like(mine_acc)
        acc[...] = jnp.zeros_like(acc)
        own_b[...] = jnp.zeros_like(own_b)
        other_b[...] = jnp.zeros_like(other_b)

    slope = slopes[0]
    sums = lax.dot_general(jnp.ones((8, TOK), jnp.bfloat16), slope, (((1,), (1,)), ((), ())), preferred_element_type=jnp.float32)
    sums = sums.astype(jnp.bfloat16).astype(jnp.float32)
    row = lax.broadcasted_iota(jnp.int32, (8, SPAN), 0)
    for hh, into in enumerate((own_b, other_b)):
        into[...] += jnp.where(row == sel[g, hh], sums[:, hh * SPAN : (hh + 1) * SPAN], 0.0)
    for i in range(0, D, CHUNK):
        nt = (((1,), (1,)), ((), ()))
        t = lax.dot_general(lat[0], err[0, i : i + CHUNK], nt, preferred_element_type=jnp.float32)
        t = t + lax.dot_general(slope, cen[0, i : i + CHUNK], nt, preferred_element_type=jnp.float32)
        t = t.astype(jnp.bfloat16).astype(jnp.float32)
        mine_acc[sel[g, 0], :, i : i + CHUNK] += t[:SPAN]
        acc[sel[g, 1], :, i : i + CHUNK] += t[SPAN:]

    @pl.when(g == 7)
    def _():
        for b in range(4):
            own[b] = mine_acc[b].astype(jnp.bfloat16)
            other[b] = acc[b].astype(jnp.bfloat16)


def grad_call(sel, err, cen, lat, slope):
    per = lambda *shape: pl.BlockSpec((1, *shape), lambda g, *_: (g, 0, 0))
    return pl.pallas_call(
        grad_kernel,
        out_shape=(
            jax.ShapeDtypeStruct((4, SPAN, D), jnp.bfloat16),
            jax.ShapeDtypeStruct((4, SPAN, D), jnp.bfloat16),
            jax.ShapeDtypeStruct((8, SPAN), jnp.float32),
            jax.ShapeDtypeStruct((8, SPAN), jnp.float32),
        ),
        grid_spec=pltpu.PrefetchScalarGridSpec(
            num_scalar_prefetch=1, grid=(8,),
            in_specs=[per(D, TOK), per(D, TOK), per(2 * SPAN, TOK), per(2 * SPAN, TOK)],
            out_specs=(VMEM, VMEM, VMEM, VMEM),
            scratch_shapes=[pltpu.VMEM((4, SPAN, D), jnp.float32)] * 2,
        ),
        compiler_params=params(), name="grad",
    )(sel, err, cen, lat, slope)


NAMES = ("x", "zh", "zl", "y", "c")
SWAP = [(0, 1), (1, 0)]


def step(activations, dictionary, enc_bias, dec_bias, block_codes):
    d = lax.axis_index("x") * 2 + lax.axis_index("zh")
    c = lax.axis_index("c")
    chip = lax.axis_index("zl") * 4 + lax.axis_index("y")
    mine = dictionary.reshape(4, SPAN, D)
    act_t = activations.T.astype(jnp.float32)
    dec = lax.dynamic_slice_in_dim(dec_bias, d * ROWS, ROWS)[:, None]
    bias = jnp.pad(enc_bias.astype(jnp.float32).reshape(4, SPAN), ((0, 4), (0, 0)))
    cen, codes, biases, theirs, wt = gather_call((act_t - dec).astype(jnp.bfloat16), block_codes, bias, mine)
    cen = cen.reshape(8, D, TOK)
    codes = lax.dynamic_index_in_dim(codes.reshape(8, 2, 8, 16), d, axis=2, keepdims=False)
    first = d * 64 + (chip * 2 + jnp.stack([c, 1 - c])) * 4
    local = codes[:, :, None, :] - first[:, None]
    hit = (codes[:, :, None, :] >= 0) & (local >= 0) & (local < 4)
    local = jnp.max(jnp.where(hit, local, -1), axis=3)
    table = jnp.concatenate([jnp.maximum(jnp.max(local, axis=1), 0), (local >= 0).astype(jnp.int32).reshape(8, 4)], axis=1)
    lat, mask = encode_call(table, cen, mine, theirs, biases)
    err_own, err, slope = error_call(table, wt, lat, mask, dec - act_t)
    own, other, own_b, other_b = grad_call(table, err.reshape(8, D, TOK), cen, lat, slope)
    grad_w = own.astype(jnp.float32) + lax.ppermute(other, "c", SWAP).astype(jnp.float32)
    grad_b = (own_b + lax.ppermute(other_b, "c", SWAP))[:4]
    return err_own.T, grad_w.reshape(4 * SPAN, D), grad_b.reshape(4 * SPAN)


def solution(mesh):
    split = Mesh(mesh.devices.reshape(4, 2, 2, 4, 2), NAMES)
    dict_, dp = ("x", "zh"), ("zl", "y", "c")
    rows = P((*dict_, *dp))
    return jax.shard_map(
        step, mesh=split,
        in_specs=(P(dp, dict_), P((*dict_, *dp), None), rows, P(), P(dp, None, None)),
        out_specs=(P(dp, dict_), P((*dict_, *dp), None), rows),
        check_vma=False,
    )
```

```python
import functools
import jax, jax.numpy as jnp
from jax import lax
from jax.experimental import pallas as pl
from jax.experimental.pallas import tpu as pltpu
from jax.sharding import Mesh, PartitionSpec as P

ROWS, TOK = 448, 256
D, SPAN = 3584, 128
C0 = (0, 144, 288)
CN = (144, 144, 160)
CH = (80, 64, 80)
ORDER = (("x", "y", "z"), ("y", "z", "x"), ("z", "x", "y"))


def coords():
    x, y = lax.axis_index("x"), lax.axis_index("y")
    z = lax.axis_index("zh") * 2 + lax.axis_index("zl")
    return {"x": x, "y": y, "z": z}


def shift(me, dim, by):
    return lax.rem(me[dim] + (by + 4), 4)


def device(dim, value):
    if dim == "z":
        return {"zh": value // 2, "zl": lax.rem(value, 2)}
    return {dim: value}


def region(ref, at, lo, n):
    z = at["z"]
    zl = slice(None) if z is None else lax.rem(z, 2)
    zh = slice(None) if z is None else z // 2
    y = slice(None) if at["y"] is None else at["y"]
    x = slice(None) if at["x"] is None else at["x"]
    return ref.at[zl, y, x, zh, pl.ds(lo, n), :]


def remote(src, dst, send, recv, dim, value):
    return pltpu.make_async_remote_copy(
        src_ref=src, dst_ref=dst, send_sem=send, recv_sem=recv,
        device_id=device(dim, value), device_id_type=pl.DeviceIdType.MESH)


def barrier(me, cores=False):
    sem = pltpu.get_barrier_semaphore()
    for dim in ("x", "y", "z"):
        for by in (-1, 1):
            pl.semaphore_signal(sem, inc=1, device_id=device(dim, shift(me, dim, by)),
                                device_id_type=pl.DeviceIdType.MESH)
    if cores:
        pl.semaphore_signal(sem, inc=1, device_id={"c": 1 - lax.axis_index("c")}, device_id_type=pl.DeviceIdType.MESH)
    pl.semaphore_wait(sem, 7 if cores else 6)


NEAR = ((0, 1), (1, -1))


def gather(me, own, out, local, send, recv, beside=iter(()), ready=lambda k: None, use=None):
    mine = pltpu.make_async_copy(own, region(out, me, 0, ROWS), local)
    copies = [{} for _ in range(3)]

    def arrived(k, by_b, by_c=0):
        if use is not None:
            a, b, c = ORDER[k]
            use.arrived(k, {a: None, b: shift(me, b, by_b), c: shift(me, c, by_c)})

    def work():
        if use is not None:
            use.work()

    def go(k, phase, name, at, by, lo=0, n=None, src=None):
        order = ORDER[k]
        where = {d: (None if i < phase - 1 else shift(me, d, at.get(i, 0))) for i, d in enumerate(order)}
        part = region(out, where, C0[k] + lo, CN[k] if n is None else n)
        dim = order[phase]
        i = len(copies[k])
        c = remote(part if src is None else src, part, send.at[k, i], recv.at[k, i], dim, shift(me, dim, by))
        c.start()
        copies[k][(phase, *name)] = c

    def got(k, *name):
        copies[k][name].wait_recv()

    for k in range(3):
        ready(k)
        src = own.at[pl.ds(C0[k], CN[k]), :]
        for s, by in NEAR:
            go(k, 0, ("near", s), {}, by, src=src)
        for s, by in NEAR:
            go(k, 1, ("near", 0, s), {}, by, src=src)
    mine.start()
    next(beside, None)
    for k in range(3):
        for s, by in NEAR:
            got(k, 0, "near", s)
            lo, n = (0, CH[k]) if s == 0 else (CH[k], CN[k] - CH[k])
            go(k, 0, ("far", s), {0: -by}, by, lo, n)
        for j in (-1, 1):
            for s, by in NEAR:
                go(k, 1, ("near", j, s), {0: j}, by)
    mine.wait()
    next(beside, None)
    for k in range(3):
        got(k, 0, "far", 0)
        got(k, 0, "far", 1)
        for s, by in NEAR:
            go(k, 1, ("near", 2, s), {0: 2}, by)
        for s, by in NEAR:
            go(k, 2, ("near", 0, s), {1: 0}, by)
        arrived(k, 0)
    for phase in (1, 2):
        next(beside, None)
        for j in (0, -1, 1, 2):
            for k in range(3):
                for s, by in NEAR:
                    got(k, phase, "near", j, s)
                    if (j in (0, 1)) == (s == 0):
                        go(k, phase, ("far", j), {phase - 1: j, phase: -by}, by)
                    if phase == 2:
                        arrived(k, j, -by)
            if phase == 2:
                work()
        if phase == 1:
            for k in range(3):
                for j in (-1, 1):
                    for s, by in NEAR:
                        go(k, 2, ("near", j, s), {1: j}, by)
                    arrived(k, j)
        next(beside, None)
        for j in (0, -1, 1, 2):
            for k in range(3):
                got(k, phase, "far", j)
                if phase == 2:
                    arrived(k, j, 2)
            if phase == 2:
                work()
        if phase == 1:
            for k in range(3):
                for s, by in NEAR:
                    go(k, 2, ("near", 2, s), {1: 2}, by)
                arrived(k, 2)
            work()
    work()
    work()
    for k in range(3):
        for c in copies[k].values():
            c.wait_send()


def gather_codes(me, own, out, send, recv):
    zl = lax.rem(me["z"], 2)
    out[zl, me["y"]] = own[...]
    copies = []

    def go(src, dst, device_id):
        i = len(copies)
        c = pltpu.make_async_remote_copy(src_ref=src, dst_ref=dst, send_sem=send.at[i], recv_sem=recv.at[i],
                                         device_id=device_id, device_id_type=pl.DeviceIdType.MESH)
        c.start()
        copies.append(c)

    for by in (1, -1):
        go(own, out.at[zl, me["y"]], device("y", shift(me, "y", by)))
    yield
    copies[0].wait_recv()
    back = out.at[zl, shift(me, "y", -1)]
    go(back, back, device("y", shift(me, "y", 1)))
    yield
    copies[1].wait_recv()
    copies[2].wait_recv()
    go(out.at[zl], out.at[zl], {"zl": 1 - zl})
    yield
    copies[3].wait_recv()
    for c in copies:
        c.wait_send()


def lead(dims):
    return tuple(s for name, s in (("zl", 2), ("y", 4), ("x", 4), ("zh", 2)) if name[0] in dims)


def each(shape, body):
    total = 1
    for s in shape:
        total *= s
    if total == 1:
        body(())
        return

    def step(i, carry):
        index = []
        for s in reversed(shape):
            index.append(lax.rem(i, s))
            i = i // s
        body(tuple(reversed(index)))
        return carry

    lax.fori_loop(0, total, step, 0)


SUBS = (2, -1, 1, 0)


def reduce_scratch():
    shapes = []
    for k in range(3):
        n, h = CN[k], CH[k]
        for q in (0, 0, 0, 0, 1, 2):
            dims = lead(ORDER[k][:1] if q < 2 else ())
            for rows in (h, n - h, h, n - h, h, n - h):
                shapes.append(pltpu.VMEM((*dims, rows, TOK), jnp.bfloat16))
    return shapes


class Reduction:
    def __init__(self, me, k, dim, at, parts, slots, send, recv, base):
        self.me, self.k, self.dim, self.at, self.parts, self.slots = me, k, dim, at, parts, slots
        self.send, self.recv, self.base = send, recv, base
        self.copies = {}
        self.lead = lead(tuple(d for d in at if d != dim and at[d] is None))
        self.halves = ((0, CH[k]), (CH[k], CN[k] - CH[k]))

    def source(self, by, half):
        lo, n = self.halves[half]
        return region(self.parts, {**self.at, self.dim: shift(self.me, self.dim, by)}, C0[self.k] + lo, n)

    def go(self, i, src, by):
        c = remote(src, self.slots[i], self.send.at[self.k, self.base + i], self.recv.at[self.k, self.base + i],
                   self.dim, shift(self.me, self.dim, by))
        c.start()
        self.copies[i] = c

    def far(self):
        self.go(0, self.source(2, 0), 1)
        self.go(1, self.source(2, 1), -1)

    def near(self):
        self.go(3, self.source(1, 1), 1)
        self.go(4, self.source(-1, 0), -1)

    def forward(self):
        for i, by in ((0, 1), (1, -1)):
            self.copies[i].wait_recv()
            slot, own = self.slots[i], self.source(by, i)

            def add(index, slot=slot, own=own):
                a = slot[index].astype(jnp.float32) + own[index].astype(jnp.float32)
                slot[index] = a.astype(jnp.bfloat16)

            each(self.lead, add)
            self.go(2 if i == 0 else 5, slot, by)

    def finish(self, store=None):
        for i in (3, 4, 2, 5):
            self.copies[i].wait_recv()
        for half, (i, j) in enumerate(((2, 4), (3, 5))):
            a, b, own = self.slots[i], self.slots[j], self.source(0, half)

            def add(index, a=a, b=b, own=own, half=half):
                total = own[index].astype(jnp.float32) + a[index].astype(jnp.float32) + b[index].astype(jnp.float32)
                if store is None:
                    own[index] = total.astype(jnp.bfloat16)
                else:
                    store(self.halves[half], total)

            each(self.lead, add)

    def drain(self):
        for c in self.copies.values():
            c.wait_send()


def pieces(at, body):
    def group(index):
        index = list(index)
        zl = index.pop(0) if at["z"] is None else lax.rem(at["z"], 2)
        y = index.pop(0) if at["y"] is None else at["y"]
        body(zl * 4 + y, [
            (zl, y, x, zh)
            for zh in ((0, 1) if at["z"] is None else (at["z"] // 2,))
            for x in (range(4) if at["x"] is None else (at["x"],))
        ])

    each((2,) * (at["z"] is None) + (4,) * (at["y"] is None), group)


def turned_rows(wt, sel, g, piece, lo, n):
    rows = pl.ds(pl.multiple_of((piece[2] * 2 + piece[3]) * ROWS + lo, 16), n)
    return jnp.concatenate([wt[sel[g, 0], rows, :], wt[4 + sel[g, 1], rows, :]], axis=1)


class Back:
    def __init__(self, sel, wt, out, held_e, back, sems):
        self.sel, self.wt, self.out, self.held, self.back, self.sems = sel, wt, out, held_e, back, sems
        self.count, self.old, self.new = 0, [], []

    def arrived(self, k, at):
        src, dst = (region(r, at, C0[k], CN[k]) for r in (self.out, self.held))
        copy = pltpu.make_async_copy(src, dst, self.sems.at[self.count])
        self.count += 1
        copy.start()
        self.new.append((k, at, copy))

    def work(self):
        todo, self.old, self.new = self.old, self.new, []
        for k, at, copy in todo:
            copy.wait()
            rows = pl.ds(C0[k], CN[k])

            def add(g, group, k=k, rows=rows):
                w = jnp.concatenate([turned_rows(self.wt, self.sel, g, piece, C0[k], CN[k]) for piece in group], axis=0)
                e = jnp.concatenate([self.held[(*piece, rows, slice(None))] for piece in group], axis=0)
                self.back[g] += lax.dot_general(w, e, (((0,), (0,)), ((), ())), preferred_element_type=jnp.float32)

            pieces(at, add)


def fill(k, at, sel, wt, lat, parts):
    lo, n = C0[k], CN[k]

    def group(g, found):
        for piece in found:
            part = jnp.dot(turned_rows(wt, sel, g, piece, lo, n), lat[g], preferred_element_type=jnp.float32)
            parts[(*piece, pl.ds(lo, n), slice(None))] = part.astype(jnp.bfloat16)

    pieces(at, group)


def reduce_error(me, make, parts, base, err, slots, send, recv):
    first, second, third = [], [], []
    for k in range(3):
        a, b, c = ORDER[k]
        mine = slots[36 * k : 36 * (k + 1)]
        at = {a: None, b: me[b], c: me[c]}

        def new(dim, at, i, k=k, mine=mine):
            return Reduction(me, k, dim, at, parts, mine[6 * i : 6 * i + 6], send, recv, 6 * i)

        first.append({m: new(c, {**at, b: shift(me, b, m)}, i) for i, m in enumerate(SUBS)})
        second.append(new(b, at, 4))
        third.append(new(a, {**at, a: me[a]}, 5))

    def whole(k, by):
        a, b, c = ORDER[k]
        make(k, {a: None, b: None, c: shift(me, c, by)})

    def push(m):
        for k in range(3):
            first[k][m].near()
            first[k][m].forward()

    for m in SUBS:
        for k in range(3):
            a, b, c = ORDER[k]
            make(k, {a: None, b: shift(me, b, m), c: shift(me, c, 2)})
            first[k][m].far()
    for k in range(3):
        whole(k, 1)
        whole(k, -1)
    push(2)
    push(-1)
    for k in range(3):
        whole(k, 0)
    for k in range(3):
        first[k][2].finish()
        second[k].far()
    push(1)
    for k in range(3):
        first[k][-1].finish()
    push(0)
    for k in range(3):
        first[k][1].finish()
        second[k].near()
    for k in range(3):
        second[k].forward()
    for k in range(3):
        first[k][0].finish()
    for k in range(3):
        second[k].finish()
        third[k].far()
        third[k].near()
    for k in range(3):
        third[k].forward()

    def last(k):
        def store(half, total):
            rows = pl.ds(C0[k] + half[0], half[1])
            err[rows, :] = (total + base[rows, :]).astype(jnp.bfloat16)

        third[k].finish(store)

    return last, [r for k in range(3) for r in (*first[k].values(), second[k], third[k])]


def params(collective=None, mib=60):
    return pltpu.CompilerParams(collective_id=collective, has_side_effects=collective is not None,
                                vmem_limit_bytes=mib * 1024 * 1024)


PIECES = (2, 4, 4, 2, ROWS, TOK)
VMEM = pl.BlockSpec(memory_space=pltpu.VMEM)
ANY = pl.BlockSpec(memory_space=pl.ANY)


def turn(mine, bias, theirs, biases, wt, held_w, turned, sems, send, recv):
    def give(i, src, dst):
        c = pltpu.make_async_remote_copy(
            src_ref=src, dst_ref=dst, send_sem=send.at[i], recv_sem=recv.at[i],
            device_id={"c": 1 - lax.axis_index("c")}, device_id_type=pl.DeviceIdType.MESH)
        c.start()
        return c

    load = pltpu.make_async_copy(mine, held_w, sems.at[0])
    load.start()
    given = [give(0, mine, theirs), give(1, bias, biases.at[1])]
    biases[0] = bias[...]
    yield
    yield
    yield
    load.wait()
    yield

    def block(i, carry):
        b, j = i // (D // SPAN), pl.multiple_of(lax.rem(i, D // SPAN) * SPAN, SPAN)
        turned[b, pl.ds(j, SPAN), :] = held_w[b, :, pl.ds(j, SPAN)].T
        return carry

    lax.fori_loop(0, 4 * (D // SPAN), block, 0)
    yield
    keep = pltpu.make_async_copy(turned, wt.at[pl.ds(0, 4)], sems.at[1])
    keep.start()
    given.append(give(2, turned, wt.at[pl.ds(4, 4)]))
    yield
    keep.wait()
    for c in given:
        c.wait()


def both(*steps):
    while True:
        done = [next(s, "end") for s in steps]
        if all(d == "end" for d in done):
            return
        yield


def gather_kernel(own, codes, bias, mine, out, all_codes, biases, theirs, wt, local, send, recv, csend, crecv, held_w, turned, sems, wsend, wrecv):
    me = coords()
    barrier(me, True)
    steps = both(gather_codes(me, codes, all_codes, csend, crecv), turn(mine, bias, theirs, biases, wt, held_w, turned, sems, wsend, wrecv))
    gather(me, own, out, local, send, recv, steps)
    for _ in steps:
        pass


DMA = pltpu.SemaphoreType.DMA
COPIES = 28


def gather_call(x, codes, bias, mine):
    return pl.pallas_call(
        gather_kernel,
        out_shape=(
            jax.ShapeDtypeStruct(PIECES, jnp.bfloat16),
            jax.ShapeDtypeStruct((2, 4, 2, 8, 16), jnp.int32),
            jax.ShapeDtypeStruct((2, 8, SPAN), jnp.float32),
            jax.ShapeDtypeStruct((4, SPAN, D), jnp.bfloat16),
            jax.ShapeDtypeStruct((8, D, SPAN), jnp.bfloat16),
        ),
        in_specs=[VMEM, VMEM, VMEM, ANY], out_specs=(ANY, VMEM, VMEM, ANY, ANY),
        scratch_shapes=[
            DMA, DMA((3, COPIES)), DMA((3, COPIES)), DMA((4,)), DMA((4,)),
            pltpu.VMEM((4, SPAN, D), jnp.bfloat16), pltpu.VMEM((4, D, SPAN), jnp.bfloat16), DMA((2,)), DMA((3,)), DMA((3,)),
        ],
        compiler_params=params(0), name="gather",
        cost_estimate=pl.CostEstimate(flops=0, bytes_accessed=150_000_000, transcendentals=0),
    )(x, codes, bias, mine)


def error_kernel(sel, wt_hbm, lat, mask, base, err, out, slope, local, send, recv, rsend, rrecv, wt, wt_sem, parts, held_e, back, sems, *slots):
    me = coords()
    loads = [pltpu.make_async_copy(wt_hbm.at[i], wt.at[i], wt_sem.at[i]) for i in range(8)]
    for c in loads:
        c.start()
    back[...] = jnp.zeros_like(back)
    barrier(me)
    for c in loads:
        c.wait()

    def make(k, at):
        fill(k, at, sel, wt, lat, parts)

    last, reductions = reduce_error(me, make, parts, base, err, slots, rsend, rrecv)
    gather(me, err, out, local, send, recv, ready=last, use=Back(sel, wt, out, held_e, back, sems))

    def round_off(g, carry):
        slope[g] = jnp.where(mask[g] > 0, back[g], 0.0).astype(jnp.bfloat16)
        return carry

    lax.fori_loop(0, 8, round_off, 0)
    for r in reductions:
        r.drain()


def error_call(sel, wt, lat, mask, base):
    return pl.pallas_call(
        error_kernel,
        out_shape=(
            jax.ShapeDtypeStruct((ROWS, TOK), jnp.bfloat16),
            jax.ShapeDtypeStruct(PIECES, jnp.bfloat16),
            jax.ShapeDtypeStruct((8, 2 * SPAN, TOK), jnp.bfloat16),
        ),
        in_specs=[pl.BlockSpec(memory_space=pltpu.SMEM), ANY, VMEM, VMEM, VMEM], out_specs=(VMEM, ANY, VMEM),
        scratch_shapes=[
            DMA, DMA((3, COPIES)), DMA((3, COPIES)), DMA((3, 36)), DMA((3, 36)),
            pltpu.VMEM((8, D, SPAN), jnp.bfloat16), DMA((8,)), pltpu.VMEM(PIECES, jnp.bfloat16), pltpu.VMEM(PIECES, jnp.bfloat16),
            pltpu.VMEM((8, 2 * SPAN, TOK), jnp.float32), DMA((48,)), *reduce_scratch(),
        ],
        compiler_params=params(1), name="error",
    )(sel, wt, lat, mask, base)


CHUNK = DEPTH = 512


def encode_kernel(table, cen, mine, theirs, bias, lat, mask):
    g = pl.program_id(0)
    pre = jnp.zeros((2 * SPAN, TOK), jnp.float32)
    for i in range(0, D, DEPTH):
        w = jnp.concatenate([mine[0, :, i : i + DEPTH], theirs[0, :, i : i + DEPTH]], axis=0)
        pre = pre + jnp.dot(w, cen[0, i : i + DEPTH], preferred_element_type=jnp.float32)
    lane = lax.broadcasted_iota(jnp.int32, (SPAN, TOK), 1)
    for hh in range(2):
        rows = slice(hh * SPAN, (hh + 1) * SPAN)
        chosen = lax.broadcasted_iota(jnp.int32, (8, TOK), 0) == table[g, hh]
        p = pre[rows] + lax.dot_general(
            bias[hh].astype(jnp.bfloat16), jnp.where(chosen, 1.0, 0.0).astype(jnp.bfloat16),
            (((0,), (0,)), ((), ())), preferred_element_type=jnp.float32)
        on = jnp.where(lane < SPAN, table[g, 2 + hh], table[g, 4 + hh])
        keep = (on > 0) & (p > 0)
        lat[0, rows] = jnp.where(keep, p, 0.0).astype(jnp.bfloat16)
        mask[0, rows] = jnp.where(keep, 1.0, 0.0).astype(jnp.bfloat16)


def encode_call(table, cen, mine, theirs, bias):
    per = lambda *shape: pl.BlockSpec((1, *shape), lambda g, *_: (g, 0, 0))
    block = lambda hh: pl.BlockSpec((1, SPAN, D), lambda g, t: (t[g, hh], 0, 0))
    return pl.pallas_call(
        encode_kernel,
        out_shape=(
            jax.ShapeDtypeStruct((8, 2 * SPAN, TOK), jnp.bfloat16),
            jax.ShapeDtypeStruct((8, 2 * SPAN, TOK), jnp.bfloat16),
        ),
        grid_spec=pltpu.PrefetchScalarGridSpec(
            num_scalar_prefetch=1, grid=(8,),
            in_specs=[per(D, TOK), block(0), block(1), VMEM],
            out_specs=(per(2 * SPAN, TOK), per(2 * SPAN, TOK)),
        ),
        compiler_params=params(), name="encode",
    )(table, cen, mine, theirs, bias)


def grad_kernel(sel, err, cen, lat, slopes, own, other, own_b, other_b, mine_acc, acc):
    g = pl.program_id(0)

    @pl.when(g == 0)
    def _():
        mine_acc[...] = jnp.zeros_like(mine_acc)
        acc[...] = jnp.zeros_like(acc)
        own_b[...] = jnp.zeros_like(own_b)
        other_b[...] = jnp.zeros_like(other_b)

    slope = slopes[0]
    sums = lax.dot_general(jnp.ones((8, TOK), jnp.bfloat16), slope, (((1,), (1,)), ((), ())), preferred_element_type=jnp.float32)
    sums = sums.astype(jnp.bfloat16).astype(jnp.float32)
    row = lax.broadcasted_iota(jnp.int32, (8, SPAN), 0)
    for hh, into in enumerate((own_b, other_b)):
        into[...] += jnp.where(row == sel[g, hh], sums[:, hh * SPAN : (hh + 1) * SPAN], 0.0)
    for i in range(0, D, CHUNK):
        nt = (((1,), (1,)), ((), ()))
        t = lax.dot_general(lat[0], err[0, i : i + CHUNK], nt, preferred_element_type=jnp.float32)
        t = t + lax.dot_general(slope, cen[0, i : i + CHUNK], nt, preferred_element_type=jnp.float32)
        t = t.astype(jnp.bfloat16).astype(jnp.float32)
        mine_acc[sel[g, 0], :, i : i + CHUNK] += t[:SPAN]
        acc[sel[g, 1], :, i : i + CHUNK] += t[SPAN:]

    @pl.when(g == 7)
    def _():
        for b in range(4):
            own[b] = mine_acc[b].astype(jnp.bfloat16)
            other[b] = acc[b].astype(jnp.bfloat16)


def grad_call(sel, err, cen, lat, slope):
    per = lambda *shape: pl.BlockSpec((1, *shape), lambda g, *_: (g, 0, 0))
    return pl.pallas_call(
        grad_kernel,
        out_shape=(
            jax.ShapeDtypeStruct((4, SPAN, D), jnp.bfloat16),
            jax.ShapeDtypeStruct((4, SPAN, D), jnp.bfloat16),
            jax.ShapeDtypeStruct((8, SPAN), jnp.float32),
            jax.ShapeDtypeStruct((8, SPAN), jnp.float32),
        ),
        grid_spec=pltpu.PrefetchScalarGridSpec(
            num_scalar_prefetch=1, grid=(8,),
            in_specs=[per(D, TOK), per(D, TOK), per(2 * SPAN, TOK), per(2 * SPAN, TOK)],
            out_specs=(VMEM, VMEM, VMEM, VMEM),
            scratch_shapes=[pltpu.VMEM((4, SPAN, D), jnp.float32)] * 2,
        ),
        compiler_params=params(mib=36), name="grad",
    )(sel, err, cen, lat, slope)


NAMES = ("x", "zh", "zl", "y", "c")
SWAP = [(0, 1), (1, 0)]


def step(activations, dictionary, enc_bias, dec_bias, block_codes):
    d = lax.axis_index("x") * 2 + lax.axis_index("zh")
    c = lax.axis_index("c")
    chip = lax.axis_index("zl") * 4 + lax.axis_index("y")
    mine = dictionary.reshape(4, SPAN, D)
    act_t = activations.T.astype(jnp.float32)
    dec = lax.dynamic_slice_in_dim(dec_bias, d * ROWS, ROWS)[:, None]
    bias = jnp.pad(enc_bias.astype(jnp.float32).reshape(4, SPAN), ((0, 4), (0, 0)))
    cen, codes, biases, theirs, wt = gather_call((act_t - dec).astype(jnp.bfloat16), block_codes, bias, mine)
    cen = cen.reshape(8, D, TOK)
    codes = lax.dynamic_index_in_dim(codes.reshape(8, 2, 8, 16), d, axis=2, keepdims=False)
    first = d * 64 + (chip * 2 + jnp.stack([c, 1 - c])) * 4
    local = codes[:, :, None, :] - first[:, None]
    hit = (codes[:, :, None, :] >= 0) & (local >= 0) & (local < 4)
    local = jnp.max(jnp.where(hit, local, -1), axis=3)
    table = jnp.concatenate([jnp.maximum(jnp.max(local, axis=1), 0), (local >= 0).astype(jnp.int32).reshape(8, 4)], axis=1)
    lat, mask = encode_call(table, cen, mine, theirs, biases)
    err_own, err, slope = error_call(table, wt, lat, mask, dec - act_t)
    own, other, own_b, other_b = grad_call(table, err.reshape(8, D, TOK), cen, lat, slope)
    grad_w = own.astype(jnp.float32) + lax.ppermute(other, "c", SWAP).astype(jnp.float32)
    grad_b = (own_b + lax.ppermute(other_b, "c", SWAP))[:4]
    return err_own.T, grad_w.reshape(4 * SPAN, D), grad_b.reshape(4 * SPAN)


def solution(mesh):
    split = Mesh(mesh.devices.reshape(4, 2, 2, 4, 2), NAMES)
    dict_, dp = ("x", "zh"), ("zl", "y", "c")
    rows = P((*dict_, *dp))
    return jax.shard_map(
        step, mesh=split,
        in_specs=(P(dp, dict_), P((*dict_, *dp), None), rows, P(), P(dp, None, None)),
        out_specs=(P(dp, dict_), P((*dict_, *dp), None), rows),
        check_vma=False,
    )
```
